256 devices in a mesh: dp: 16 (over z, core), tx: 4 (over y), ty: 4 (over x).
Axes of the slice: x: 4, y: 4, z: 8, core: 2. Of those that a mesh axis runs over, the one named last changes fastest.
Arguments:
- hidden_in: bfloat16 [8192, 2048], P('dp', 'ty'), may hold values from -24 to 24
- norm_gain: bfloat16 [2048], replicated, may hold values from 0.099609375 to 1.8984375
- w_qkv: bfloat16 [2048, 3072], P('ty', 'tx'), may hold values from -16 to 16
- w_out: bfloat16 [2048, 2048], P('tx', 'ty'), may hold values from -0.125 to 0.125
- k_cache: bfloat16 [128, 8192, 512], P('dp', 'ty', 'tx'), may hold values from -3300 to 3300
- v_cache: bfloat16 [128, 8192, 512], P('dp', 'ty', 'tx'), may hold values from -6.5 to 6.5
- cache_lens: int32 [128], replicated, may hold values from 1 to 8192, 524288 in all
- home_slot: int32 [128], replicated, may hold values from 0 to 127, as said below
- parents: int32 [128, 64], replicated, may hold values from 0 to 6, as said below
- tree_sizes: int32 [128], P('dp'), may hold values from 32 to 64, as said below
- leaf_node: int32 [128], P('dp'), may hold values from 0 to 31
Outputs:
- layer_out: bfloat16 [8192, 2048], P(('dp', 'tx'), 'ty')
- accepted_kv: bfloat16 [128, 8, 2, 512], P('dp', None, None, 'tx')
The draws below stay inside these ranges and needn't reach their ends.
Inputs may be any that keep to these rules, and one draw needn't show every extreme that they name: A permutation of the 128 cache slots; the slot lies in group home_slot[r] // 8 of dp. Of the 8 requests of one group, at most 1 have their slots in any one group, and 1 is reached. parents[r, 0] = 0 is the root; parents[r, t] = t - 1 for 0 < t < 8; every other node's parent is one of the nodes 0 to 6. Slots from tree_sizes[r] to 63 are padding; some request fills all 64. Positions from cache_lens[s] on in slot s are unused; some slot is full.
All inputs are finite; a program needn't handle non-finite values.
Results may differ from the reference program's by a relative error of at most 0.012.
Values may be sent and summed in bfloat16 or wider, within the bound.
A program may use at most 128 MiB of HBM per device.

```python
import math
import jax
import jax.numpy as jnp
import numpy as np
from jax import lax

D = 2048
KVH = 8
HD = 64
GROUP = 4
TREE = 64
ACC = 8
R_DEV = 8
CACHE = 8192
HQ = 32
REQS = 128
ROWS = 8192
N_DP = 16
N_TY = 4


def draw_hidden_in(key, part):
    first, second = jax.random.split(jax.random.fold_in(key, 3), 2)
    values = jax.random.truncated_normal(first, -4.0, 4.0, (ROWS, D), jnp.float32)
    row_scale = 0.3 * jnp.exp(jax.random.uniform(second, (ROWS, 1), jnp.float32, 0.0, math.log(10.0)))
    values = values * row_scale
    return values.astype(jnp.bfloat16)


def draw_w_qkv(key, part):
    base = jax.random.truncated_normal(jax.random.fold_in(key, 5), -4.0, 4.0, (D, KVH, GROUP + 2, HD), jnp.float32) / math.sqrt(D)
    query_part = base[:, :, :GROUP, :]
    shared = jnp.sum(query_part, axis=2) / math.sqrt(GROUP)
    key_part = 14.0 * (0.9 * shared + 0.44 * base[:, :, GROUP, :])
    value_part = base[:, :, GROUP + 1, :]
    whole = jnp.concatenate([query_part, key_part[:, :, None, :], value_part[:, :, None, :]], axis=2)
    return whole.reshape(D, KVH * (GROUP + 2) * HD).astype(jnp.bfloat16)


def draw_k_cache(key, part):
    first = jax.random.fold_in(jax.random.fold_in(key, 7), 0)
    values = jax.random.truncated_normal(first, -4.0, 4.0, (REQS, CACHE, KVH * HD), jnp.float32)
    values = 16.0 * values
    return values.astype(jnp.bfloat16)


def draw_v_cache(key, part):
    first, second = jax.random.split(jax.random.fold_in(key, 19))
    noise = jax.random.truncated_normal(first, -4.0, 4.0, (REQS, N_TY, CACHE // N_TY, KVH * HD), jnp.float32)
    offsets = jax.random.uniform(second, (REQS, N_TY, 1, KVH * HD), jnp.float32, -2.5, 2.5)
    values = noise + offsets
    return values.reshape(REQS, CACHE, KVH * HD).astype(jnp.bfloat16)


def draw_home_slot(key, part):
    first, second = jax.random.split(jax.random.fold_in(key, 11))
    pool_size = max(R_DEV, N_DP)
    drawn = jax.random.permutation(first, pool_size).astype(jnp.int32)
    one_value = 1 % pool_size
    where_one = jnp.sum(jnp.where(drawn == one_value, jnp.arange(pool_size, dtype=jnp.int32), 0)).astype(jnp.int32)
    shuffled = drawn.at[where_one].set(drawn[0]).at[0].set(one_value)[:R_DEV]
    offsets = shuffled % N_DP
    source_ids = jnp.arange(N_DP, dtype=jnp.int32)[:, None]
    target = (source_ids + offsets[None, :]) % N_DP
    ranking = jax.random.randint(second, (N_DP, R_DEV), 0, 1 << 20) * R_DEV + jnp.arange(R_DEV, dtype=jnp.int32)[None, :]
    placement = jnp.argsort(jnp.argsort(ranking, axis=1), axis=1)
    local_ids = jnp.broadcast_to(jnp.arange(R_DEV, dtype=jnp.int32)[None, :], (N_DP, R_DEV))
    landing = placement[target, local_ids]
    return (target * R_DEV + landing).reshape(R_DEV * N_DP).astype(jnp.int32)


def draw_parents(key, part):
    node_ids = jnp.arange(TREE, dtype=jnp.int32)
    branch = jax.random.randint(jax.random.fold_in(key, 13), (REQS, TREE), 0, ACC - 1)
    chain = jnp.maximum(node_ids - 1, 0)
    return jnp.where(node_ids[None, :] < ACC, chain[None, :], branch).astype(jnp.int32)


def draw_tree_sizes(key, part):
    first, second = jax.random.split(jax.random.fold_in(key, 17))
    sizes = jax.random.randint(first, (REQS,), TREE // 2, TREE + 1)
    full_one = jax.random.randint(second, (), 0, REQS)
    return sizes.at[full_one].set(TREE).astype(jnp.int32)


def set_ends(values, stream_key, least, top_value):
    longest = values.shape.index(max(values.shape))
    spots = []
    for shift in (0, 1):
        where = [jax.random.randint(jax.random.fold_in(stream_key, axis), (), 0, length) for axis, length in enumerate(values.shape)]
        where[longest] = (where[longest] + shift) % values.shape[longest]
        spots.append(tuple(where))
    return values.at[spots[0]].set(least).at[spots[1]].set(top_value)


def levels(stream_key, dims, cuts, low, top_value):
    factor_of = 1.0
    for dim, blocks in cuts:
        heights = jax.random.uniform(jax.random.fold_in(jax.random.fold_in(stream_key, 6), dim), (blocks,), jnp.float32, low / len(cuts), top_value / len(cuts))
        factor_of = factor_of * jnp.repeat(jnp.exp(heights), dims[dim] // blocks).reshape((-1,) + (1,) * (len(dims) - 1 - dim))
    return factor_of


def length_profile(count, total, most, lean):
    weights = [(1 << 20) // math.isqrt(standing ** lean) + 1 for standing in range(2, count + 1)]
    rest, counts = total - most - (count - 1), [1] * (count - 1)
    while rest > 0:
        candidates = [i for i in range(count - 1) if counts[i] < most]
        pool, budget = sum([weights[i] for i in candidates]), rest
        for i in candidates:
            extra = min(most - counts[i], max(1, budget * weights[i] // pool), rest)
            counts[i] = counts[i] + extra
            rest = rest - extra
    return np.array([most] + counts)


def uneven(key, count, total, bound, skew):
    if count == 2:
        one = jax.random.randint(key, (), max(1, total - bound), min(bound, total - 1) + 1)
        return jnp.stack([one, total - one])
    lengths = jnp.asarray(length_profile(count, total, bound, skew), jnp.int32)
    couples = (count - 1) // 2
    donor, taker = lengths[1:1 + 2 * couples:2], lengths[2:2 + 2 * couples:2]
    room = jnp.minimum(donor - 1, bound - taker)
    passed = jax.random.randint(jax.random.fold_in(key, 1), (couples,), 0, 1 << 20) % (room + 1)
    lengths = lengths.at[1:1 + 2 * couples:2].set(donor - passed).at[2:2 + 2 * couples:2].set(taker + passed)
    return lengths[jax.random.permutation(jax.random.fold_in(key, 2), count)]


def centred(own_key, extent, width, limit, cuts=(), kind=jnp.bfloat16):
    values = width * jax.random.normal(own_key, extent, jnp.float32)
    if cuts:
        values = values * levels(own_key, extent, cuts, -0.22, 0.18)
    return jnp.clip(values, -limit, limit).astype(kind)


def setup_inputs(seed: int = 0) -> dict:
    key_list = jax.random.split(jax.random.key(seed), 12)
    return {
        "hidden_in": draw_hidden_in(jax.random.fold_in(key_list[11], 71), 0),
        "norm_gain": jnp.clip(1.0 + 0.18 * jax.random.normal(key_list[1], (D,), jnp.float32), 0.099609375, 1.8984375).astype(jnp.bfloat16),
        "w_qkv": draw_w_qkv(jax.random.fold_in(key_list[11], 71), 0),
        "w_out": centred(key_list[3], (HQ * HD, D), (HQ * HD) ** -0.5, 0.125, ((0, 4), (1, 4))),
        "k_cache": draw_k_cache(jax.random.fold_in(key_list[11], 71), 0),
        "v_cache": draw_v_cache(jax.random.fold_in(key_list[11], 71), 0),
        "cache_lens": uneven(key_list[6], REQS, REQS * CACHE // 2, CACHE, 2).astype(jnp.int32),
        "home_slot": draw_home_slot(jax.random.fold_in(key_list[11], 71), 0),
        "parents": draw_parents(jax.random.fold_in(key_list[11], 71), 0),
        "tree_sizes": draw_tree_sizes(jax.random.fold_in(key_list[11], 71), 0),
        "leaf_node": set_ends(jax.random.randint(key_list[10], (REQS,), 0, TREE // 2), jax.random.fold_in(key_list[10], 1), 0, (TREE // 2) - 1).astype(jnp.int32),
    }


rope_base = 10000000.0
attn_mult = 0.015625
norm_eps = 1e-05
neg_fill = -1e+30

def ancestry(parent_rows):
    node_count = parent_rows.shape[-1]
    node_ids = jnp.arange(node_count, dtype=jnp.int32)
    linked = (node_ids[None, :] == parent_rows[:, None]) | (node_ids[None, :] == node_ids[:, None])
    reachable = linked.astype(jnp.float32)
    for repeat in range(max(1, (node_count - 1).bit_length())):
        reachable = jnp.minimum(jnp.dot(reachable, reachable, precision=lax.Precision.HIGHEST), 1.0)
    return reachable

def rotated(values, positions):
    half_size = values.shape[-1] // 2
    frequency = rope_base ** (-2.0 * jnp.arange(half_size, dtype=jnp.float32) / values.shape[-1])
    angles = positions.astype(jnp.float32)[..., None] * frequency
    cosine = jnp.cos(angles)
    sine_part = jnp.sin(angles)
    front_half = values[..., :half_size]
    back_half = values[..., half_size:]
    return jnp.concatenate([front_half * cosine - back_half * sine_part, back_half * cosine + front_half * sine_part], axis=-1)

def reference(hidden_in, norm_gain, w_qkv, w_out, k_cache, v_cache, cache_lens, home_slot, parents, tree_sizes, leaf_node):

    def per_request(request):
        rows_in = lax.dynamic_slice_in_dim(hidden_in, request * TREE, TREE, 0)
        slot_id = home_slot[request]
        cached_len = cache_lens[slot_id]
        keys_old = lax.dynamic_index_in_dim(k_cache, slot_id, 0, keepdims=False).astype(jnp.float32).reshape(CACHE, KVH, HD)
        values_old = lax.dynamic_index_in_dim(v_cache, slot_id, 0, keepdims=False).astype(jnp.float32).reshape(CACHE, KVH, HD)
        floats = rows_in.astype(jnp.float32)
        rms_inverse = lax.rsqrt(lax.optimization_barrier(jnp.mean(floats * floats, axis=1)) + norm_eps)
        scaled = (floats * norm_gain.astype(jnp.float32)).astype(jnp.bfloat16)
        projected = jnp.dot(scaled, w_qkv, preferred_element_type=jnp.float32) * rms_inverse[:, None]
        projected = projected.reshape(TREE, KVH, GROUP + 2, HD)
        ancestors = ancestry(parents[request])
        node_depth = lax.optimization_barrier(jnp.sum(ancestors > 0.5, axis=1)).astype(jnp.int32) - 1
        positions = cached_len + node_depth
        queries = rotated(projected[:, :, :GROUP, :], positions[:, None, None]).astype(jnp.bfloat16)
        keys_new = rotated(projected[:, :, GROUP, :], positions[:, None]).astype(jnp.bfloat16)
        values_new = projected[:, :, GROUP + 1, :].astype(jnp.bfloat16)
        query_float = queries.astype(jnp.float32)
        cache_scores = attn_mult * jnp.einsum('tkgd,pkd->kgtp', query_float, keys_old)
        tree_scores = attn_mult * jnp.einsum('tkgd,ukd->kgtu', query_float, keys_new.astype(jnp.float32))
        cache_mask = jnp.arange(CACHE, dtype=jnp.int32) < cached_len
        tree_mask = ancestors > 0.5
        cache_scores = jnp.where(cache_mask, cache_scores, neg_fill)
        tree_scores = jnp.where(tree_mask, tree_scores, neg_fill)
        top_score = jnp.maximum(lax.optimization_barrier(jnp.max(cache_scores, axis=-1)), lax.optimization_barrier(jnp.max(tree_scores, axis=-1)))
        cache_weights = jnp.where(cache_mask, jnp.exp(cache_scores - top_score[..., None]), 0.0)
        tree_weights = jnp.where(tree_mask, jnp.exp(tree_scores - top_score[..., None]), 0.0)
        weight_sum = lax.optimization_barrier(jnp.sum(cache_weights, axis=-1)) + lax.optimization_barrier(jnp.sum(tree_weights, axis=-1))
        cache_rounded = lax.optimization_barrier(cache_weights.astype(jnp.bfloat16)).astype(jnp.float32)
        tree_rounded = lax.optimization_barrier(tree_weights.astype(jnp.bfloat16)).astype(jnp.float32)
        summed = jnp.einsum('kgtp,pkd->tkgd', cache_rounded, values_old) + jnp.einsum('kgtu,ukd->tkgd', tree_rounded, values_new.astype(jnp.float32))
        attention = (summed / jnp.transpose(weight_sum, (2, 0, 1))[..., None]).astype(jnp.bfloat16)
        attention = attention.reshape(TREE, KVH * GROUP * HD)
        mixed_sum = floats + jnp.dot(attention, w_out, preferred_element_type=jnp.float32)
        real_slot = jnp.arange(TREE, dtype=jnp.int32) < tree_sizes[request]
        layer_rows = jnp.where(real_slot[:, None], mixed_sum, 0.0).astype(jnp.bfloat16)
        path_nodes = lax.dynamic_index_in_dim(ancestors, leaf_node[request], 0, keepdims=False)
        depth_hit = node_depth[None, :] == jnp.arange(ACC, dtype=jnp.int32)[:, None]
        chooser = jnp.where(depth_hit, path_nodes[None, :], 0.0)
        stacked = jnp.stack([keys_new.reshape(TREE, KVH * HD), values_new.reshape(TREE, KVH * HD)], axis=1).astype(jnp.float32)
        accepted = jnp.einsum('su,uwc->swc', chooser, stacked).astype(jnp.bfloat16)
        return (layer_rows, accepted)
    layer_rows, accepted = lax.map(per_request, jnp.arange(REQS, dtype=jnp.int32))
    return (layer_rows.reshape(REQS * TREE, D), accepted)
```

```python
import jax
import jax.numpy as jnp
from jax import lax
from jax.experimental import pallas as pl
from jax.experimental.pallas import tpu as pltpu
from jax.sharding import PartitionSpec as P

D = 2048
HD = 64
GROUP = 4
ACC = 8


rope_base = 10000000.0
attn_mult = 0.015625
norm_eps = 1e-05
neg_fill = -1e30


def joined(value, axis, join):
    pieces = jax.tree.map(lambda part: lax.all_gather(part, axis), value)
    head = jax.tree.map(lambda part: part[0], pieces)
    tail = jax.tree.map(lambda part: part[1:], pieces)
    so_far, _ = lax.scan(lambda so_far, slab: (join(so_far, slab), None), head, tail)
    return so_far


def ancestry(parent_rows):
    node_count = parent_rows.shape[-1]
    node_ids = jnp.arange(node_count, dtype=jnp.int32)
    linked = (node_ids[None, :] == parent_rows[:, None]) | (node_ids[None, :] == node_ids[:, None])
    reachable = linked.astype(jnp.float32)
    for repeat in range(max(1, (node_count - 1).bit_length())):
        reachable = jnp.minimum(jnp.dot(reachable, reachable, precision=lax.Precision.HIGHEST), 1.0)
    return reachable


def rotated(values, positions):
    half_size = values.shape[-1] // 2
    frequency = rope_base ** (-2.0 * jnp.arange(half_size, dtype=jnp.float32) / values.shape[-1])
    angles = positions.astype(jnp.float32)[..., None] * frequency
    cosine = jnp.cos(angles)
    sine_part = jnp.sin(angles)
    front_half = values[..., :half_size]
    back_half = values[..., half_size:]
    return jnp.concatenate(
        [front_half * cosine - back_half * sine_part, back_half * cosine + front_half * sine_part],
        axis=-1,
    )


def combine_stats(first_stats, second_stats):
    top_first, sum_first, summed_first = first_stats
    top_second, sum_second, summed_second = second_stats
    top_both = jnp.maximum(top_first, top_second)
    scale_first = jnp.exp(top_first - top_both)
    scale_second = jnp.exp(top_second - top_both)
    return (
        top_both,
        sum_first * scale_first + sum_second * scale_second,
        summed_first * scale_first[..., None] + summed_second * scale_second[..., None],
    )


def packed(values, index):
    return jnp.take(values, index, axis=0, mode="fill", fill_value=0)


def routing(home_slot, group_count, local_reqs):
    dest_group = (home_slot // local_reqs).reshape(group_count, local_reqs)
    local_ids = jnp.arange(local_reqs, dtype=jnp.int32)
    earlier = local_ids[None, :] < local_ids[:, None]
    same_dest = dest_group[:, :, None] == dest_group[:, None, :]
    dest_rank = jnp.sum(same_dest & earlier[None], axis=2)
    return (dest_group, dest_rank)


def tree_part(queries, keys_new, values_new, ancestors):
    scores = attn_mult * jnp.einsum(
        "rtkgd,rukd->rtkgu", queries, keys_new, preferred_element_type=jnp.float32
    )
    valid_keys = (ancestors > 0.5)[:, :, None, None, :]
    masked = jnp.where(valid_keys, scores, neg_fill)
    top_score = jnp.max(masked, axis=-1)
    weights = jnp.where(valid_keys, jnp.exp(masked - top_score[..., None]), 0.0)
    summed = jnp.einsum(
        "rtkgu,rukd->rtkgd",
        weights.astype(jnp.bfloat16),
        values_new,
        preferred_element_type=jnp.float32,
    )
    return (top_score, jnp.sum(weights, axis=-1), summed)


def cache_kernel(lens_ref, start_ref, q_ref, k_ref, v_ref, top_ref, sum_ref, acc_ref):
    slot = pl.program_id(0)
    head_local = q_ref.shape[1]
    cache_local = k_ref.shape[1]
    limit = lens_ref[slot] - start_ref[0]
    valid = lax.broadcasted_iota(jnp.int32, (1, cache_local), 1) < limit
    keys = k_ref[0]
    values = v_ref[0]
    lane = lax.broadcasted_iota(jnp.int32, (1, head_local * HD), 1)
    result = None
    for head in range(head_local):
        scores = attn_mult * lax.dot_general(
            q_ref[0, head], keys, (((1,), (1,)), ((), ())), preferred_element_type=jnp.float32
        )
        masked = jnp.where(valid, scores, neg_fill)
        top = jnp.max(masked, axis=1, keepdims=True)
        weights = jnp.where(valid, jnp.exp(masked - top), 0.0)
        summed = jnp.dot(weights.astype(jnp.bfloat16), values, preferred_element_type=jnp.float32)
        top_ref[0, head] = top
        sum_ref[0, head] = jnp.sum(weights, axis=1, keepdims=True)
        mine = (lane >= head * HD) & (lane < (head + 1) * HD)
        result = summed if result is None else jnp.where(mine, summed, result)
    acc_ref[0] = result


def cache_merged(slot_queries, k_cache, v_cache, home_lens):
    local_reqs, tree_slots, head_local = slot_queries.shape[:3]
    cache_local = k_cache.shape[1]
    width = head_local * HD
    rows = tree_slots * GROUP
    key_start = (lax.axis_index("ty") * cache_local).astype(jnp.int32).reshape(1)
    own_head = jnp.arange(head_local)[:, None] == jnp.arange(head_local)[None, :]
    spread = jnp.where(
        own_head[None, :, None, None, :, None],
        slot_queries.transpose(0, 2, 1, 3, 4)[:, :, :, :, None, :],
        jnp.zeros((), slot_queries.dtype),
    ).reshape(local_reqs, head_local, rows, width)
    top, total, summed = pl.pallas_call(
        cache_kernel,
        grid_spec=pltpu.PrefetchScalarGridSpec(
            num_scalar_prefetch=2,
            grid=(local_reqs,),
            in_specs=[
                pl.BlockSpec((1, head_local, rows, width), lambda s, lens, start: (s, 0, 0, 0)),
                pl.BlockSpec((1, cache_local, width), lambda s, lens, start: (s, 0, 0)),
                pl.BlockSpec((1, cache_local, width), lambda s, lens, start: (s, 0, 0)),
            ],
            out_specs=[
                pl.BlockSpec((1, head_local, rows, 1), lambda s, lens, start: (s, 0, 0, 0)),
                pl.BlockSpec((1, head_local, rows, 1), lambda s, lens, start: (s, 0, 0, 0)),
                pl.BlockSpec((1, rows, width), lambda s, lens, start: (s, 0, 0)),
            ],
        ),
        out_shape=[
            jax.ShapeDtypeStruct((local_reqs, head_local, rows, 1), jnp.float32),
            jax.ShapeDtypeStruct((local_reqs, head_local, rows, 1), jnp.float32),
            jax.ShapeDtypeStruct((local_reqs, rows, width), jnp.float32),
        ],
        cost_estimate=pl.CostEstimate(
            flops=4 * local_reqs * head_local * rows * cache_local * width,
            transcendentals=local_reqs * head_local * rows * cache_local,
            bytes_accessed=2 * k_cache.size * 2 + spread.size * 2 + local_reqs * rows * width * 4,
        ),
    )(home_lens, key_start, spread, k_cache, v_cache)
    top = top.reshape(local_reqs, head_local, tree_slots, GROUP).transpose(0, 2, 1, 3)
    total = total.reshape(local_reqs, head_local, tree_slots, GROUP).transpose(0, 2, 1, 3)
    summed = summed.reshape(local_reqs, tree_slots, GROUP, head_local, HD).transpose(0, 1, 3, 2, 4)
    top_all = lax.pmax(top, "ty")
    scale = jnp.exp(top - top_all)
    total, summed = lax.psum((total * scale, summed * scale[..., None]), "ty")
    return (top_all, total, summed)


def shards(
    hidden_in,
    norm_gain,
    w_qkv,
    w_out,
    k_cache,
    v_cache,
    cache_lens,
    home_slot,
    parents,
    tree_sizes,
    leaf_node,
):
    group_count = lax.axis_size("dp")
    group_index = lax.axis_index("dp")
    local_reqs = k_cache.shape[0]
    tree_slots = parents.shape[1]
    capacity = (local_reqs + group_count - 1) // group_count
    head_local = k_cache.shape[2] // HD
    row_count = hidden_in.shape[0]
    float_in = hidden_in.astype(jnp.float32)
    feature_local = hidden_in.shape[1]
    gain_part = lax.dynamic_slice_in_dim(
        norm_gain, lax.axis_index("ty") * feature_local, feature_local
    )
    scaled = (float_in * gain_part.astype(jnp.float32)).astype(jnp.bfloat16)
    partial_proj = jnp.dot(scaled, w_qkv, preferred_element_type=jnp.float32)
    partial_square = jnp.sum(float_in * float_in, axis=1)
    projected, square_sum = lax.psum((partial_proj, partial_square), "ty")
    rms_inverse = lax.rsqrt(square_sum / D + norm_eps)
    projected = (projected * rms_inverse[:, None]).reshape(
        local_reqs, tree_slots, head_local, GROUP + 2, HD
    )
    first_request = group_index * local_reqs
    local_ids = jnp.arange(local_reqs, dtype=jnp.int32)
    request_ids = jnp.arange(home_slot.shape[0], dtype=jnp.int32)
    my_parents = lax.dynamic_slice_in_dim(parents, first_request, local_reqs, 0)
    my_slots = lax.dynamic_slice_in_dim(home_slot, first_request, local_reqs, 0)
    ancestors = jax.vmap(ancestry)(my_parents)
    node_depth = jnp.sum(ancestors > 0.5, axis=2) - 1
    slot_match = my_slots[:, None] == request_ids[None, :]
    my_lens = jnp.sum(jnp.where(slot_match, cache_lens[None, :], 0), axis=1)
    positions = my_lens[:, None] + node_depth
    queries = rotated(projected[:, :, :, :GROUP, :], positions[:, :, None, None]).astype(
        jnp.bfloat16
    )
    keys_new = rotated(projected[:, :, :, GROUP, :], positions[:, :, None]).astype(jnp.bfloat16)
    values_new = projected[:, :, :, GROUP + 1, :].astype(jnp.bfloat16)
    dest_group, dest_rank = routing(home_slot, group_count, local_reqs)
    send_pos = lax.dynamic_index_in_dim(
        dest_group, group_index, 0, keepdims=False
    ) * capacity + lax.dynamic_index_in_dim(dest_rank, group_index, 0, keepdims=False)
    buffer_ids = jnp.arange(group_count * capacity, dtype=jnp.int32)
    send_hit = send_pos[None, :] == buffer_ids[:, None]
    send_index = jnp.where(
        jnp.any(send_hit, axis=1),
        jnp.sum(jnp.where(send_hit, local_ids[None, :], 0), axis=1),
        local_reqs,
    )
    target_slots = first_request + local_ids
    owner_match = home_slot[None, :] == target_slots[:, None]
    owner_request = jnp.sum(jnp.where(owner_match, request_ids[None, :], 0), axis=1)
    owner_rank = jnp.sum(jnp.where(owner_match, dest_rank.reshape(-1)[None, :], 0), axis=1)
    recv_index = owner_request // local_reqs * capacity + owner_rank
    back_hit = recv_index[None, :] == buffer_ids[:, None]
    back_index = jnp.where(
        jnp.any(back_hit, axis=1),
        jnp.sum(jnp.where(back_hit, local_ids[None, :], 0), axis=1),
        local_reqs,
    )
    home_lens = lax.dynamic_slice_in_dim(cache_lens, first_request, local_reqs, 0)
    arrived = lax.all_to_all(
        packed(queries.reshape(local_reqs, -1), send_index),
        "dp",
        split_axis=0,
        concat_axis=0,
        tiled=True,
    )
    slot_queries = packed(arrived, recv_index).reshape(queries.shape)
    top_score, weight_sum, summed = cache_merged(slot_queries, k_cache, v_cache, home_lens)
    normalized = summed / weight_sum[..., None]
    log_total = top_score + jnp.log(weight_sum)
    back_values, back_logs = (
        lax.all_to_all(
            packed(normalized.reshape(local_reqs, -1), back_index),
            "dp",
            split_axis=0,
            concat_axis=0,
            tiled=True,
        ),
        lax.all_to_all(
            packed(log_total.reshape(local_reqs, -1), back_index),
            "dp",
            split_axis=0,
            concat_axis=0,
            tiled=True,
        ),
    )
    cache_values = packed(back_values, send_pos).reshape(
        local_reqs, tree_slots, head_local, GROUP, HD
    )
    cache_top = packed(back_logs, send_pos).reshape(local_reqs, tree_slots, head_local, GROUP)
    tree_stats = tree_part(queries, keys_new, values_new, ancestors)
    top_all, sum_all, summed_all = combine_stats(
        (cache_top, jnp.ones_like(cache_top), cache_values), tree_stats
    )
    attention = (summed_all / sum_all[..., None]).astype(jnp.bfloat16)
    attention_rows = attention.reshape(row_count, -1)
    rows_mine = row_count // lax.axis_size("tx")
    mixed_sum = lax.psum_scatter(
        jnp.dot(attention_rows, w_out, preferred_element_type=jnp.float32),
        "tx",
        scatter_dimension=0,
        tiled=True,
    )
    row_start = lax.axis_index("tx") * rows_mine
    residual = lax.dynamic_slice_in_dim(float_in, row_start, rows_mine, 0)
    row_ids = row_start + jnp.arange(rows_mine, dtype=jnp.int32)
    request_of = row_ids // tree_slots
    slot_of = row_ids % tree_slots
    size_of = jnp.sum(
        jnp.where(request_of[:, None] == local_ids[None, :], tree_sizes[None, :], 0), axis=1
    )
    layer_out = jnp.where((slot_of < size_of)[:, None], residual + mixed_sum, 0.0).astype(
        jnp.bfloat16
    )
    node_ids = jnp.arange(tree_slots, dtype=jnp.int32)
    leaf_hit = (leaf_node[:, None] == node_ids[None, :]).astype(jnp.float32)
    path_nodes = jnp.einsum("rt,rtu->ru", leaf_hit, ancestors)
    depth_hit = node_depth[:, None, :] == jnp.arange(ACC, dtype=jnp.int32)[None, :, None]
    chooser = jnp.where(depth_hit, path_nodes[:, None, :], 0.0).astype(jnp.bfloat16)
    stacked = jnp.stack(
        [
            keys_new.reshape(local_reqs, tree_slots, -1),
            values_new.reshape(local_reqs, tree_slots, -1),
        ],
        axis=2,
    )
    accepted_kv = jnp.einsum(
        "rsu,ruwc->rswc", chooser, stacked, preferred_element_type=jnp.float32
    ).astype(jnp.bfloat16)
    return (layer_out, accepted_kv)


def solution(mesh):
    return jax.shard_map(
        shards,
        mesh=mesh,
        in_specs=(
            P("dp", "ty"),
            P(),
            P("ty", "tx"),
            P("tx", "ty"),
            P("dp", "ty", "tx"),
            P("dp", "ty", "tx"),
            P(),
            P(),
            P(),
            P("dp"),
            P("dp"),
        ),
        out_specs=(P(("dp", "tx"), "ty"), P("dp", None, None, "tx")),
        check_vma=False,
    )
```

```python
import jax
import jax.numpy as jnp
from jax import lax
from jax.experimental import pallas as pl
from jax.experimental.pallas import tpu as pltpu
from jax.sharding import PartitionSpec as P

D = 2048
HD = 64
GROUP = 4
ACC = 8


rope_base = 10000000.0
attn_mult = 0.015625
norm_eps = 1e-05
neg_fill = -1e30


def joined(value, axis, join):
    pieces = jax.tree.map(lambda part: lax.all_gather(part, axis), value)
    head = jax.tree.map(lambda part: part[0], pieces)
    tail = jax.tree.map(lambda part: part[1:], pieces)
    so_far, _ = lax.scan(lambda so_far, slab: (join(so_far, slab), None), head, tail)
    return so_far


def ancestry(parent_rows):
    node_count = parent_rows.shape[-1]
    node_ids = jnp.arange(node_count, dtype=jnp.int32)
    linked = (node_ids[None, :] == parent_rows[:, None]) | (node_ids[None, :] == node_ids[:, None])
    reachable = linked.astype(jnp.float32)
    for repeat in range(max(1, (node_count - 1).bit_length())):
        reachable = jnp.minimum(jnp.dot(reachable, reachable, precision=lax.Precision.HIGHEST), 1.0)
    return reachable


def rotated(values, positions):
    half_size = values.shape[-1] // 2
    frequency = rope_base ** (-2.0 * jnp.arange(half_size, dtype=jnp.float32) / values.shape[-1])
    angles = positions.astype(jnp.float32)[..., None] * frequency
    cosine = jnp.cos(angles)
    sine_part = jnp.sin(angles)
    front_half = values[..., :half_size]
    back_half = values[..., half_size:]
    return jnp.concatenate(
        [front_half * cosine - back_half * sine_part, back_half * cosine + front_half * sine_part],
        axis=-1,
    )


def combine_stats(first_stats, second_stats):
    top_first, sum_first, summed_first = first_stats
    top_second, sum_second, summed_second = second_stats
    top_both = jnp.maximum(top_first, top_second)
    scale_first = jnp.exp(top_first - top_both)
    scale_second = jnp.exp(top_second - top_both)
    return (
        top_both,
        sum_first * scale_first + sum_second * scale_second,
        summed_first * scale_first[..., None] + summed_second * scale_second[..., None],
    )


def packed(values, index):
    return jnp.take(values, index, axis=0, mode="fill", fill_value=0)


def routing(home_slot, group_count, local_reqs):
    dest_group = (home_slot // local_reqs).reshape(group_count, local_reqs)
    local_ids = jnp.arange(local_reqs, dtype=jnp.int32)
    earlier = local_ids[None, :] < local_ids[:, None]
    same_dest = dest_group[:, :, None] == dest_group[:, None, :]
    dest_rank = jnp.sum(same_dest & earlier[None], axis=2)
    return (dest_group, dest_rank)


def tree_part(queries, keys_new, values_new, ancestors):
    scores = attn_mult * jnp.einsum(
        "rtkgd,rukd->rtkgu", queries, keys_new, preferred_element_type=jnp.float32
    )
    valid_keys = (ancestors > 0.5)[:, :, None, None, :]
    masked = jnp.where(valid_keys, scores, neg_fill)
    top_score = jnp.max(masked, axis=-1)
    weights = jnp.where(valid_keys, jnp.exp(masked - top_score[..., None]), 0.0)
    summed = jnp.einsum(
        "rtkgu,rukd->rtkgd",
        weights.astype(jnp.bfloat16),
        values_new,
        preferred_element_type=jnp.float32,
    )
    return (top_score, jnp.sum(weights, axis=-1), summed)


def cache_kernel(lens_ref, start_ref, q_ref, k_ref, v_ref, top_ref, sum_ref, acc_ref):
    slot = pl.program_id(0)
    head_local = q_ref.shape[1]
    cache_local = k_ref.shape[1]
    limit = lens_ref[slot] - start_ref[0]
    valid = lax.broadcasted_iota(jnp.int32, (1, cache_local), 1) < limit
    keys = k_ref[0]
    values = v_ref[0]
    lane = lax.broadcasted_iota(jnp.int32, (1, head_local * HD), 1)
    result = None
    for head in range(head_local):
        scores = attn_mult * lax.dot_general(
            q_ref[0, head], keys, (((1,), (1,)), ((), ())), preferred_element_type=jnp.float32
        )
        masked = jnp.where(valid, scores, neg_fill)
        top = jnp.max(masked, axis=1, keepdims=True)
        weights = jnp.where(valid, jnp.exp(masked - top), 0.0)
        summed = jnp.dot(weights.astype(jnp.bfloat16), values, preferred_element_type=jnp.float32)
        top_ref[0, head] = top
        sum_ref[0, head] = jnp.sum(weights, axis=1, keepdims=True)
        mine = (lane >= head * HD) & (lane < (head + 1) * HD)
        result = summed if result is None else jnp.where(mine, summed, result)
    acc_ref[0] = result


def cache_merged(slot_queries, k_cache, v_cache, home_lens):
    local_reqs, tree_slots, head_local = slot_queries.shape[:3]
    cache_local = k_cache.shape[1]
    width = head_local * HD
    rows = tree_slots * GROUP
    key_start = (lax.axis_index("ty") * cache_local).astype(jnp.int32).reshape(1)
    own_head = jnp.arange(head_local)[:, None] == jnp.arange(head_local)[None, :]
    spread = jnp.where(
        own_head[None, :, None, None, :, None],
        slot_queries.transpose(0, 2, 1, 3, 4)[:, :, :, :, None, :],
        jnp.zeros((), slot_queries.dtype),
    ).reshape(local_reqs, head_local, rows, width)
    top, total, summed = pl.pallas_call(
        cache_kernel,
        grid_spec=pltpu.PrefetchScalarGridSpec(
            num_scalar_prefetch=2,
            grid=(local_reqs,),
            in_specs=[
                pl.BlockSpec((1, head_local, rows, width), lambda s, lens, start: (s, 0, 0, 0)),
                pl.BlockSpec((1, cache_local, width), lambda s, lens, start: (s, 0, 0)),
                pl.BlockSpec((1, cache_local, width), lambda s, lens, start: (s, 0, 0)),
            ],
            out_specs=[
                pl.BlockSpec((1, head_local, rows, 1), lambda s, lens, start: (s, 0, 0, 0)),
                pl.BlockSpec((1, head_local, rows, 1), lambda s, lens, start: (s, 0, 0, 0)),
                pl.BlockSpec((1, rows, width), lambda s, lens, start: (s, 0, 0)),
            ],
        ),
        out_shape=[
            jax.ShapeDtypeStruct((local_reqs, head_local, rows, 1), jnp.float32),
            jax.ShapeDtypeStruct((local_reqs, head_local, rows, 1), jnp.float32),
            jax.ShapeDtypeStruct((local_reqs, rows, width), jnp.float32),
        ],
        cost_estimate=pl.CostEstimate(
            flops=4 * local_reqs * head_local * rows * cache_local * width,
            transcendentals=local_reqs * head_local * rows * cache_local,
            bytes_accessed=2 * k_cache.size * 2 + spread.size * 2 + local_reqs * rows * width * 4,
        ),
    )(home_lens, key_start, spread, k_cache, v_cache)
    top = top.reshape(local_reqs, head_local, tree_slots, GROUP).transpose(0, 2, 1, 3)
    total = total.reshape(local_reqs, head_local, tree_slots, GROUP).transpose(0, 2, 1, 3)
    summed = summed.reshape(local_reqs, tree_slots, GROUP, head_local, HD).transpose(0, 1, 3, 2, 4)
    top_all = ty_max(top)
    scale = jnp.exp(top - top_all)
    count = total.size
    joint = jnp.concatenate(
        [(summed * scale[..., None]).reshape(-1, 128), (total * scale).reshape(count // 128, 128)],
        axis=0,
    )
    joint = lax.psum(joint, "ty")
    summed = joint[: summed.size // 128].reshape(summed.shape)
    total = joint[summed.size // 128 :].reshape(total.shape)
    return (top_all, total, summed)


def ty_max_kernel(x_ref, out_ref, held, send_sem, recv_sem):
    n = lax.axis_size("ty")
    me = lax.axis_index("ty")
    row = lax.axis_index("dp")
    col = lax.axis_index("tx")
    barrier = pltpu.get_barrier_semaphore()
    for step in range(1, n):
        peer = lax.rem(me + step, n)
        pl.semaphore_signal(
            barrier, inc=1, device_id=(row, col, peer), device_id_type=pl.DeviceIdType.MESH
        )
    pl.semaphore_wait(barrier, n - 1)
    copies = []
    for step in range(1, n):
        peer = lax.rem(me + step, n)
        copy = pltpu.make_async_remote_copy(
            src_ref=x_ref,
            dst_ref=held.at[step - 1],
            send_sem=send_sem.at[step - 1],
            recv_sem=recv_sem.at[step - 1],
            device_id=(row, col, peer),
            device_id_type=pl.DeviceIdType.MESH,
        )
        copy.start()
        copies.append(copy)
    for copy in copies:
        copy.wait()
    result = x_ref[...]
    for step in range(1, n):
        result = jnp.maximum(result, held[step - 1])
    out_ref[...] = result


def ty_max(values):
    n = lax.axis_size("ty")
    flat = values.reshape(-1, 128)
    out = pl.pallas_call(
        ty_max_kernel,
        out_shape=jax.ShapeDtypeStruct(flat.shape, flat.dtype),
        in_specs=[pl.BlockSpec(memory_space=pltpu.VMEM)],
        out_specs=pl.BlockSpec(memory_space=pltpu.VMEM),
        scratch_shapes=[
            pltpu.VMEM((n - 1,) + flat.shape, flat.dtype),
            pltpu.SemaphoreType.DMA((n - 1,)),
            pltpu.SemaphoreType.DMA((n - 1,)),
        ],
        compiler_params=pltpu.CompilerParams(collective_id=0, has_side_effects=True),
    )(flat)
    return out.reshape(values.shape)


def shards(
    hidden_in,
    norm_gain,
    w_qkv,
    w_out,
    k_cache,
    v_cache,
    cache_lens,
    home_slot,
    parents,
    tree_sizes,
    leaf_node,
):
    group_count = lax.axis_size("dp")
    group_index = lax.axis_index("dp")
    local_reqs = k_cache.shape[0]
    tree_slots = parents.shape[1]
    capacity = (local_reqs + group_count - 1) // group_count
    head_local = k_cache.shape[2] // HD
    row_count = hidden_in.shape[0]
    float_in = hidden_in.astype(jnp.float32)
    feature_local = hidden_in.shape[1]
    gain_part = lax.dynamic_slice_in_dim(
        norm_gain, lax.axis_index("ty") * feature_local, feature_local
    )
    scaled = (float_in * gain_part.astype(jnp.float32)).astype(jnp.bfloat16)
    partial_proj = jnp.dot(scaled, w_qkv, preferred_element_type=jnp.float32)
    partial_square = jnp.sum(float_in * float_in, axis=1)
    proj_cols = partial_proj.shape[1]
    square_rows = jnp.pad(
        partial_square.reshape(-1, 128), ((0, 0), (0, proj_cols - 128))
    )
    joint = lax.psum(jnp.concatenate([partial_proj, square_rows], axis=0), "ty")
    projected = joint[:row_count]
    square_sum = joint[row_count:, :128].reshape(row_count)
    rms_inverse = lax.rsqrt(square_sum / D + norm_eps)
    projected = (projected * rms_inverse[:, None]).reshape(
        local_reqs, tree_slots, head_local, GROUP + 2, HD
    )
    first_request = group_index * local_reqs
    local_ids = jnp.arange(local_reqs, dtype=jnp.int32)
    request_ids = jnp.arange(home_slot.shape[0], dtype=jnp.int32)
    my_parents = lax.dynamic_slice_in_dim(parents, first_request, local_reqs, 0)
    my_slots = lax.dynamic_slice_in_dim(home_slot, first_request, local_reqs, 0)
    ancestors = jax.vmap(ancestry)(my_parents)
    node_depth = jnp.sum(ancestors > 0.5, axis=2) - 1
    slot_match = my_slots[:, None] == request_ids[None, :]
    my_lens = jnp.sum(jnp.where(slot_match, cache_lens[None, :], 0), axis=1)
    positions = my_lens[:, None] + node_depth
    queries = rotated(projected[:, :, :, :GROUP, :], positions[:, :, None, None]).astype(
        jnp.bfloat16
    )
    keys_new = rotated(projected[:, :, :, GROUP, :], positions[:, :, None]).astype(jnp.bfloat16)
    values_new = projected[:, :, :, GROUP + 1, :].astype(jnp.bfloat16)
    dest_group, dest_rank = routing(home_slot, group_count, local_reqs)
    send_pos = lax.dynamic_index_in_dim(
        dest_group, group_index, 0, keepdims=False
    ) * capacity + lax.dynamic_index_in_dim(dest_rank, group_index, 0, keepdims=False)
    buffer_ids = jnp.arange(group_count * capacity, dtype=jnp.int32)
    send_hit = send_pos[None, :] == buffer_ids[:, None]
    send_index = jnp.where(
        jnp.any(send_hit, axis=1),
        jnp.sum(jnp.where(send_hit, local_ids[None, :], 0), axis=1),
        local_reqs,
    )
    target_slots = first_request + local_ids
    owner_match = home_slot[None, :] == target_slots[:, None]
    owner_request = jnp.sum(jnp.where(owner_match, request_ids[None, :], 0), axis=1)
    owner_rank = jnp.sum(jnp.where(owner_match, dest_rank.reshape(-1)[None, :], 0), axis=1)
    recv_index = owner_request // local_reqs * capacity + owner_rank
    back_hit = recv_index[None, :] == buffer_ids[:, None]
    back_index = jnp.where(
        jnp.any(back_hit, axis=1),
        jnp.sum(jnp.where(back_hit, local_ids[None, :], 0), axis=1),
        local_reqs,
    )
    home_lens = lax.dynamic_slice_in_dim(cache_lens, first_request, local_reqs, 0)
    arrived = lax.all_to_all(
        packed(queries.reshape(local_reqs, -1), send_index),
        "dp",
        split_axis=0,
        concat_axis=0,
        tiled=True,
    )
    slot_queries = packed(arrived, recv_index).reshape(queries.shape)
    top_score, weight_sum, summed = cache_merged(slot_queries, k_cache, v_cache, home_lens)
    normalized = summed / weight_sum[..., None]
    log_total = top_score + jnp.log(weight_sum)
    value_width = normalized.size // local_reqs
    log_flat = log_total.reshape(local_reqs, -1)
    log_high = lax.reduce_precision(log_flat, exponent_bits=8, mantissa_bits=7)
    log_rest = log_flat - log_high
    log_mid = lax.reduce_precision(log_rest, exponent_bits=8, mantissa_bits=7)
    log_low = log_rest - log_mid
    payload = jnp.concatenate(
        [normalized.reshape(local_reqs, -1), log_high, log_mid, log_low], axis=1
    ).astype(jnp.bfloat16)
    back = lax.all_to_all(
        packed(payload, back_index), "dp", split_axis=0, concat_axis=0, tiled=True
    )
    back = packed(back, send_pos).astype(jnp.float32)
    log_width = log_flat.shape[1]
    cache_values = back[:, :value_width].reshape(local_reqs, tree_slots, head_local, GROUP, HD)
    cache_top = (
        back[:, value_width : value_width + log_width]
        + back[:, value_width + log_width : value_width + 2 * log_width]
        + back[:, value_width + 2 * log_width :]
    ).reshape(local_reqs, tree_slots, head_local, GROUP)
    tree_stats = tree_part(queries, keys_new, values_new, ancestors)
    top_all, sum_all, summed_all = combine_stats(
        (cache_top, jnp.ones_like(cache_top), cache_values), tree_stats
    )
    attention = (summed_all / sum_all[..., None]).astype(jnp.bfloat16)
    attention_rows = attention.reshape(row_count, -1)
    rows_mine = row_count // lax.axis_size("tx")
    mixed_sum = lax.psum_scatter(
        jnp.dot(attention_rows, w_out, preferred_element_type=jnp.float32),
        "tx",
        scatter_dimension=0,
        tiled=True,
    )
    row_start = lax.axis_index("tx") * rows_mine
    residual = lax.dynamic_slice_in_dim(float_in, row_start, rows_mine, 0)
    row_ids = row_start + jnp.arange(rows_mine, dtype=jnp.int32)
    request_of = row_ids // tree_slots
    slot_of = row_ids % tree_slots
    size_of = jnp.sum(
        jnp.where(request_of[:, None] == local_ids[None, :], tree_sizes[None, :], 0), axis=1
    )
    layer_out = jnp.where((slot_of < size_of)[:, None], residual + mixed_sum, 0.0).astype(
        jnp.bfloat16
    )
    node_ids = jnp.arange(tree_slots, dtype=jnp.int32)
    leaf_hit = (leaf_node[:, None] == node_ids[None, :]).astype(jnp.float32)
    path_nodes = jnp.einsum("rt,rtu->ru", leaf_hit, ancestors)
    depth_hit = node_depth[:, None, :] == jnp.arange(ACC, dtype=jnp.int32)[None, :, None]
    chooser = jnp.where(depth_hit, path_nodes[:, None, :], 0.0).astype(jnp.bfloat16)
    stacked = jnp.stack(
        [
            keys_new.reshape(local_reqs, tree_slots, -1),
            values_new.reshape(local_reqs, tree_slots, -1),
        ],
        axis=2,
    )
    accepted_kv = jnp.einsum(
        "rsu,ruwc->rswc", chooser, stacked, preferred_element_type=jnp.float32
    ).astype(jnp.bfloat16)
    return (layer_out, accepted_kv)


def solution(mesh):
    return jax.shard_map(
        shards,
        mesh=mesh,
        in_specs=(
            P("dp", "ty"),
            P(),
            P("ty", "tx"),
            P("tx", "ty"),
            P("dp", "ty", "tx"),
            P("dp", "ty", "tx"),
            P(),
            P(),
            P(),
            P("dp"),
            P("dp"),
        ),
        out_specs=(P(("dp", "tx"), "ty"), P("dp", None, None, "tx")),
        check_vma=False,
    )
```

```python
import jax
import jax.numpy as jnp
from jax import lax
from jax.experimental import pallas as pl
from jax.experimental.pallas import tpu as pltpu
from jax.sharding import PartitionSpec as P

D = 2048
HD = 64
GROUP = 4
ACC = 8


rope_base = 10000000.0
attn_mult = 0.015625
norm_eps = 1e-05
neg_fill = -1e30


def joined(value, axis, join):
    pieces = jax.tree.map(lambda part: lax.all_gather(part, axis), value)
    head = jax.tree.map(lambda part: part[0], pieces)
    tail = jax.tree.map(lambda part: part[1:], pieces)
    so_far, _ = lax.scan(lambda so_far, slab: (join(so_far, slab), None), head, tail)
    return so_far


def ancestry(parent_rows):
    node_count = parent_rows.shape[-1]
    node_ids = jnp.arange(node_count, dtype=jnp.int32)
    linked = (node_ids[None, :] == parent_rows[:, None]) | (node_ids[None, :] == node_ids[:, None])
    reachable = linked.astype(jnp.float32)
    for repeat in range(max(1, (node_count - 1).bit_length())):
        reachable = jnp.minimum(jnp.dot(reachable, reachable, precision=lax.Precision.HIGHEST), 1.0)
    return reachable


def rotated(values, positions):
    half_size = values.shape[-1] // 2
    frequency = rope_base ** (-2.0 * jnp.arange(half_size, dtype=jnp.float32) / values.shape[-1])
    angles = positions.astype(jnp.float32)[..., None] * frequency
    cosine = jnp.cos(angles)
    sine_part = jnp.sin(angles)
    front_half = values[..., :half_size]
    back_half = values[..., half_size:]
    return jnp.concatenate(
        [front_half * cosine - back_half * sine_part, back_half * cosine + front_half * sine_part],
        axis=-1,
    )


def combine_stats(first_stats, second_stats):
    top_first, sum_first, summed_first = first_stats
    top_second, sum_second, summed_second = second_stats
    top_both = jnp.maximum(top_first, top_second)
    scale_first = jnp.exp(top_first - top_both)
    scale_second = jnp.exp(top_second - top_both)
    return (
        top_both,
        sum_first * scale_first + sum_second * scale_second,
        summed_first * scale_first[..., None] + summed_second * scale_second[..., None],
    )


def packed(values, index):
    return jnp.take(values, index, axis=0, mode="fill", fill_value=0)


def routing(home_slot, group_count, local_reqs):
    dest_group = (home_slot // local_reqs).reshape(group_count, local_reqs)
    local_ids = jnp.arange(local_reqs, dtype=jnp.int32)
    earlier = local_ids[None, :] < local_ids[:, None]
    same_dest = dest_group[:, :, None] == dest_group[:, None, :]
    dest_rank = jnp.sum(same_dest & earlier[None], axis=2)
    return (dest_group, dest_rank)


def tree_part(queries, keys_new, values_new, ancestors):
    scores = attn_mult * jnp.einsum(
        "rtkgd,rukd->rtkgu", queries, keys_new, preferred_element_type=jnp.float32
    )
    valid_keys = (ancestors > 0.5)[:, :, None, None, :]
    masked = jnp.where(valid_keys, scores, neg_fill)
    top_score = jnp.max(masked, axis=-1)
    weights = jnp.where(valid_keys, jnp.exp(masked - top_score[..., None]), 0.0)
    summed = jnp.einsum(
        "rtkgu,rukd->rtkgd",
        weights.astype(jnp.bfloat16),
        values_new,
        preferred_element_type=jnp.float32,
    )
    return (top_score, jnp.sum(weights, axis=-1), summed)


def cache_kernel(lens_ref, start_ref, q_ref, k_ref, v_ref, top_ref, sum_ref, acc_ref):
    slot = pl.program_id(0)
    head_local = top_ref.shape[1]
    cache_local = k_ref.shape[1]
    limit = lens_ref[slot] - start_ref[0]
    valid = lax.broadcasted_iota(jnp.int32, (1, cache_local), 1) < limit
    keys = k_ref[0]
    values = v_ref[0]
    lane = lax.broadcasted_iota(jnp.int32, (1, head_local * HD), 1)
    queries = q_ref[0] * jnp.asarray(attn_mult, q_ref.dtype)
    any_valid = limit > 0
    result = None
    for head in range(head_local):
        mine = (lane >= head * HD) & (lane < (head + 1) * HD)
        own = jnp.where(mine, queries, jnp.zeros((), queries.dtype))
        scores = lax.dot_general(
            own, keys, (((1,), (1,)), ((), ())), preferred_element_type=jnp.float32
        )
        masked = jnp.where(valid, scores, neg_fill)
        top = jnp.max(masked, axis=1, keepdims=True)
        weights = jnp.exp(masked - top)
        summed = jnp.dot(weights.astype(jnp.bfloat16), values, preferred_element_type=jnp.float32)
        top_ref[0, head] = top
        sum_ref[0, head] = jnp.where(any_valid, jnp.sum(weights, axis=1, keepdims=True), 0.0)
        result = summed if result is None else jnp.where(mine, summed, result)
    acc_ref[0] = jnp.where(any_valid, result, 0.0)


def cache_merged(slot_queries, k_cache, v_cache, home_lens):
    local_reqs, tree_slots, head_local = slot_queries.shape[:3]
    cache_local = k_cache.shape[1]
    width = head_local * HD
    rows = tree_slots * GROUP
    key_start = (lax.axis_index("ty") * cache_local).astype(jnp.int32).reshape(1)
    spread = slot_queries.transpose(0, 1, 3, 2, 4).reshape(local_reqs, rows, width)
    top, total, summed = pl.pallas_call(
        cache_kernel,
        grid_spec=pltpu.PrefetchScalarGridSpec(
            num_scalar_prefetch=2,
            grid=(local_reqs,),
            in_specs=[
                pl.BlockSpec((1, rows, width), lambda s, lens, start: (s, 0, 0)),
                pl.BlockSpec((1, cache_local, width), lambda s, lens, start: (s, 0, 0)),
                pl.BlockSpec((1, cache_local, width), lambda s, lens, start: (s, 0, 0)),
            ],
            out_specs=[
                pl.BlockSpec((1, head_local, rows, 1), lambda s, lens, start: (s, 0, 0, 0)),
                pl.BlockSpec((1, head_local, rows, 1), lambda s, lens, start: (s, 0, 0, 0)),
                pl.BlockSpec((1, rows, width), lambda s, lens, start: (s, 0, 0)),
            ],
        ),
        out_shape=[
            jax.ShapeDtypeStruct((local_reqs, head_local, rows, 1), jnp.float32),
            jax.ShapeDtypeStruct((local_reqs, head_local, rows, 1), jnp.float32),
            jax.ShapeDtypeStruct((local_reqs, rows, width), jnp.float32),
        ],
        cost_estimate=pl.CostEstimate(
            flops=4 * local_reqs * head_local * rows * cache_local * width,
            transcendentals=local_reqs * head_local * rows * cache_local,
            bytes_accessed=2 * k_cache.size * 2 + spread.size * 2 + local_reqs * rows * width * 4,
        ),
    )(home_lens, key_start, spread, k_cache, v_cache)
    top = top.reshape(local_reqs, head_local, tree_slots, GROUP).transpose(0, 2, 1, 3)
    total = total.reshape(local_reqs, head_local, tree_slots, GROUP).transpose(0, 2, 1, 3)
    summed = summed.reshape(local_reqs, tree_slots, GROUP, head_local, HD).transpose(0, 1, 3, 2, 4)
    top_all = ty_max(top)
    scale = jnp.exp(top - top_all)
    count = total.size
    joint = jnp.concatenate(
        [(summed * scale[..., None]).reshape(-1, 128), (total * scale).reshape(count // 128, 128)],
        axis=0,
    )
    joint = lax.psum(joint.astype(jnp.bfloat16), "ty").astype(jnp.float32)
    summed = joint[: summed.size // 128].reshape(summed.shape)
    total = joint[summed.size // 128 :].reshape(total.shape)
    return (top_all, total, summed)


def ty_max_kernel(x_ref, out_ref, held, send_sem, recv_sem):
    n = lax.axis_size("ty")
    me = lax.axis_index("ty")
    row = lax.axis_index("dp")
    col = lax.axis_index("tx")
    barrier = pltpu.get_barrier_semaphore()
    for step in range(1, n):
        peer = lax.rem(me + step, n)
        pl.semaphore_signal(
            barrier, inc=1, device_id=(row, col, peer), device_id_type=pl.DeviceIdType.MESH
        )
    pl.semaphore_wait(barrier, n - 1)
    copies = []
    for step in range(1, n):
        peer = lax.rem(me + step, n)
        copy = pltpu.make_async_remote_copy(
            src_ref=x_ref,
            dst_ref=held.at[step - 1],
            send_sem=send_sem.at[step - 1],
            recv_sem=recv_sem.at[step - 1],
            device_id=(row, col, peer),
            device_id_type=pl.DeviceIdType.MESH,
        )
        copy.start()
        copies.append(copy)
    for copy in copies:
        copy.wait()
    result = x_ref[...]
    for step in range(1, n):
        result = jnp.maximum(result, held[step - 1])
    out_ref[...] = result


def ty_max(values):
    n = lax.axis_size("ty")
    flat = values.reshape(-1, 128)
    out = pl.pallas_call(
        ty_max_kernel,
        out_shape=jax.ShapeDtypeStruct(flat.shape, flat.dtype),
        in_specs=[pl.BlockSpec(memory_space=pltpu.VMEM)],
        out_specs=pl.BlockSpec(memory_space=pltpu.VMEM),
        scratch_shapes=[
            pltpu.VMEM((n - 1,) + flat.shape, flat.dtype),
            pltpu.SemaphoreType.DMA((n - 1,)),
            pltpu.SemaphoreType.DMA((n - 1,)),
        ],
        compiler_params=pltpu.CompilerParams(collective_id=0, has_side_effects=True),
    )(flat)
    return out.reshape(values.shape)


def shards(
    hidden_in,
    norm_gain,
    w_qkv,
    w_out,
    k_cache,
    v_cache,
    cache_lens,
    home_slot,
    parents,
    tree_sizes,
    leaf_node,
):
    group_count = lax.axis_size("dp")
    group_index = lax.axis_index("dp")
    local_reqs = k_cache.shape[0]
    tree_slots = parents.shape[1]
    capacity = (local_reqs + group_count - 1) // group_count
    head_local = k_cache.shape[2] // HD
    row_count = hidden_in.shape[0]
    float_in = hidden_in.astype(jnp.float32)
    feature_local = hidden_in.shape[1]
    gain_part = lax.dynamic_slice_in_dim(
        norm_gain, lax.axis_index("ty") * feature_local, feature_local
    )
    scaled = (float_in * gain_part.astype(jnp.float32)).astype(jnp.bfloat16)
    partial_proj = jnp.dot(scaled, w_qkv, preferred_element_type=jnp.float32)
    partial_square = jnp.sum(float_in * float_in, axis=1)
    proj_cols = partial_proj.shape[1]
    square_rows = jnp.pad(
        partial_square.reshape(-1, 128), ((0, 0), (0, proj_cols - 128))
    )
    joint = lax.psum(jnp.concatenate([partial_proj, square_rows], axis=0), "ty")
    projected = joint[:row_count]
    square_sum = joint[row_count:, :128].reshape(row_count)
    rms_inverse = lax.rsqrt(square_sum / D + norm_eps)
    projected = (projected * rms_inverse[:, None]).reshape(
        local_reqs, tree_slots, head_local, GROUP + 2, HD
    )
    first_request = group_index * local_reqs
    local_ids = jnp.arange(local_reqs, dtype=jnp.int32)
    request_ids = jnp.arange(home_slot.shape[0], dtype=jnp.int32)
    my_parents = lax.dynamic_slice_in_dim(parents, first_request, local_reqs, 0)
    my_slots = lax.dynamic_slice_in_dim(home_slot, first_request, local_reqs, 0)
    ancestors = jax.vmap(ancestry)(my_parents)
    node_depth = jnp.sum(ancestors > 0.5, axis=2) - 1
    slot_match = my_slots[:, None] == request_ids[None, :]
    my_lens = jnp.sum(jnp.where(slot_match, cache_lens[None, :], 0), axis=1)
    positions = my_lens[:, None] + node_depth
    queries = rotated(projected[:, :, :, :GROUP, :], positions[:, :, None, None]).astype(
        jnp.bfloat16
    )
    keys_new = rotated(projected[:, :, :, GROUP, :], positions[:, :, None]).astype(jnp.bfloat16)
    values_new = projected[:, :, :, GROUP + 1, :].astype(jnp.bfloat16)
    dest_group, dest_rank = routing(home_slot, group_count, local_reqs)
    send_pos = lax.dynamic_index_in_dim(
        dest_group, group_index, 0, keepdims=False
    ) * capacity + lax.dynamic_index_in_dim(dest_rank, group_index, 0, keepdims=False)
    buffer_ids = jnp.arange(group_count * capacity, dtype=jnp.int32)
    send_hit = send_pos[None, :] == buffer_ids[:, None]
    send_index = jnp.where(
        jnp.any(send_hit, axis=1),
        jnp.sum(jnp.where(send_hit, local_ids[None, :], 0), axis=1),
        local_reqs,
    )
    target_slots = first_request + local_ids
    owner_match = home_slot[None, :] == target_slots[:, None]
    owner_request = jnp.sum(jnp.where(owner_match, request_ids[None, :], 0), axis=1)
    owner_rank = jnp.sum(jnp.where(owner_match, dest_rank.reshape(-1)[None, :], 0), axis=1)
    recv_index = owner_request // local_reqs * capacity + owner_rank
    back_hit = recv_index[None, :] == buffer_ids[:, None]
    back_index = jnp.where(
        jnp.any(back_hit, axis=1),
        jnp.sum(jnp.where(back_hit, local_ids[None, :], 0), axis=1),
        local_reqs,
    )
    home_lens = lax.dynamic_slice_in_dim(cache_lens, first_request, local_reqs, 0)
    arrived = lax.all_to_all(
        packed(queries.reshape(local_reqs, -1), send_index),
        "dp",
        split_axis=0,
        concat_axis=0,
        tiled=True,
    )
    slot_queries = packed(arrived, recv_index).reshape(queries.shape)
    top_score, weight_sum, summed = cache_merged(slot_queries, k_cache, v_cache, home_lens)
    normalized = summed / weight_sum[..., None]
    log_total = top_score + jnp.log(weight_sum)
    value_width = normalized.size // local_reqs
    log_flat = log_total.reshape(local_reqs, -1)
    log_high = lax.reduce_precision(log_flat, exponent_bits=8, mantissa_bits=7)
    log_rest = log_flat - log_high
    log_mid = lax.reduce_precision(log_rest, exponent_bits=8, mantissa_bits=7)
    log_low = log_rest - log_mid
    payload = jnp.concatenate(
        [normalized.reshape(local_reqs, -1), log_high, log_mid, log_low], axis=1
    ).astype(jnp.bfloat16)
    back = lax.all_to_all(
        packed(payload, back_index), "dp", split_axis=0, concat_axis=0, tiled=True
    )
    back = packed(back, send_pos).astype(jnp.float32)
    log_width = log_flat.shape[1]
    cache_values = back[:, :value_width].reshape(local_reqs, tree_slots, head_local, GROUP, HD)
    cache_top = (
        back[:, value_width : value_width + log_width]
        + back[:, value_width + log_width : value_width + 2 * log_width]
        + back[:, value_width + 2 * log_width :]
    ).reshape(local_reqs, tree_slots, head_local, GROUP)
    tree_stats = tree_part(queries, keys_new, values_new, ancestors)
    top_all, sum_all, summed_all = combine_stats(
        (cache_top, jnp.ones_like(cache_top), cache_values), tree_stats
    )
    attention = (summed_all / sum_all[..., None]).astype(jnp.bfloat16)
    attention_rows = attention.reshape(row_count, -1)
    rows_mine = row_count // lax.axis_size("tx")
    mixed_sum = lax.psum_scatter(
        jnp.dot(attention_rows, w_out, preferred_element_type=jnp.float32).astype(jnp.bfloat16),
        "tx",
        scatter_dimension=0,
        tiled=True,
    )
    row_start = lax.axis_index("tx") * rows_mine
    residual = lax.dynamic_slice_in_dim(float_in, row_start, rows_mine, 0)
    row_ids = row_start + jnp.arange(rows_mine, dtype=jnp.int32)
    request_of = row_ids // tree_slots
    slot_of = row_ids % tree_slots
    size_of = jnp.sum(
        jnp.where(request_of[:, None] == local_ids[None, :], tree_sizes[None, :], 0), axis=1
    )
    layer_out = jnp.where((slot_of < size_of)[:, None], residual + mixed_sum, 0.0).astype(
        jnp.bfloat16
    )
    node_ids = jnp.arange(tree_slots, dtype=jnp.int32)
    leaf_hit = (leaf_node[:, None] == node_ids[None, :]).astype(jnp.float32)
    path_nodes = jnp.einsum("rt,rtu->ru", leaf_hit, ancestors)
    depth_hit = node_depth[:, None, :] == jnp.arange(ACC, dtype=jnp.int32)[None, :, None]
    chooser = jnp.where(depth_hit, path_nodes[:, None, :], 0.0).astype(jnp.bfloat16)
    stacked = jnp.stack(
        [
            keys_new.reshape(local_reqs, tree_slots, -1),
            values_new.reshape(local_reqs, tree_slots, -1),
        ],
        axis=2,
    )
    accepted_kv = jnp.einsum(
        "rsu,ruwc->rswc", chooser, stacked, preferred_element_type=jnp.float32
    ).astype(jnp.bfloat16)
    return (layer_out, accepted_kv)


def solution(mesh):
    return jax.shard_map(
        shards,
        mesh=mesh,
        in_specs=(
            P("dp", "ty"),
            P(),
            P("ty", "tx"),
            P("tx", "ty"),
            P("dp", "ty", "tx"),
            P("dp", "ty", "tx"),
            P(),
            P(),
            P(),
            P("dp"),
            P("dp"),
        ),
        out_specs=(P(("dp", "tx"), "ty"), P("dp", None, None, "tx")),
        check_vma=False,
    )
```

```python
import functools

import jax
import jax.numpy as jnp
from jax import lax
from jax.experimental import pallas as pl
from jax.experimental.pallas import tpu as pltpu
from jax.sharding import PartitionSpec as P

D = 2048
HD = 64
GROUP = 4
ACC = 8


rope_base = 10000000.0
attn_mult = 0.015625
norm_eps = 1e-05
neg_fill = -1e30


def joined(value, axis, join):
    pieces = jax.tree.map(lambda part: lax.all_gather(part, axis), value)
    head = jax.tree.map(lambda part: part[0], pieces)
    tail = jax.tree.map(lambda part: part[1:], pieces)
    so_far, _ = lax.scan(lambda so_far, slab: (join(so_far, slab), None), head, tail)
    return so_far


def ancestry(parent_rows):
    node_count = parent_rows.shape[-1]
    node_ids = jnp.arange(node_count, dtype=jnp.int32)
    linked = (node_ids[None, :] == parent_rows[:, None]) | (node_ids[None, :] == node_ids[:, None])
    reachable = linked.astype(jnp.float32)
    for repeat in range(max(1, (node_count - 1).bit_length())):
        reachable = jnp.minimum(jnp.dot(reachable, reachable, precision=lax.Precision.HIGHEST), 1.0)
    return reachable


def rotated(values, positions):
    half_size = values.shape[-1] // 2
    frequency = rope_base ** (-2.0 * jnp.arange(half_size, dtype=jnp.float32) / values.shape[-1])
    angles = positions.astype(jnp.float32)[..., None] * frequency
    cosine = jnp.cos(angles)
    sine_part = jnp.sin(angles)
    front_half = values[..., :half_size]
    back_half = values[..., half_size:]
    return jnp.concatenate(
        [front_half * cosine - back_half * sine_part, back_half * cosine + front_half * sine_part],
        axis=-1,
    )


def combine_stats(first_stats, second_stats):
    top_first, sum_first, summed_first = first_stats
    top_second, sum_second, summed_second = second_stats
    top_both = jnp.maximum(top_first, top_second)
    scale_first = jnp.exp(top_first - top_both)
    scale_second = jnp.exp(top_second - top_both)
    return (
        top_both,
        sum_first * scale_first + sum_second * scale_second,
        summed_first * scale_first[..., None] + summed_second * scale_second[..., None],
    )


def packed(values, index):
    return jnp.take(values, index, axis=0, mode="fill", fill_value=0)


def routing(home_slot, group_count, local_reqs):
    dest_group = (home_slot // local_reqs).reshape(group_count, local_reqs)
    local_ids = jnp.arange(local_reqs, dtype=jnp.int32)
    earlier = local_ids[None, :] < local_ids[:, None]
    same_dest = dest_group[:, :, None] == dest_group[:, None, :]
    dest_rank = jnp.sum(same_dest & earlier[None], axis=2)
    return (dest_group, dest_rank)


def tree_part(queries, keys_new, values_new, ancestors):
    scores = attn_mult * jnp.einsum(
        "rtkgd,rukd->rtkgu", queries, keys_new, preferred_element_type=jnp.float32
    )
    valid_keys = (ancestors > 0.5)[:, :, None, None, :]
    masked = jnp.where(valid_keys, scores, neg_fill)
    top_score = jnp.max(masked, axis=-1)
    weights = jnp.where(valid_keys, jnp.exp(masked - top_score[..., None]), 0.0)
    summed = jnp.einsum(
        "rtkgu,rukd->rtkgd",
        weights.astype(jnp.bfloat16),
        values_new,
        preferred_element_type=jnp.float32,
    )
    return (top_score, jnp.sum(weights, axis=-1), summed)


def cache_kernel(lens_ref, start_ref, q_ref, k_ref, v_ref, top_ref, sum_ref, acc_ref):
    slot = pl.program_id(0)
    head_local = top_ref.shape[1]
    cache_local = k_ref.shape[1]
    limit = lens_ref[slot] - start_ref[0]
    valid = lax.broadcasted_iota(jnp.int32, (1, cache_local), 1) < limit
    keys = k_ref[0]
    values = v_ref[0]
    lane = lax.broadcasted_iota(jnp.int32, (1, head_local * HD), 1)
    queries = q_ref[0] * jnp.asarray(attn_mult, q_ref.dtype)
    any_valid = limit > 0
    result = None
    for head in range(head_local):
        mine = (lane >= head * HD) & (lane < (head + 1) * HD)
        own = jnp.where(mine, queries, jnp.zeros((), queries.dtype))
        scores = lax.dot_general(
            own, keys, (((1,), (1,)), ((), ())), preferred_element_type=jnp.float32
        )
        masked = jnp.where(valid, scores, neg_fill)
        top = jnp.max(masked, axis=1, keepdims=True)
        weights = jnp.exp(masked - top)
        summed = jnp.dot(weights.astype(jnp.bfloat16), values, preferred_element_type=jnp.float32)
        top_ref[0, head] = top
        sum_ref[0, head] = jnp.where(any_valid, jnp.sum(weights, axis=1, keepdims=True), 0.0)
        result = summed if result is None else jnp.where(mine, summed, result)
    acc_ref[0] = jnp.where(any_valid, result, 0.0)


def cache_merged(slot_queries, k_cache, v_cache, home_lens):
    local_reqs, tree_slots, head_local = slot_queries.shape[:3]
    cache_local = k_cache.shape[1]
    width = head_local * HD
    rows = tree_slots * GROUP
    key_start = (lax.axis_index("ty") * cache_local).astype(jnp.int32).reshape(1)
    spread = slot_queries.transpose(0, 1, 3, 2, 4).reshape(local_reqs, rows, width)
    top, total, summed = pl.pallas_call(
        cache_kernel,
        grid_spec=pltpu.PrefetchScalarGridSpec(
            num_scalar_prefetch=2,
            grid=(local_reqs,),
            in_specs=[
                pl.BlockSpec((1, rows, width), lambda s, lens, start: (s, 0, 0)),
                pl.BlockSpec((1, cache_local, width), lambda s, lens, start: (s, 0, 0)),
                pl.BlockSpec((1, cache_local, width), lambda s, lens, start: (s, 0, 0)),
            ],
            out_specs=[
                pl.BlockSpec((1, head_local, rows, 1), lambda s, lens, start: (s, 0, 0, 0)),
                pl.BlockSpec((1, head_local, rows, 1), lambda s, lens, start: (s, 0, 0, 0)),
                pl.BlockSpec((1, rows, width), lambda s, lens, start: (s, 0, 0)),
            ],
        ),
        out_shape=[
            jax.ShapeDtypeStruct((local_reqs, head_local, rows, 1), jnp.float32),
            jax.ShapeDtypeStruct((local_reqs, head_local, rows, 1), jnp.float32),
            jax.ShapeDtypeStruct((local_reqs, rows, width), jnp.float32),
        ],
        cost_estimate=pl.CostEstimate(
            flops=4 * local_reqs * head_local * rows * cache_local * width,
            transcendentals=local_reqs * head_local * rows * cache_local,
            bytes_accessed=2 * k_cache.size * 2 + spread.size * 2 + local_reqs * rows * width * 4,
        ),
    )(home_lens, key_start, spread, k_cache, v_cache)
    top = top.reshape(local_reqs, head_local, tree_slots, GROUP).transpose(0, 2, 1, 3)
    total = total.reshape(local_reqs, head_local, tree_slots, GROUP).transpose(0, 2, 1, 3)
    summed = summed.reshape(local_reqs, tree_slots, GROUP, head_local, HD).transpose(0, 1, 3, 2, 4)
    top_all = ty_max(top)
    scale = jnp.exp(top - top_all)
    count = total.size
    joint = jnp.concatenate(
        [(summed * scale[..., None]).reshape(-1, 128), (total * scale).reshape(count // 128, 128)],
        axis=0,
    )
    joint = axis_sum(joint, "ty", True, jnp.bfloat16, jnp.bfloat16, 2)[: joint.shape[0]]
    joint = joint.astype(jnp.float32)
    summed = joint[: summed.size // 128].reshape(summed.shape)
    total = joint[summed.size // 128 :].reshape(total.shape)
    return (top_all, total, summed)


def ty_max_kernel(x_ref, out_ref, held, send_sem, recv_sem):
    n = lax.axis_size("ty")
    me = lax.axis_index("ty")
    row = lax.axis_index("dp")
    col = lax.axis_index("tx")
    barrier = pltpu.get_barrier_semaphore()
    for step in range(1, n):
        peer = lax.rem(me + step, n)
        pl.semaphore_signal(
            barrier, inc=1, device_id=(row, col, peer), device_id_type=pl.DeviceIdType.MESH
        )
    pl.semaphore_wait(barrier, n - 1)
    copies = []
    for step in range(1, n):
        peer = lax.rem(me + step, n)
        copy = pltpu.make_async_remote_copy(
            src_ref=x_ref,
            dst_ref=held.at[step - 1],
            send_sem=send_sem.at[step - 1],
            recv_sem=recv_sem.at[step - 1],
            device_id=(row, col, peer),
            device_id_type=pl.DeviceIdType.MESH,
        )
        copy.start()
        copies.append(copy)
    for copy in copies:
        copy.wait()
    result = x_ref[...]
    for step in range(1, n):
        result = jnp.maximum(result, held[step - 1])
    out_ref[...] = result


def axis_sum_kernel(axis, gather, x_ref, out_ref, held, gathered, sems):
    n = lax.axis_size(axis)
    me = lax.axis_index(axis)
    chunk = held.shape[1]
    where = {name: lax.axis_index(name) for name in ("dp", "tx", "ty")}

    def device(peer):
        return tuple(peer if name == axis else where[name] for name in ("dp", "tx", "ty"))

    barrier = pltpu.get_barrier_semaphore()
    for step in range(1, n):
        pl.semaphore_signal(
            barrier, inc=1, device_id=device(lax.rem(me + step, n)), device_id_type=pl.DeviceIdType.MESH
        )
    pl.semaphore_wait(barrier, n - 1)
    copies = []
    for step in range(1, n):
        peer = lax.rem(me + step, n)
        copy = pltpu.make_async_remote_copy(
            src_ref=x_ref.at[pl.ds(pl.multiple_of(peer * chunk, 16), chunk)],
            dst_ref=held.at[step - 1],
            send_sem=sems.at[0, step - 1],
            recv_sem=sems.at[1, step - 1],
            device_id=device(peer),
            device_id_type=pl.DeviceIdType.MESH,
        )
        copy.start()
        copies.append(copy)
    for copy in copies:
        copy.wait()
    own = pl.ds(pl.multiple_of(me * chunk, 16), chunk)
    total = x_ref[own].astype(jnp.float32)
    for step in range(1, n):
        total = total + held[step - 1].astype(jnp.float32)
    if not gather:
        out_ref[...] = total.astype(out_ref.dtype)
        return
    out_ref[own] = total.astype(out_ref.dtype)
    copies = []
    for step in range(1, n):
        peer = lax.rem(me + step, n)
        copy = pltpu.make_async_remote_copy(
            src_ref=out_ref.at[own],
            dst_ref=gathered.at[step - 1],
            send_sem=sems.at[2, step - 1],
            recv_sem=sems.at[3, step - 1],
            device_id=device(peer),
            device_id_type=pl.DeviceIdType.MESH,
        )
        copy.start()
        copies.append(copy)
    for copy in copies:
        copy.wait()
    for step in range(1, n):
        source = lax.rem(me - step + n, n)
        out_ref[pl.ds(pl.multiple_of(source * chunk, 16), chunk)] = gathered[step - 1]


def axis_sum(values, axis, gather, send_type, out_type, collective_id):
    n = lax.axis_size(axis)
    flat = values.reshape(-1, 128).astype(send_type)
    rows = flat.shape[0]
    padded = -(-rows // (16 * n)) * 16 * n
    flat = jnp.pad(flat, ((0, padded - rows), (0, 0)))
    chunk = padded // n
    out = pl.pallas_call(
        functools.partial(axis_sum_kernel, axis, gather),
        out_shape=jax.ShapeDtypeStruct((padded if gather else chunk, 128), out_type),
        in_specs=[pl.BlockSpec(memory_space=pltpu.VMEM)],
        out_specs=pl.BlockSpec(memory_space=pltpu.VMEM),
        scratch_shapes=[
            pltpu.VMEM((n - 1, chunk, 128), send_type),
            pltpu.VMEM((n - 1, chunk, 128), out_type),
            pltpu.SemaphoreType.DMA((4, n - 1)),
        ],
        compiler_params=pltpu.CompilerParams(collective_id=collective_id, has_side_effects=True),
    )(flat)
    return out


def ty_max(values):
    n = lax.axis_size("ty")
    flat = values.reshape(-1, 128)
    out = pl.pallas_call(
        ty_max_kernel,
        out_shape=jax.ShapeDtypeStruct(flat.shape, flat.dtype),
        in_specs=[pl.BlockSpec(memory_space=pltpu.VMEM)],
        out_specs=pl.BlockSpec(memory_space=pltpu.VMEM),
        scratch_shapes=[
            pltpu.VMEM((n - 1,) + flat.shape, flat.dtype),
            pltpu.SemaphoreType.DMA((n - 1,)),
            pltpu.SemaphoreType.DMA((n - 1,)),
        ],
        compiler_params=pltpu.CompilerParams(collective_id=0, has_side_effects=True),
    )(flat)
    return out.reshape(values.shape)


def shards(
    hidden_in,
    norm_gain,
    w_qkv,
    w_out,
    k_cache,
    v_cache,
    cache_lens,
    home_slot,
    parents,
    tree_sizes,
    leaf_node,
):
    group_count = lax.axis_size("dp")
    group_index = lax.axis_index("dp")
    local_reqs = k_cache.shape[0]
    tree_slots = parents.shape[1]
    capacity = (local_reqs + group_count - 1) // group_count
    head_local = k_cache.shape[2] // HD
    row_count = hidden_in.shape[0]
    float_in = hidden_in.astype(jnp.float32)
    feature_local = hidden_in.shape[1]
    gain_part = lax.dynamic_slice_in_dim(
        norm_gain, lax.axis_index("ty") * feature_local, feature_local
    )
    scaled = (float_in * gain_part.astype(jnp.float32)).astype(jnp.bfloat16)
    partial_proj = jnp.dot(scaled, w_qkv, preferred_element_type=jnp.float32)
    partial_square = jnp.sum(float_in * float_in, axis=1)
    proj_cols = partial_proj.shape[1]
    square_rows = jnp.pad(
        partial_square.reshape(-1, 128), ((0, 0), (0, proj_cols - 128))
    )
    joint = jnp.concatenate([partial_proj, square_rows], axis=0)
    joint = axis_sum(joint, "ty", True, jnp.float32, jnp.float32, 1)[: joint.size // 128]
    joint = joint.reshape(-1, proj_cols)
    projected = joint[:row_count]
    square_sum = joint[row_count:, :128].reshape(row_count)
    rms_inverse = lax.rsqrt(square_sum / D + norm_eps)
    projected = (projected * rms_inverse[:, None]).reshape(
        local_reqs, tree_slots, head_local, GROUP + 2, HD
    )
    first_request = group_index * local_reqs
    local_ids = jnp.arange(local_reqs, dtype=jnp.int32)
    request_ids = jnp.arange(home_slot.shape[0], dtype=jnp.int32)
    my_parents = lax.dynamic_slice_in_dim(parents, first_request, local_reqs, 0)
    my_slots = lax.dynamic_slice_in_dim(home_slot, first_request, local_reqs, 0)
    ancestors = jax.vmap(ancestry)(my_parents)
    node_depth = jnp.sum(ancestors > 0.5, axis=2) - 1
    slot_match = my_slots[:, None] == request_ids[None, :]
    my_lens = jnp.sum(jnp.where(slot_match, cache_lens[None, :], 0), axis=1)
    positions = my_lens[:, None] + node_depth
    queries = rotated(projected[:, :, :, :GROUP, :], positions[:, :, None, None]).astype(
        jnp.bfloat16
    )
    keys_new = rotated(projected[:, :, :, GROUP, :], positions[:, :, None]).astype(jnp.bfloat16)
    values_new = projected[:, :, :, GROUP + 1, :].astype(jnp.bfloat16)
    dest_group, dest_rank = routing(home_slot, group_count, local_reqs)
    send_pos = lax.dynamic_index_in_dim(
        dest_group, group_index, 0, keepdims=False
    ) * capacity + lax.dynamic_index_in_dim(dest_rank, group_index, 0, keepdims=False)
    buffer_ids = jnp.arange(group_count * capacity, dtype=jnp.int32)
    send_hit = send_pos[None, :] == buffer_ids[:, None]
    send_index = jnp.where(
        jnp.any(send_hit, axis=1),
        jnp.sum(jnp.where(send_hit, local_ids[None, :], 0), axis=1),
        local_reqs,
    )
    target_slots = first_request + local_ids
    owner_match = home_slot[None, :] == target_slots[:, None]
    owner_request = jnp.sum(jnp.where(owner_match, request_ids[None, :], 0), axis=1)
    owner_rank = jnp.sum(jnp.where(owner_match, dest_rank.reshape(-1)[None, :], 0), axis=1)
    recv_index = owner_request // local_reqs * capacity + owner_rank
    back_hit = recv_index[None, :] == buffer_ids[:, None]
    back_index = jnp.where(
        jnp.any(back_hit, axis=1),
        jnp.sum(jnp.where(back_hit, local_ids[None, :], 0), axis=1),
        local_reqs,
    )
    home_lens = lax.dynamic_slice_in_dim(cache_lens, first_request, local_reqs, 0)
    arrived = lax.all_to_all(
        packed(queries.reshape(local_reqs, -1), send_index),
        "dp",
        split_axis=0,
        concat_axis=0,
        tiled=True,
    )
    slot_queries = packed(arrived, recv_index).reshape(queries.shape)
    top_score, weight_sum, summed = cache_merged(slot_queries, k_cache, v_cache, home_lens)
    normalized = summed / weight_sum[..., None]
    log_total = top_score + jnp.log(weight_sum)
    value_width = normalized.size // local_reqs
    log_flat = log_total.reshape(local_reqs, -1)
    log_high = lax.reduce_precision(log_flat, exponent_bits=8, mantissa_bits=7)
    log_rest = log_flat - log_high
    log_mid = lax.reduce_precision(log_rest, exponent_bits=8, mantissa_bits=7)
    log_low = log_rest - log_mid
    payload = jnp.concatenate(
        [normalized.reshape(local_reqs, -1), log_high, log_mid, log_low], axis=1
    ).astype(jnp.bfloat16)
    back = lax.all_to_all(
        packed(payload, back_index), "dp", split_axis=0, concat_axis=0, tiled=True
    )
    back = packed(back, send_pos).astype(jnp.float32)
    log_width = log_flat.shape[1]
    cache_values = back[:, :value_width].reshape(local_reqs, tree_slots, head_local, GROUP, HD)
    cache_top = (
        back[:, value_width : value_width + log_width]
        + back[:, value_width + log_width : value_width + 2 * log_width]
        + back[:, value_width + 2 * log_width :]
    ).reshape(local_reqs, tree_slots, head_local, GROUP)
    tree_stats = tree_part(queries, keys_new, values_new, ancestors)
    top_all, sum_all, summed_all = combine_stats(
        (cache_top, jnp.ones_like(cache_top), cache_values), tree_stats
    )
    attention = (summed_all / sum_all[..., None]).astype(jnp.bfloat16)
    attention_rows = attention.reshape(row_count, -1)
    rows_mine = row_count // lax.axis_size("tx")
    mixed_sum = axis_sum(
        jnp.dot(attention_rows, w_out, preferred_element_type=jnp.float32),
        "tx",
        False,
        jnp.bfloat16,
        jnp.float32,
        3,
    ).reshape(row_count // lax.axis_size("tx"), -1)
    row_start = lax.axis_index("tx") * rows_mine
    residual = lax.dynamic_slice_in_dim(float_in, row_start, rows_mine, 0)
    row_ids = row_start + jnp.arange(rows_mine, dtype=jnp.int32)
    request_of = row_ids // tree_slots
    slot_of = row_ids % tree_slots
    size_of = jnp.sum(
        jnp.where(request_of[:, None] == local_ids[None, :], tree_sizes[None, :], 0), axis=1
    )
    layer_out = jnp.where((slot_of < size_of)[:, None], residual + mixed_sum, 0.0).astype(
        jnp.bfloat16
    )
    node_ids = jnp.arange(tree_slots, dtype=jnp.int32)
    leaf_hit = (leaf_node[:, None] == node_ids[None, :]).astype(jnp.float32)
    path_nodes = jnp.einsum("rt,rtu->ru", leaf_hit, ancestors)
    depth_hit = node_depth[:, None, :] == jnp.arange(ACC, dtype=jnp.int32)[None, :, None]
    chooser = jnp.where(depth_hit, path_nodes[:, None, :], 0.0).astype(jnp.bfloat16)
    stacked = jnp.stack(
        [
            keys_new.reshape(local_reqs, tree_slots, -1),
            values_new.reshape(local_reqs, tree_slots, -1),
        ],
        axis=2,
    )
    accepted_kv = jnp.einsum(
        "rsu,ruwc->rswc", chooser, stacked, preferred_element_type=jnp.float32
    ).astype(jnp.bfloat16)
    return (layer_out, accepted_kv)


def solution(mesh):
    return jax.shard_map(
        shards,
        mesh=mesh,
        in_specs=(
            P("dp", "ty"),
            P(),
            P("ty", "tx"),
            P("tx", "ty"),
            P("dp", "ty", "tx"),
            P("dp", "ty", "tx"),
            P(),
            P(),
            P(),
            P("dp"),
            P("dp"),
        ),
        out_specs=(P(("dp", "tx"), "ty"), P("dp", None, None, "tx")),
        check_vma=False,
    )
```

```python
import functools

import jax
import jax.numpy as jnp
from jax import lax
from jax.experimental import pallas as pl
from jax.experimental.pallas import tpu as pltpu
from jax.sharding import PartitionSpec as P

D = 2048
HD = 64
GROUP = 4
ACC = 8


rope_base = 10000000.0
attn_mult = 0.015625
norm_eps = 1e-05
neg_fill = -1e30


def joined(value, axis, join):
    pieces = jax.tree.map(lambda part: lax.all_gather(part, axis), value)
    head = jax.tree.map(lambda part: part[0], pieces)
    tail = jax.tree.map(lambda part: part[1:], pieces)
    so_far, _ = lax.scan(lambda so_far, slab: (join(so_far, slab), None), head, tail)
    return so_far


def ancestry(parent_rows):
    node_count = parent_rows.shape[-1]
    node_ids = jnp.arange(node_count, dtype=jnp.int32)
    linked = (node_ids[None, :] == parent_rows[:, None]) | (node_ids[None, :] == node_ids[:, None])
    reachable = linked.astype(jnp.float32)
    for repeat in range(max(1, (node_count - 1).bit_length())):
        reachable = jnp.minimum(jnp.dot(reachable, reachable, precision=lax.Precision.HIGHEST), 1.0)
    return reachable


def rotated(values, positions):
    half_size = values.shape[-1] // 2
    frequency = rope_base ** (-2.0 * jnp.arange(half_size, dtype=jnp.float32) / values.shape[-1])
    angles = positions.astype(jnp.float32)[..., None] * frequency
    cosine = jnp.cos(angles)
    sine_part = jnp.sin(angles)
    front_half = values[..., :half_size]
    back_half = values[..., half_size:]
    return jnp.concatenate(
        [front_half * cosine - back_half * sine_part, back_half * cosine + front_half * sine_part],
        axis=-1,
    )


def combine_stats(first_stats, second_stats):
    top_first, sum_first, summed_first = first_stats
    top_second, sum_second, summed_second = second_stats
    top_both = jnp.maximum(top_first, top_second)
    scale_first = jnp.exp(top_first - top_both)
    scale_second = jnp.exp(top_second - top_both)
    return (
        top_both,
        sum_first * scale_first + sum_second * scale_second,
        summed_first * scale_first[..., None] + summed_second * scale_second[..., None],
    )


def packed(values, index):
    return jnp.take(values, index, axis=0, mode="fill", fill_value=0)


def routing(home_slot, group_count, local_reqs):
    dest_group = (home_slot // local_reqs).reshape(group_count, local_reqs)
    local_ids = jnp.arange(local_reqs, dtype=jnp.int32)
    earlier = local_ids[None, :] < local_ids[:, None]
    same_dest = dest_group[:, :, None] == dest_group[:, None, :]
    dest_rank = jnp.sum(same_dest & earlier[None], axis=2)
    return (dest_group, dest_rank)


def tree_part(queries, keys_new, values_new, ancestors):
    scores = attn_mult * jnp.einsum(
        "rtkgd,rukd->rtkgu", queries, keys_new, preferred_element_type=jnp.float32
    )
    valid_keys = (ancestors > 0.5)[:, :, None, None, :]
    masked = jnp.where(valid_keys, scores, neg_fill)
    top_score = jnp.max(masked, axis=-1)
    weights = jnp.where(valid_keys, jnp.exp(masked - top_score[..., None]), 0.0)
    summed = jnp.einsum(
        "rtkgu,rukd->rtkgd",
        weights.astype(jnp.bfloat16),
        values_new,
        preferred_element_type=jnp.float32,
    )
    return (top_score, jnp.sum(weights, axis=-1), summed)


def cache_kernel(lens_ref, start_ref, q_ref, k_ref, v_ref, top_ref, sum_ref, acc_ref):
    slot = pl.program_id(0)
    head_local = top_ref.shape[1]
    cache_local = k_ref.shape[1]
    limit = lens_ref[slot] - start_ref[0]
    valid = lax.broadcasted_iota(jnp.int32, (1, cache_local), 1) < limit
    keys = k_ref[0]
    values = v_ref[0]
    lane = lax.broadcasted_iota(jnp.int32, (1, head_local * HD), 1)
    queries = q_ref[0] * jnp.asarray(attn_mult, q_ref.dtype)
    any_valid = limit > 0
    result = None
    for head in range(head_local):
        mine = (lane >= head * HD) & (lane < (head + 1) * HD)
        own = jnp.where(mine, queries, jnp.zeros((), queries.dtype))
        scores = lax.dot_general(
            own, keys, (((1,), (1,)), ((), ())), preferred_element_type=jnp.float32
        )
        masked = jnp.where(valid, scores, neg_fill)
        top = jnp.max(masked, axis=1, keepdims=True)
        weights = jnp.exp(masked - top)
        summed = jnp.dot(weights.astype(jnp.bfloat16), values, preferred_element_type=jnp.float32)
        top_ref[0, head] = top
        sum_ref[0, head] = jnp.where(any_valid, jnp.sum(weights, axis=1, keepdims=True), 0.0)
        result = summed if result is None else jnp.where(mine, summed, result)
    acc_ref[0] = jnp.where(any_valid, result, 0.0)


def cache_merged(slot_queries, k_cache, v_cache, home_lens):
    local_reqs, tree_slots, head_local = slot_queries.shape[:3]
    cache_local = k_cache.shape[1]
    width = head_local * HD
    rows = tree_slots * GROUP
    key_start = (lax.axis_index("ty") * cache_local).astype(jnp.int32).reshape(1)
    spread = slot_queries.transpose(0, 1, 3, 2, 4).reshape(local_reqs, rows, width)
    top, total, summed = pl.pallas_call(
        cache_kernel,
        grid_spec=pltpu.PrefetchScalarGridSpec(
            num_scalar_prefetch=2,
            grid=(local_reqs,),
            in_specs=[
                pl.BlockSpec((1, rows, width), lambda s, lens, start: (s, 0, 0)),
                pl.BlockSpec((1, cache_local, width), lambda s, lens, start: (s, 0, 0)),
                pl.BlockSpec((1, cache_local, width), lambda s, lens, start: (s, 0, 0)),
            ],
            out_specs=[
                pl.BlockSpec((1, head_local, rows, 1), lambda s, lens, start: (s, 0, 0, 0)),
                pl.BlockSpec((1, head_local, rows, 1), lambda s, lens, start: (s, 0, 0, 0)),
                pl.BlockSpec((1, rows, width), lambda s, lens, start: (s, 0, 0)),
            ],
        ),
        out_shape=[
            jax.ShapeDtypeStruct((local_reqs, head_local, rows, 1), jnp.float32),
            jax.ShapeDtypeStruct((local_reqs, head_local, rows, 1), jnp.float32),
            jax.ShapeDtypeStruct((local_reqs, rows, width), jnp.float32),
        ],
        cost_estimate=pl.CostEstimate(
            flops=4 * local_reqs * head_local * rows * cache_local * width,
            transcendentals=local_reqs * head_local * rows * cache_local,
            bytes_accessed=2 * k_cache.size * 2 + spread.size * 2 + local_reqs * rows * width * 4,
        ),
    )(home_lens, key_start, spread, k_cache, v_cache)
    top = top.reshape(local_reqs, head_local, tree_slots, GROUP).transpose(0, 2, 1, 3)
    total = total.reshape(local_reqs, head_local, tree_slots, GROUP).transpose(0, 2, 1, 3)
    summed = summed.reshape(local_reqs, tree_slots, GROUP, head_local, HD).transpose(0, 1, 3, 2, 4)
    top_all = ty_max(top)
    scale = jnp.exp(top - top_all)
    count = total.size
    joint = jnp.concatenate(
        [(summed * scale[..., None]).reshape(-1, 128), (total * scale).reshape(count // 128, 128)],
        axis=0,
    )
    joint = axis_sum(joint, "ty", True, jnp.bfloat16, jnp.bfloat16, 2)[: joint.shape[0]]
    joint = joint.astype(jnp.float32)
    summed = joint[: summed.size // 128].reshape(summed.shape)
    total = joint[summed.size // 128 :].reshape(total.shape)
    return (top_all, total, summed)


def ty_max_kernel(x_ref, out_ref, held, send_sem, recv_sem):
    n = lax.axis_size("ty")
    me = lax.axis_index("ty")
    row = lax.axis_index("dp")
    col = lax.axis_index("tx")
    barrier = pltpu.get_barrier_semaphore()
    for step in range(1, n):
        peer = lax.rem(me + step, n)
        pl.semaphore_signal(
            barrier, inc=1, device_id=(row, col, peer), device_id_type=pl.DeviceIdType.MESH
        )
    pl.semaphore_wait(barrier, n - 1)
    copies = []
    for step in range(1, n):
        peer = lax.rem(me + step, n)
        copy = pltpu.make_async_remote_copy(
            src_ref=x_ref,
            dst_ref=held.at[step - 1],
            send_sem=send_sem.at[step - 1],
            recv_sem=recv_sem.at[step - 1],
            device_id=(row, col, peer),
            device_id_type=pl.DeviceIdType.MESH,
        )
        copy.start()
        copies.append(copy)
    for copy in copies:
        copy.wait()
    result = x_ref[...]
    for step in range(1, n):
        result = jnp.maximum(result, held[step - 1])
    out_ref[...] = result


def axis_sum_kernel(axis, gather, x_ref, out_ref, held, gathered, sems):
    n = lax.axis_size(axis)
    me = lax.axis_index(axis)
    chunk = held.shape[1]
    where = {name: lax.axis_index(name) for name in ("dp", "tx", "ty")}

    def device(peer):
        return tuple(peer if name == axis else where[name] for name in ("dp", "tx", "ty"))

    barrier = pltpu.get_barrier_semaphore()
    for step in range(1, n):
        pl.semaphore_signal(
            barrier, inc=1, device_id=device(lax.rem(me + step, n)), device_id_type=pl.DeviceIdType.MESH
        )
    pl.semaphore_wait(barrier, n - 1)
    copies = []
    for step in range(1, n):
        peer = lax.rem(me + step, n)
        copy = pltpu.make_async_remote_copy(
            src_ref=x_ref.at[pl.ds(pl.multiple_of(peer * chunk, 16), chunk)],
            dst_ref=held.at[step - 1],
            send_sem=sems.at[0, step - 1],
            recv_sem=sems.at[1, step - 1],
            device_id=device(peer),
            device_id_type=pl.DeviceIdType.MESH,
        )
        copy.start()
        copies.append(copy)
    for copy in copies:
        copy.wait()
    own = pl.ds(pl.multiple_of(me * chunk, 16), chunk)
    total = x_ref[own].astype(jnp.float32)
    for step in range(1, n):
        total = total + held[step - 1].astype(jnp.float32)
    if not gather:
        out_ref[...] = total.astype(out_ref.dtype)
        return
    out_ref[own] = total.astype(out_ref.dtype)
    copies = []
    for step in range(1, n):
        peer = lax.rem(me + step, n)
        copy = pltpu.make_async_remote_copy(
            src_ref=out_ref.at[own],
            dst_ref=gathered.at[step - 1],
            send_sem=sems.at[2, step - 1],
            recv_sem=sems.at[3, step - 1],
            device_id=device(peer),
            device_id_type=pl.DeviceIdType.MESH,
        )
        copy.start()
        copies.append(copy)
    for copy in copies:
        copy.wait()
    for step in range(1, n):
        source = lax.rem(me - step + n, n)
        out_ref[pl.ds(pl.multiple_of(source * chunk, 16), chunk)] = gathered[step - 1]


def axis_sum(values, axis, gather, send_type, out_type, collective_id):
    n = lax.axis_size(axis)
    flat = values.reshape(-1, 128).astype(send_type)
    rows = flat.shape[0]
    padded = -(-rows // (16 * n)) * 16 * n
    flat = jnp.pad(flat, ((0, padded - rows), (0, 0)))
    chunk = padded // n
    out = pl.pallas_call(
        functools.partial(axis_sum_kernel, axis, gather),
        out_shape=jax.ShapeDtypeStruct((padded if gather else chunk, 128), out_type),
        in_specs=[pl.BlockSpec(memory_space=pltpu.VMEM)],
        out_specs=pl.BlockSpec(memory_space=pltpu.VMEM),
        scratch_shapes=[
            pltpu.VMEM((n - 1, chunk, 128), send_type),
            pltpu.VMEM((n - 1, chunk, 128), out_type),
            pltpu.SemaphoreType.DMA((4, n - 1)),
        ],
        compiler_params=pltpu.CompilerParams(collective_id=collective_id, has_side_effects=True),
    )(flat)
    return out


def dp_exchange_kernel(x_ref, out_ref, held, sems):
    n = lax.axis_size("dp")
    me = lax.axis_index("dp")
    col = lax.axis_index("tx")
    row = lax.axis_index("ty")
    barrier = pltpu.get_barrier_semaphore()
    for step in range(1, n):
        pl.semaphore_signal(
            barrier, inc=1, device_id=(lax.rem(me + step, n), col, row), device_id_type=pl.DeviceIdType.MESH
        )
    pl.semaphore_wait(barrier, n - 1)
    copies = []
    for step in range(1, n):
        peer = lax.rem(me + step, n)
        copy = pltpu.make_async_remote_copy(
            src_ref=x_ref.at[peer],
            dst_ref=held.at[step - 1],
            send_sem=sems.at[0, step - 1],
            recv_sem=sems.at[1, step - 1],
            device_id=(peer, col, row),
            device_id_type=pl.DeviceIdType.MESH,
        )
        copy.start()
        copies.append(copy)
    out_ref[me] = x_ref[me]
    for copy in copies:
        copy.wait()
    for step in range(1, n):
        out_ref[lax.rem(me - step + n, n)] = held[step - 1]


def dp_exchange(blocks, collective_id):
    n = lax.axis_size("dp")
    shape = blocks.shape
    tiles = blocks.reshape(n, -1, 128)
    out = pl.pallas_call(
        dp_exchange_kernel,
        out_shape=jax.ShapeDtypeStruct(tiles.shape, tiles.dtype),
        in_specs=[pl.BlockSpec(memory_space=pltpu.VMEM)],
        out_specs=pl.BlockSpec(memory_space=pltpu.VMEM),
        scratch_shapes=[
            pltpu.VMEM((n - 1,) + tiles.shape[1:], tiles.dtype),
            pltpu.SemaphoreType.DMA((2, n - 1)),
        ],
        compiler_params=pltpu.CompilerParams(collective_id=collective_id, has_side_effects=True),
    )(tiles)
    return out.reshape(shape)


def ty_max(values):
    n = lax.axis_size("ty")
    flat = values.reshape(-1, 128)
    out = pl.pallas_call(
        ty_max_kernel,
        out_shape=jax.ShapeDtypeStruct(flat.shape, flat.dtype),
        in_specs=[pl.BlockSpec(memory_space=pltpu.VMEM)],
        out_specs=pl.BlockSpec(memory_space=pltpu.VMEM),
        scratch_shapes=[
            pltpu.VMEM((n - 1,) + flat.shape, flat.dtype),
            pltpu.SemaphoreType.DMA((n - 1,)),
            pltpu.SemaphoreType.DMA((n - 1,)),
        ],
        compiler_params=pltpu.CompilerParams(collective_id=0, has_side_effects=True),
    )(flat)
    return out.reshape(values.shape)


def shards(
    hidden_in,
    norm_gain,
    w_qkv,
    w_out,
    k_cache,
    v_cache,
    cache_lens,
    home_slot,
    parents,
    tree_sizes,
    leaf_node,
):
    group_count = lax.axis_size("dp")
    group_index = lax.axis_index("dp")
    local_reqs = k_cache.shape[0]
    tree_slots = parents.shape[1]
    capacity = (local_reqs + group_count - 1) // group_count
    head_local = k_cache.shape[2] // HD
    row_count = hidden_in.shape[0]
    float_in = hidden_in.astype(jnp.float32)
    feature_local = hidden_in.shape[1]
    gain_part = lax.dynamic_slice_in_dim(
        norm_gain, lax.axis_index("ty") * feature_local, feature_local
    )
    scaled = (float_in * gain_part.astype(jnp.float32)).astype(jnp.bfloat16)
    partial_proj = jnp.dot(scaled, w_qkv, preferred_element_type=jnp.float32)
    partial_square = jnp.sum(float_in * float_in, axis=1)
    proj_cols = partial_proj.shape[1]
    square_rows = jnp.pad(
        partial_square.reshape(-1, 128), ((0, 0), (0, proj_cols - 128))
    )
    joint = jnp.concatenate([partial_proj, square_rows], axis=0)
    joint = axis_sum(joint, "ty", True, jnp.float32, jnp.float32, 1)[: joint.size // 128]
    joint = joint.reshape(-1, proj_cols)
    projected = joint[:row_count]
    square_sum = joint[row_count:, :128].reshape(row_count)
    rms_inverse = lax.rsqrt(square_sum / D + norm_eps)
    projected = (projected * rms_inverse[:, None]).reshape(
        local_reqs, tree_slots, head_local, GROUP + 2, HD
    )
    first_request = group_index * local_reqs
    local_ids = jnp.arange(local_reqs, dtype=jnp.int32)
    request_ids = jnp.arange(home_slot.shape[0], dtype=jnp.int32)
    my_parents = lax.dynamic_slice_in_dim(parents, first_request, local_reqs, 0)
    my_slots = lax.dynamic_slice_in_dim(home_slot, first_request, local_reqs, 0)
    ancestors = jax.vmap(ancestry)(my_parents)
    node_depth = jnp.sum(ancestors > 0.5, axis=2) - 1
    slot_match = my_slots[:, None] == request_ids[None, :]
    my_lens = jnp.sum(jnp.where(slot_match, cache_lens[None, :], 0), axis=1)
    positions = my_lens[:, None] + node_depth
    queries = rotated(projected[:, :, :, :GROUP, :], positions[:, :, None, None]).astype(
        jnp.bfloat16
    )
    keys_new = rotated(projected[:, :, :, GROUP, :], positions[:, :, None]).astype(jnp.bfloat16)
    values_new = projected[:, :, :, GROUP + 1, :].astype(jnp.bfloat16)
    dest_group, dest_rank = routing(home_slot, group_count, local_reqs)
    send_pos = lax.dynamic_index_in_dim(
        dest_group, group_index, 0, keepdims=False
    ) * capacity + lax.dynamic_index_in_dim(dest_rank, group_index, 0, keepdims=False)
    buffer_ids = jnp.arange(group_count * capacity, dtype=jnp.int32)
    send_hit = send_pos[None, :] == buffer_ids[:, None]
    send_index = jnp.where(
        jnp.any(send_hit, axis=1),
        jnp.sum(jnp.where(send_hit, local_ids[None, :], 0), axis=1),
        local_reqs,
    )
    target_slots = first_request + local_ids
    owner_match = home_slot[None, :] == target_slots[:, None]
    owner_request = jnp.sum(jnp.where(owner_match, request_ids[None, :], 0), axis=1)
    owner_rank = jnp.sum(jnp.where(owner_match, dest_rank.reshape(-1)[None, :], 0), axis=1)
    recv_index = owner_request // local_reqs * capacity + owner_rank
    back_hit = recv_index[None, :] == buffer_ids[:, None]
    back_index = jnp.where(
        jnp.any(back_hit, axis=1),
        jnp.sum(jnp.where(back_hit, local_ids[None, :], 0), axis=1),
        local_reqs,
    )
    home_lens = lax.dynamic_slice_in_dim(cache_lens, first_request, local_reqs, 0)
    arrived = dp_exchange(packed(queries.reshape(local_reqs, -1), send_index), 4)
    slot_queries = packed(arrived, recv_index).reshape(queries.shape)
    top_score, weight_sum, summed = cache_merged(slot_queries, k_cache, v_cache, home_lens)
    normalized = summed / weight_sum[..., None]
    log_total = top_score + jnp.log(weight_sum)
    value_width = normalized.size // local_reqs
    log_flat = log_total.reshape(local_reqs, -1)
    log_high = lax.reduce_precision(log_flat, exponent_bits=8, mantissa_bits=7)
    log_rest = log_flat - log_high
    log_mid = lax.reduce_precision(log_rest, exponent_bits=8, mantissa_bits=7)
    log_low = log_rest - log_mid
    payload = jnp.concatenate(
        [normalized.reshape(local_reqs, -1), log_high, log_mid, log_low], axis=1
    ).astype(jnp.bfloat16)
    back = dp_exchange(packed(payload, back_index), 5)
    back = packed(back, send_pos).astype(jnp.float32)
    log_width = log_flat.shape[1]
    cache_values = back[:, :value_width].reshape(local_reqs, tree_slots, head_local, GROUP, HD)
    cache_top = (
        back[:, value_width : value_width + log_width]
        + back[:, value_width + log_width : value_width + 2 * log_width]
        + back[:, value_width + 2 * log_width :]
    ).reshape(local_reqs, tree_slots, head_local, GROUP)
    tree_stats = tree_part(queries, keys_new, values_new, ancestors)
    top_all, sum_all, summed_all = combine_stats(
        (cache_top, jnp.ones_like(cache_top), cache_values), tree_stats
    )
    attention = (summed_all / sum_all[..., None]).astype(jnp.bfloat16)
    attention_rows = attention.reshape(row_count, -1)
    rows_mine = row_count // lax.axis_size("tx")
    mixed_sum = axis_sum(
        jnp.dot(attention_rows, w_out, preferred_element_type=jnp.float32),
        "tx",
        False,
        jnp.bfloat16,
        jnp.float32,
        3,
    ).reshape(row_count // lax.axis_size("tx"), -1)
    row_start = lax.axis_index("tx") * rows_mine
    residual = lax.dynamic_slice_in_dim(float_in, row_start, rows_mine, 0)
    row_ids = row_start + jnp.arange(rows_mine, dtype=jnp.int32)
    request_of = row_ids // tree_slots
    slot_of = row_ids % tree_slots
    size_of = jnp.sum(
        jnp.where(request_of[:, None] == local_ids[None, :], tree_sizes[None, :], 0), axis=1
    )
    layer_out = jnp.where((slot_of < size_of)[:, None], residual + mixed_sum, 0.0).astype(
        jnp.bfloat16
    )
    node_ids = jnp.arange(tree_slots, dtype=jnp.int32)
    leaf_hit = (leaf_node[:, None] == node_ids[None, :]).astype(jnp.float32)
    path_nodes = jnp.einsum("rt,rtu->ru", leaf_hit, ancestors)
    depth_hit = node_depth[:, None, :] == jnp.arange(ACC, dtype=jnp.int32)[None, :, None]
    chooser = jnp.where(depth_hit, path_nodes[:, None, :], 0.0).astype(jnp.bfloat16)
    stacked = jnp.stack(
        [
            keys_new.reshape(local_reqs, tree_slots, -1),
            values_new.reshape(local_reqs, tree_slots, -1),
        ],
        axis=2,
    )
    accepted_kv = jnp.einsum(
        "rsu,ruwc->rswc", chooser, stacked, preferred_element_type=jnp.float32
    ).astype(jnp.bfloat16)
    return (layer_out, accepted_kv)


def solution(mesh):
    return jax.shard_map(
        shards,
        mesh=mesh,
        in_specs=(
            P("dp", "ty"),
            P(),
            P("ty", "tx"),
            P("tx", "ty"),
            P("dp", "ty", "tx"),
            P("dp", "ty", "tx"),
            P(),
            P(),
            P(),
            P("dp"),
            P("dp"),
        ),
        out_specs=(P(("dp", "tx"), "ty"), P("dp", None, None, "tx")),
        check_vma=False,
    )
```

```python
import functools

import jax
import jax.numpy as jnp
from jax import lax
from jax.experimental import pallas as pl
from jax.experimental.pallas import tpu as pltpu
from jax.sharding import PartitionSpec as P

D = 2048
HD = 64
GROUP = 4
ACC = 8


rope_base = 10000000.0
attn_mult = 0.015625
norm_eps = 1e-05
neg_fill = -1e30


def joined(value, axis, join):
    pieces = jax.tree.map(lambda part: lax.all_gather(part, axis), value)
    head = jax.tree.map(lambda part: part[0], pieces)
    tail = jax.tree.map(lambda part: part[1:], pieces)
    so_far, _ = lax.scan(lambda so_far, slab: (join(so_far, slab), None), head, tail)
    return so_far


def ancestry(parent_rows):
    node_count = parent_rows.shape[-1]
    node_ids = jnp.arange(node_count, dtype=jnp.int32)
    linked = (node_ids[None, :] == parent_rows[:, None]) | (node_ids[None, :] == node_ids[:, None])
    reachable = linked.astype(jnp.float32)
    for repeat in range(max(1, (node_count - 1).bit_length())):
        reachable = jnp.minimum(jnp.dot(reachable, reachable, precision=lax.Precision.HIGHEST), 1.0)
    return reachable


def rotated(values, positions):
    half_size = values.shape[-1] // 2
    frequency = rope_base ** (-2.0 * jnp.arange(half_size, dtype=jnp.float32) / values.shape[-1])
    angles = positions.astype(jnp.float32)[..., None] * frequency
    cosine = jnp.cos(angles)
    sine_part = jnp.sin(angles)
    front_half = values[..., :half_size]
    back_half = values[..., half_size:]
    return jnp.concatenate(
        [front_half * cosine - back_half * sine_part, back_half * cosine + front_half * sine_part],
        axis=-1,
    )


def combine_stats(first_stats, second_stats):
    top_first, sum_first, summed_first = first_stats
    top_second, sum_second, summed_second = second_stats
    top_both = jnp.maximum(top_first, top_second)
    scale_first = jnp.exp(top_first - top_both)
    scale_second = jnp.exp(top_second - top_both)
    return (
        top_both,
        sum_first * scale_first + sum_second * scale_second,
        summed_first * scale_first[..., None] + summed_second * scale_second[..., None],
    )


def packed(values, index):
    return jnp.take(values, index, axis=0, mode="fill", fill_value=0)


def routing(home_slot, group_count, local_reqs):
    dest_group = (home_slot // local_reqs).reshape(group_count, local_reqs)
    local_ids = jnp.arange(local_reqs, dtype=jnp.int32)
    earlier = local_ids[None, :] < local_ids[:, None]
    same_dest = dest_group[:, :, None] == dest_group[:, None, :]
    dest_rank = jnp.sum(same_dest & earlier[None], axis=2)
    return (dest_group, dest_rank)


def tree_part(queries, keys_new, values_new, ancestors):
    scores = attn_mult * jnp.einsum(
        "rtkgd,rukd->rtkgu", queries, keys_new, preferred_element_type=jnp.float32
    )
    valid_keys = (ancestors > 0.5)[:, :, None, None, :]
    masked = jnp.where(valid_keys, scores, neg_fill)
    top_score = jnp.max(masked, axis=-1)
    weights = jnp.where(valid_keys, jnp.exp(masked - top_score[..., None]), 0.0)
    summed = jnp.einsum(
        "rtkgu,rukd->rtkgd",
        weights.astype(jnp.bfloat16),
        values_new,
        preferred_element_type=jnp.float32,
    )
    return (top_score, jnp.sum(weights, axis=-1), summed)


def cache_kernel(lens_ref, start_ref, q_ref, k_ref, v_ref, top_ref, sum_ref, acc_ref):
    slot = pl.program_id(0)
    head_local = top_ref.shape[1]
    cache_local = k_ref.shape[1]
    limit = lens_ref[slot] - start_ref[0]
    valid = lax.broadcasted_iota(jnp.int32, (1, cache_local), 1) < limit
    keys = k_ref[0]
    values = v_ref[0]
    lane = lax.broadcasted_iota(jnp.int32, (1, head_local * HD), 1)
    queries = q_ref[0] * jnp.asarray(attn_mult, q_ref.dtype)
    any_valid = limit > 0
    result = None
    for head in range(head_local):
        mine = (lane >= head * HD) & (lane < (head + 1) * HD)
        own = jnp.where(mine, queries, jnp.zeros((), queries.dtype))
        scores = lax.dot_general(
            own, keys, (((1,), (1,)), ((), ())), preferred_element_type=jnp.float32
        )
        masked = jnp.where(valid, scores, neg_fill)
        top = jnp.max(masked, axis=1, keepdims=True)
        weights = jnp.exp(masked - top)
        summed = jnp.dot(weights.astype(jnp.bfloat16), values, preferred_element_type=jnp.float32)
        top_ref[0, head] = top
        sum_ref[0, head] = jnp.where(any_valid, jnp.sum(weights, axis=1, keepdims=True), 0.0)
        result = summed if result is None else jnp.where(mine, summed, result)
    acc_ref[0] = jnp.where(any_valid, result, 0.0)


def cache_merged(slot_queries, k_cache, v_cache, home_lens):
    local_reqs, tree_slots, head_local = slot_queries.shape[:3]
    cache_local = k_cache.shape[1]
    width = head_local * HD
    rows = tree_slots * GROUP
    key_start = (lax.axis_index("ty") * cache_local).astype(jnp.int32).reshape(1)
    spread = slot_queries.transpose(0, 1, 3, 2, 4).reshape(local_reqs, rows, width)
    top, total, summed = pl.pallas_call(
        cache_kernel,
        grid_spec=pltpu.PrefetchScalarGridSpec(
            num_scalar_prefetch=2,
            grid=(local_reqs,),
            in_specs=[
                pl.BlockSpec((1, rows, width), lambda s, lens, start: (s, 0, 0)),
                pl.BlockSpec((1, cache_local, width), lambda s, lens, start: (s, 0, 0)),
                pl.BlockSpec((1, cache_local, width), lambda s, lens, start: (s, 0, 0)),
            ],
            out_specs=[
                pl.BlockSpec((1, head_local, rows, 1), lambda s, lens, start: (s, 0, 0, 0)),
                pl.BlockSpec((1, head_local, rows, 1), lambda s, lens, start: (s, 0, 0, 0)),
                pl.BlockSpec((1, rows, width), lambda s, lens, start: (s, 0, 0)),
            ],
        ),
        out_shape=[
            jax.ShapeDtypeStruct((local_reqs, head_local, rows, 1), jnp.float32),
            jax.ShapeDtypeStruct((local_reqs, head_local, rows, 1), jnp.float32),
            jax.ShapeDtypeStruct((local_reqs, rows, width), jnp.float32),
        ],
        cost_estimate=pl.CostEstimate(
            flops=4 * local_reqs * head_local * rows * cache_local * width,
            transcendentals=local_reqs * head_local * rows * cache_local,
            bytes_accessed=2 * k_cache.size * 2 + spread.size * 2 + local_reqs * rows * width * 4,
        ),
    )(home_lens, key_start, spread, k_cache, v_cache)
    top = top.reshape(local_reqs, head_local, tree_slots, GROUP).transpose(0, 2, 1, 3)
    total = total.reshape(local_reqs, head_local, tree_slots, GROUP).transpose(0, 2, 1, 3)
    summed = summed.reshape(local_reqs, tree_slots, GROUP, head_local, HD).transpose(0, 1, 3, 2, 4)
    top_all = ty_max(top)
    scale = jnp.exp(top - top_all)
    count = total.size
    joint = jnp.concatenate(
        [(summed * scale[..., None]).reshape(-1, 128), (total * scale).reshape(count // 128, 128)],
        axis=0,
    )
    joint = axis_sum(joint, "ty", True, jnp.bfloat16, jnp.bfloat16, 2)[: joint.shape[0]]
    joint = joint.astype(jnp.float32)
    summed = joint[: summed.size // 128].reshape(summed.shape)
    total = joint[summed.size // 128 :].reshape(total.shape)
    return (top_all, total, summed)


def ty_max_kernel(x_ref, out_ref, held, send_sem, recv_sem):
    n = lax.axis_size("ty")
    me = lax.axis_index("ty")
    row = lax.axis_index("dp")
    col = lax.axis_index("tx")
    barrier = pltpu.get_barrier_semaphore()
    for step in range(1, n):
        peer = lax.rem(me + step, n)
        pl.semaphore_signal(
            barrier, inc=1, device_id=(row, col, peer), device_id_type=pl.DeviceIdType.MESH
        )
    pl.semaphore_wait(barrier, n - 1)
    copies = []
    for step in range(1, n):
        peer = lax.rem(me + step, n)
        copy = pltpu.make_async_remote_copy(
            src_ref=x_ref,
            dst_ref=held.at[step - 1],
            send_sem=send_sem.at[step - 1],
            recv_sem=recv_sem.at[step - 1],
            device_id=(row, col, peer),
            device_id_type=pl.DeviceIdType.MESH,
        )
        copy.start()
        copies.append(copy)
    for copy in copies:
        copy.wait()
    result = x_ref[...]
    for step in range(1, n):
        result = jnp.maximum(result, held[step - 1])
    out_ref[...] = result


def axis_sum_kernel(axis, gather, x_ref, out_ref, held, gathered, sems):
    n = lax.axis_size(axis)
    me = lax.axis_index(axis)
    chunk = held.shape[1]
    where = {name: lax.axis_index(name) for name in ("dp", "tx", "ty")}

    def device(peer):
        return tuple(peer if name == axis else where[name] for name in ("dp", "tx", "ty"))

    barrier = pltpu.get_barrier_semaphore()
    for step in range(1, n):
        pl.semaphore_signal(
            barrier, inc=1, device_id=device(lax.rem(me + step, n)), device_id_type=pl.DeviceIdType.MESH
        )
    pl.semaphore_wait(barrier, n - 1)
    copies = []
    for step in range(1, n):
        peer = lax.rem(me + step, n)
        copy = pltpu.make_async_remote_copy(
            src_ref=x_ref.at[pl.ds(pl.multiple_of(peer * chunk, 16), chunk)],
            dst_ref=held.at[step - 1],
            send_sem=sems.at[0, step - 1],
            recv_sem=sems.at[1, step - 1],
            device_id=device(peer),
            device_id_type=pl.DeviceIdType.MESH,
        )
        copy.start()
        copies.append(copy)
    for copy in copies:
        copy.wait()
    own = pl.ds(pl.multiple_of(me * chunk, 16), chunk)
    total = x_ref[own].astype(jnp.float32)
    for step in range(1, n):
        total = total + held[step - 1].astype(jnp.float32)
    if not gather:
        out_ref[...] = total.astype(out_ref.dtype)
        return
    out_ref[own] = total.astype(out_ref.dtype)
    copies = []
    for step in range(1, n):
        peer = lax.rem(me + step, n)
        copy = pltpu.make_async_remote_copy(
            src_ref=out_ref.at[own],
            dst_ref=gathered.at[step - 1],
            send_sem=sems.at[2, step - 1],
            recv_sem=sems.at[3, step - 1],
            device_id=device(peer),
            device_id_type=pl.DeviceIdType.MESH,
        )
        copy.start()
        copies.append(copy)
    for copy in copies:
        copy.wait()
    for step in range(1, n):
        source = lax.rem(me - step + n, n)
        out_ref[pl.ds(pl.multiple_of(source * chunk, 16), chunk)] = gathered[step - 1]


def axis_sum(values, axis, gather, send_type, out_type, collective_id):
    n = lax.axis_size(axis)
    flat = values.reshape(-1, 128).astype(send_type)
    rows = flat.shape[0]
    padded = -(-rows // (16 * n)) * 16 * n
    flat = jnp.pad(flat, ((0, padded - rows), (0, 0)))
    chunk = padded // n
    out = pl.pallas_call(
        functools.partial(axis_sum_kernel, axis, gather),
        out_shape=jax.ShapeDtypeStruct((padded if gather else chunk, 128), out_type),
        in_specs=[pl.BlockSpec(memory_space=pltpu.VMEM)],
        out_specs=pl.BlockSpec(memory_space=pltpu.VMEM),
        scratch_shapes=[
            pltpu.VMEM((n - 1, chunk, 128), send_type),
            pltpu.VMEM((n - 1, chunk, 128), out_type),
            pltpu.SemaphoreType.DMA((4, n - 1)),
        ],
        compiler_params=pltpu.CompilerParams(collective_id=collective_id, has_side_effects=True),
    )(flat)
    return out


def dp_exchange_kernel(x_ref, out_ref, held, sems):
    n = lax.axis_size("dp")
    me = lax.axis_index("dp")
    col = lax.axis_index("tx")
    row = lax.axis_index("ty")
    barrier = pltpu.get_barrier_semaphore()
    for step in range(1, n):
        pl.semaphore_signal(
            barrier, inc=1, device_id=(lax.rem(me + step, n), col, row), device_id_type=pl.DeviceIdType.MESH
        )
    pl.semaphore_wait(barrier, n - 1)
    copies = []
    for step in range(1, n):
        peer = lax.rem(me + step, n)
        copy = pltpu.make_async_remote_copy(
            src_ref=x_ref.at[peer],
            dst_ref=held.at[step - 1],
            send_sem=sems.at[0, step - 1],
            recv_sem=sems.at[1, step - 1],
            device_id=(peer, col, row),
            device_id_type=pl.DeviceIdType.MESH,
        )
        copy.start()
        copies.append(copy)
    out_ref[me] = x_ref[me]
    for copy in copies:
        copy.wait()
    for step in range(1, n):
        out_ref[lax.rem(me - step + n, n)] = held[step - 1]


def dp_exchange(blocks, collective_id):
    n = lax.axis_size("dp")
    shape = blocks.shape
    tiles = blocks.reshape(n, -1, 128)
    out = pl.pallas_call(
        dp_exchange_kernel,
        out_shape=jax.ShapeDtypeStruct(tiles.shape, tiles.dtype),
        in_specs=[pl.BlockSpec(memory_space=pltpu.VMEM)],
        out_specs=pl.BlockSpec(memory_space=pltpu.VMEM),
        scratch_shapes=[
            pltpu.VMEM((n - 1,) + tiles.shape[1:], tiles.dtype),
            pltpu.SemaphoreType.DMA((2, n - 1)),
        ],
        compiler_params=pltpu.CompilerParams(collective_id=collective_id, has_side_effects=True),
    )(tiles)
    return out.reshape(shape)


def axis_gather_kernel(axis, x_ref, out_ref, gathered, sems):
    n = lax.axis_size(axis)
    me = lax.axis_index(axis)
    chunk = x_ref.shape[0]
    where = {name: lax.axis_index(name) for name in ("dp", "tx", "ty")}

    def device(peer):
        return tuple(peer if name == axis else where[name] for name in ("dp", "tx", "ty"))

    barrier = pltpu.get_barrier_semaphore()
    for step in range(1, n):
        pl.semaphore_signal(
            barrier, inc=1, device_id=device(lax.rem(me + step, n)), device_id_type=pl.DeviceIdType.MESH
        )
    pl.semaphore_wait(barrier, n - 1)
    copies = []
    for step in range(1, n):
        peer = lax.rem(me + step, n)
        copy = pltpu.make_async_remote_copy(
            src_ref=x_ref,
            dst_ref=gathered.at[step - 1],
            send_sem=sems.at[0, step - 1],
            recv_sem=sems.at[1, step - 1],
            device_id=device(peer),
            device_id_type=pl.DeviceIdType.MESH,
        )
        copy.start()
        copies.append(copy)
    out_ref[pl.ds(pl.multiple_of(me * chunk, 16), chunk)] = x_ref[...]
    for copy in copies:
        copy.wait()
    for step in range(1, n):
        source = lax.rem(me - step + n, n)
        out_ref[pl.ds(pl.multiple_of(source * chunk, 16), chunk)] = gathered[step - 1]


def axis_gather(values, axis, collective_id):
    n = lax.axis_size(axis)
    flat = values.reshape(-1, 128)
    chunk = flat.shape[0]
    out = pl.pallas_call(
        functools.partial(axis_gather_kernel, axis),
        out_shape=jax.ShapeDtypeStruct((n * chunk, 128), flat.dtype),
        in_specs=[pl.BlockSpec(memory_space=pltpu.VMEM)],
        out_specs=pl.BlockSpec(memory_space=pltpu.VMEM),
        scratch_shapes=[
            pltpu.VMEM((n - 1, chunk, 128), flat.dtype),
            pltpu.SemaphoreType.DMA((2, n - 1)),
        ],
        compiler_params=pltpu.CompilerParams(collective_id=collective_id, has_side_effects=True),
    )(flat)
    return out.reshape((n * values.shape[0],) + values.shape[1:])


def ty_max(values):
    n = lax.axis_size("ty")
    flat = values.reshape(-1, 128)
    out = pl.pallas_call(
        ty_max_kernel,
        out_shape=jax.ShapeDtypeStruct(flat.shape, flat.dtype),
        in_specs=[pl.BlockSpec(memory_space=pltpu.VMEM)],
        out_specs=pl.BlockSpec(memory_space=pltpu.VMEM),
        scratch_shapes=[
            pltpu.VMEM((n - 1,) + flat.shape, flat.dtype),
            pltpu.SemaphoreType.DMA((n - 1,)),
            pltpu.SemaphoreType.DMA((n - 1,)),
        ],
        compiler_params=pltpu.CompilerParams(collective_id=0, has_side_effects=True),
    )(flat)
    return out.reshape(values.shape)


def shards(
    hidden_in,
    norm_gain,
    w_qkv,
    w_out,
    k_cache,
    v_cache,
    cache_lens,
    home_slot,
    parents,
    tree_sizes,
    leaf_node,
):
    group_count = lax.axis_size("dp")
    group_index = lax.axis_index("dp")
    local_reqs = k_cache.shape[0]
    tree_slots = parents.shape[1]
    capacity = (local_reqs + group_count - 1) // group_count
    head_local = k_cache.shape[2] // HD
    row_count = hidden_in.shape[0]
    float_in = hidden_in.astype(jnp.float32)
    feature_local = hidden_in.shape[1]
    gain_part = lax.dynamic_slice_in_dim(
        norm_gain, lax.axis_index("ty") * feature_local, feature_local
    )
    scaled = (float_in * gain_part.astype(jnp.float32)).astype(jnp.bfloat16)
    partial_proj = jnp.dot(scaled, w_qkv, preferred_element_type=jnp.float32)
    partial_square = jnp.sum(float_in * float_in, axis=1)
    proj_cols = partial_proj.shape[1]
    n_ty = lax.axis_size("ty")
    chunk_rows = row_count // n_ty
    reqs_mine = local_reqs // n_ty
    square_block = jnp.pad(
        partial_square.reshape(n_ty, 1, chunk_rows),
        ((0, 0), (0, 7), (0, proj_cols - chunk_rows)),
    )
    joint = jnp.concatenate(
        [partial_proj.reshape(n_ty, chunk_rows, proj_cols), square_block], axis=1
    )
    mine = axis_sum(joint, "ty", False, jnp.float32, jnp.float32, 1).reshape(-1, proj_cols)
    square_sum = mine[chunk_rows, :chunk_rows]
    rms_inverse = lax.rsqrt(square_sum / D + norm_eps)
    projected = (mine[:chunk_rows] * rms_inverse[:, None]).reshape(
        reqs_mine, tree_slots, head_local, GROUP + 2, HD
    )
    first_request = group_index * local_reqs
    local_ids = jnp.arange(local_reqs, dtype=jnp.int32)
    request_ids = jnp.arange(home_slot.shape[0], dtype=jnp.int32)
    my_parents = lax.dynamic_slice_in_dim(parents, first_request, local_reqs, 0)
    my_slots = lax.dynamic_slice_in_dim(home_slot, first_request, local_reqs, 0)
    ancestors = jax.vmap(ancestry)(my_parents)
    node_depth = jnp.sum(ancestors > 0.5, axis=2) - 1
    slot_match = my_slots[:, None] == request_ids[None, :]
    my_lens = jnp.sum(jnp.where(slot_match, cache_lens[None, :], 0), axis=1)
    positions = my_lens[:, None] + node_depth
    positions_mine = lax.dynamic_slice_in_dim(
        positions, lax.axis_index("ty") * reqs_mine, reqs_mine, 0
    )
    queries_mine = rotated(
        projected[:, :, :, :GROUP, :], positions_mine[:, :, None, None]
    ).astype(jnp.bfloat16)
    keys_mine = rotated(projected[:, :, :, GROUP, :], positions_mine[:, :, None]).astype(
        jnp.bfloat16
    )
    values_mine = projected[:, :, :, GROUP + 1, :].astype(jnp.bfloat16)
    piece = jnp.concatenate(
        [
            queries_mine.reshape(chunk_rows, -1),
            keys_mine.reshape(chunk_rows, -1),
            values_mine.reshape(chunk_rows, -1),
        ],
        axis=1,
    )
    everything = axis_gather(piece, "ty", 6)
    query_cols = head_local * GROUP * HD
    queries = everything[:, :query_cols].reshape(local_reqs, tree_slots, head_local, GROUP, HD)
    keys_new = everything[:, query_cols : query_cols + head_local * HD].reshape(
        local_reqs, tree_slots, head_local, HD
    )
    values_new = everything[:, query_cols + head_local * HD :].reshape(
        local_reqs, tree_slots, head_local, HD
    )
    dest_group, dest_rank = routing(home_slot, group_count, local_reqs)
    send_pos = lax.dynamic_index_in_dim(
        dest_group, group_index, 0, keepdims=False
    ) * capacity + lax.dynamic_index_in_dim(dest_rank, group_index, 0, keepdims=False)
    buffer_ids = jnp.arange(group_count * capacity, dtype=jnp.int32)
    send_hit = send_pos[None, :] == buffer_ids[:, None]
    send_index = jnp.where(
        jnp.any(send_hit, axis=1),
        jnp.sum(jnp.where(send_hit, local_ids[None, :], 0), axis=1),
        local_reqs,
    )
    target_slots = first_request + local_ids
    owner_match = home_slot[None, :] == target_slots[:, None]
    owner_request = jnp.sum(jnp.where(owner_match, request_ids[None, :], 0), axis=1)
    owner_rank = jnp.sum(jnp.where(owner_match, dest_rank.reshape(-1)[None, :], 0), axis=1)
    recv_index = owner_request // local_reqs * capacity + owner_rank
    back_hit = recv_index[None, :] == buffer_ids[:, None]
    back_index = jnp.where(
        jnp.any(back_hit, axis=1),
        jnp.sum(jnp.where(back_hit, local_ids[None, :], 0), axis=1),
        local_reqs,
    )
    home_lens = lax.dynamic_slice_in_dim(cache_lens, first_request, local_reqs, 0)
    arrived = dp_exchange(packed(queries.reshape(local_reqs, -1), send_index), 4)
    slot_queries = packed(arrived, recv_index).reshape(queries.shape)
    top_score, weight_sum, summed = cache_merged(slot_queries, k_cache, v_cache, home_lens)
    normalized = summed / weight_sum[..., None]
    log_total = top_score + jnp.log(weight_sum)
    value_width = normalized.size // local_reqs
    log_flat = log_total.reshape(local_reqs, -1)
    log_high = lax.reduce_precision(log_flat, exponent_bits=8, mantissa_bits=7)
    log_rest = log_flat - log_high
    log_mid = lax.reduce_precision(log_rest, exponent_bits=8, mantissa_bits=7)
    log_low = log_rest - log_mid
    payload = jnp.concatenate(
        [normalized.reshape(local_reqs, -1), log_high, log_mid, log_low], axis=1
    ).astype(jnp.bfloat16)
    back = lax.all_to_all(
        packed(payload, back_index), "dp", split_axis=0, concat_axis=0, tiled=True
    )
    back = packed(back, send_pos).astype(jnp.float32)
    log_width = log_flat.shape[1]
    cache_values = back[:, :value_width].reshape(local_reqs, tree_slots, head_local, GROUP, HD)
    cache_top = (
        back[:, value_width : value_width + log_width]
        + back[:, value_width + log_width : value_width + 2 * log_width]
        + back[:, value_width + 2 * log_width :]
    ).reshape(local_reqs, tree_slots, head_local, GROUP)
    tree_stats = tree_part(queries, keys_new, values_new, ancestors)
    top_all, sum_all, summed_all = combine_stats(
        (cache_top, jnp.ones_like(cache_top), cache_values), tree_stats
    )
    attention = (summed_all / sum_all[..., None]).astype(jnp.bfloat16)
    attention_rows = attention.reshape(row_count, -1)
    rows_mine = row_count // lax.axis_size("tx")
    mixed_sum = axis_sum(
        jnp.dot(attention_rows, w_out, preferred_element_type=jnp.float32),
        "tx",
        False,
        jnp.bfloat16,
        jnp.float32,
        3,
    ).reshape(row_count // lax.axis_size("tx"), -1)
    row_start = lax.axis_index("tx") * rows_mine
    residual = lax.dynamic_slice_in_dim(float_in, row_start, rows_mine, 0)
    row_ids = row_start + jnp.arange(rows_mine, dtype=jnp.int32)
    request_of = row_ids // tree_slots
    slot_of = row_ids % tree_slots
    size_of = jnp.sum(
        jnp.where(request_of[:, None] == local_ids[None, :], tree_sizes[None, :], 0), axis=1
    )
    layer_out = jnp.where((slot_of < size_of)[:, None], residual + mixed_sum, 0.0).astype(
        jnp.bfloat16
    )
    node_ids = jnp.arange(tree_slots, dtype=jnp.int32)
    leaf_hit = (leaf_node[:, None] == node_ids[None, :]).astype(jnp.float32)
    path_nodes = jnp.einsum("rt,rtu->ru", leaf_hit, ancestors)
    depth_hit = node_depth[:, None, :] == jnp.arange(ACC, dtype=jnp.int32)[None, :, None]
    chooser = jnp.where(depth_hit, path_nodes[:, None, :], 0.0).astype(jnp.bfloat16)
    stacked = jnp.stack(
        [
            keys_new.reshape(local_reqs, tree_slots, -1),
            values_new.reshape(local_reqs, tree_slots, -1),
        ],
        axis=2,
    )
    accepted_kv = jnp.einsum(
        "rsu,ruwc->rswc", chooser, stacked, preferred_element_type=jnp.float32
    ).astype(jnp.bfloat16)
    return (layer_out, accepted_kv)


def solution(mesh):
    return jax.shard_map(
        shards,
        mesh=mesh,
        in_specs=(
            P("dp", "ty"),
            P(),
            P("ty", "tx"),
            P("tx", "ty"),
            P("dp", "ty", "tx"),
            P("dp", "ty", "tx"),
            P(),
            P(),
            P(),
            P("dp"),
            P("dp"),
        ),
        out_specs=(P(("dp", "tx"), "ty"), P("dp", None, None, "tx")),
        check_vma=False,
    )
```

```python
import functools

import jax
import jax.numpy as jnp
from jax import lax
from jax.experimental import pallas as pl
from jax.experimental.pallas import tpu as pltpu
from jax.sharding import PartitionSpec as P

D = 2048
HD = 64
GROUP = 4
ACC = 8


rope_base = 10000000.0
attn_mult = 0.015625
norm_eps = 1e-05
neg_fill = -1e30


def joined(value, axis, join):
    pieces = jax.tree.map(lambda part: lax.all_gather(part, axis), value)
    head = jax.tree.map(lambda part: part[0], pieces)
    tail = jax.tree.map(lambda part: part[1:], pieces)
    so_far, _ = lax.scan(lambda so_far, slab: (join(so_far, slab), None), head, tail)
    return so_far


def ancestry(parent_rows):
    node_count = parent_rows.shape[-1]
    node_ids = jnp.arange(node_count, dtype=jnp.int32)
    linked = (node_ids[None, :] == parent_rows[:, None]) | (node_ids[None, :] == node_ids[:, None])
    reachable = linked.astype(jnp.float32)
    for repeat in range(max(1, (node_count - 1).bit_length())):
        reachable = jnp.minimum(jnp.dot(reachable, reachable, precision=lax.Precision.HIGHEST), 1.0)
    return reachable


def rotated(values, positions):
    half_size = values.shape[-1] // 2
    frequency = rope_base ** (-2.0 * jnp.arange(half_size, dtype=jnp.float32) / values.shape[-1])
    angles = positions.astype(jnp.float32)[..., None] * frequency
    cosine = jnp.cos(angles)
    sine_part = jnp.sin(angles)
    front_half = values[..., :half_size]
    back_half = values[..., half_size:]
    return jnp.concatenate(
        [front_half * cosine - back_half * sine_part, back_half * cosine + front_half * sine_part],
        axis=-1,
    )


def combine_stats(first_stats, second_stats):
    top_first, sum_first, summed_first = first_stats
    top_second, sum_second, summed_second = second_stats
    top_both = jnp.maximum(top_first, top_second)
    scale_first = jnp.exp(top_first - top_both)
    scale_second = jnp.exp(top_second - top_both)
    return (
        top_both,
        sum_first * scale_first + sum_second * scale_second,
        summed_first * scale_first[..., None] + summed_second * scale_second[..., None],
    )


def packed(values, index):
    return jnp.take(values, index, axis=0, mode="fill", fill_value=0)


def routing(home_slot, group_count, local_reqs):
    dest_group = (home_slot // local_reqs).reshape(group_count, local_reqs)
    local_ids = jnp.arange(local_reqs, dtype=jnp.int32)
    earlier = local_ids[None, :] < local_ids[:, None]
    same_dest = dest_group[:, :, None] == dest_group[:, None, :]
    dest_rank = jnp.sum(same_dest & earlier[None], axis=2)
    return (dest_group, dest_rank)


def tree_part(queries, keys_new, values_new, ancestors):
    scores = attn_mult * jnp.einsum(
        "rtkgd,rukd->rtkgu", queries, keys_new, preferred_element_type=jnp.float32
    )
    valid_keys = (ancestors > 0.5)[:, :, None, None, :]
    masked = jnp.where(valid_keys, scores, neg_fill)
    top_score = jnp.max(masked, axis=-1)
    weights = jnp.where(valid_keys, jnp.exp(masked - top_score[..., None]), 0.0)
    summed = jnp.einsum(
        "rtkgu,rukd->rtkgd",
        weights.astype(jnp.bfloat16),
        values_new,
        preferred_element_type=jnp.float32,
    )
    return (top_score, jnp.sum(weights, axis=-1), summed)


def cache_kernel(lens_ref, start_ref, q_ref, k_ref, v_ref, top_ref, sum_ref, acc_ref):
    slot = pl.program_id(0)
    head_local = top_ref.shape[1]
    cache_local = k_ref.shape[1]
    limit = lens_ref[slot] - start_ref[0]
    valid = lax.broadcasted_iota(jnp.int32, (1, cache_local), 1) < limit
    keys = k_ref[0]
    values = v_ref[0]
    lane = lax.broadcasted_iota(jnp.int32, (1, head_local * HD), 1)
    queries = q_ref[0] * jnp.asarray(attn_mult, q_ref.dtype)
    any_valid = limit > 0
    result = None
    for head in range(head_local):
        mine = (lane >= head * HD) & (lane < (head + 1) * HD)
        own = jnp.where(mine, queries, jnp.zeros((), queries.dtype))
        scores = lax.dot_general(
            own, keys, (((1,), (1,)), ((), ())), preferred_element_type=jnp.float32
        )
        masked = jnp.where(valid, scores, neg_fill)
        top = jnp.max(masked, axis=1, keepdims=True)
        weights = jnp.exp(masked - top)
        summed = jnp.dot(weights.astype(jnp.bfloat16), values, preferred_element_type=jnp.float32)
        total = jnp.where(any_valid, jnp.sum(weights, axis=1, keepdims=True), 0.0)
        top_ref[0, head : head + 1, :] = jnp.broadcast_to(top, (top.shape[0], 128)).T[0:1, :]
        sum_ref[0, head : head + 1, :] = jnp.broadcast_to(total, (total.shape[0], 128)).T[0:1, :]
        result = summed if result is None else jnp.where(mine, summed, result)
    acc_ref[0] = jnp.where(any_valid, result, 0.0)


def cache_merged(slot_queries, k_cache, v_cache, home_lens):
    local_reqs, tree_slots, head_local = slot_queries.shape[:3]
    cache_local = k_cache.shape[1]
    width = head_local * HD
    rows = tree_slots * GROUP
    key_start = (lax.axis_index("ty") * cache_local).astype(jnp.int32).reshape(1)
    spread = slot_queries.transpose(0, 1, 3, 2, 4).reshape(local_reqs, rows, width)
    top, total, summed = pl.pallas_call(
        cache_kernel,
        grid_spec=pltpu.PrefetchScalarGridSpec(
            num_scalar_prefetch=2,
            grid=(local_reqs,),
            in_specs=[
                pl.BlockSpec((1, rows, width), lambda s, lens, start: (s, 0, 0)),
                pl.BlockSpec((1, cache_local, width), lambda s, lens, start: (s, 0, 0)),
                pl.BlockSpec((1, cache_local, width), lambda s, lens, start: (s, 0, 0)),
            ],
            out_specs=[
                pl.BlockSpec((1, head_local, rows), lambda s, lens, start: (s, 0, 0)),
                pl.BlockSpec((1, head_local, rows), lambda s, lens, start: (s, 0, 0)),
                pl.BlockSpec((1, rows, width), lambda s, lens, start: (s, 0, 0)),
            ],
        ),
        out_shape=[
            jax.ShapeDtypeStruct((local_reqs, head_local, rows), jnp.float32),
            jax.ShapeDtypeStruct((local_reqs, head_local, rows), jnp.float32),
            jax.ShapeDtypeStruct((local_reqs, rows, width), jnp.float32),
        ],
        cost_estimate=pl.CostEstimate(
            flops=4 * local_reqs * head_local * rows * cache_local * width,
            transcendentals=local_reqs * head_local * rows * cache_local,
            bytes_accessed=2 * k_cache.size * 2 + spread.size * 2 + local_reqs * rows * width * 4,
        ),
    )(home_lens, key_start, spread, k_cache, v_cache)
    top_all = ty_max(top)
    scale = jnp.exp(top - top_all)
    scale_lanes = jnp.repeat(scale.transpose(0, 2, 1), HD, axis=2)
    count = total.size
    joint = jnp.concatenate(
        [(summed * scale_lanes).reshape(-1, 128), (total * scale).reshape(count // 128, 128)],
        axis=0,
    )
    joint = axis_sum(joint, "ty", True, jnp.bfloat16, jnp.bfloat16, 2)[: joint.shape[0]]
    joint = joint.astype(jnp.float32)
    summed = joint[: summed.size // 128].reshape(summed.shape)
    total = joint[summed.size // 128 :].reshape(total.shape)
    return (top_all, total, summed)


def ty_max_kernel(x_ref, out_ref, held, send_sem, recv_sem):
    n = lax.axis_size("ty")
    me = lax.axis_index("ty")
    row = lax.axis_index("dp")
    col = lax.axis_index("tx")
    barrier = pltpu.get_barrier_semaphore()
    for step in range(1, n):
        peer = lax.rem(me + step, n)
        pl.semaphore_signal(
            barrier, inc=1, device_id=(row, col, peer), device_id_type=pl.DeviceIdType.MESH
        )
    pl.semaphore_wait(barrier, n - 1)
    copies = []
    for step in range(1, n):
        peer = lax.rem(me + step, n)
        copy = pltpu.make_async_remote_copy(
            src_ref=x_ref,
            dst_ref=held.at[step - 1],
            send_sem=send_sem.at[step - 1],
            recv_sem=recv_sem.at[step - 1],
            device_id=(row, col, peer),
            device_id_type=pl.DeviceIdType.MESH,
        )
        copy.start()
        copies.append(copy)
    for copy in copies:
        copy.wait()
    result = x_ref[...]
    for step in range(1, n):
        result = jnp.maximum(result, held[step - 1])
    out_ref[...] = result


def axis_sum_kernel(axis, gather, x_ref, out_ref, held, gathered, sems):
    n = lax.axis_size(axis)
    me = lax.axis_index(axis)
    chunk = held.shape[1]
    where = {name: lax.axis_index(name) for name in ("dp", "tx", "ty")}

    def device(peer):
        return tuple(peer if name == axis else where[name] for name in ("dp", "tx", "ty"))

    barrier = pltpu.get_barrier_semaphore()
    for step in range(1, n):
        pl.semaphore_signal(
            barrier, inc=1, device_id=device(lax.rem(me + step, n)), device_id_type=pl.DeviceIdType.MESH
        )
    pl.semaphore_wait(barrier, n - 1)
    copies = []
    for step in range(1, n):
        peer = lax.rem(me + step, n)
        copy = pltpu.make_async_remote_copy(
            src_ref=x_ref.at[pl.ds(pl.multiple_of(peer * chunk, 16), chunk)],
            dst_ref=held.at[step - 1],
            send_sem=sems.at[0, step - 1],
            recv_sem=sems.at[1, step - 1],
            device_id=device(peer),
            device_id_type=pl.DeviceIdType.MESH,
        )
        copy.start()
        copies.append(copy)
    for copy in copies:
        copy.wait()
    own = pl.ds(pl.multiple_of(me * chunk, 16), chunk)
    total = x_ref[own].astype(jnp.float32)
    for step in range(1, n):
        total = total + held[step - 1].astype(jnp.float32)
    if not gather:
        out_ref[...] = total.astype(out_ref.dtype)
        return
    out_ref[own] = total.astype(out_ref.dtype)
    copies = []
    for step in range(1, n):
        peer = lax.rem(me + step, n)
        copy = pltpu.make_async_remote_copy(
            src_ref=out_ref.at[own],
            dst_ref=gathered.at[step - 1],
            send_sem=sems.at[2, step - 1],
            recv_sem=sems.at[3, step - 1],
            device_id=device(peer),
            device_id_type=pl.DeviceIdType.MESH,
        )
        copy.start()
        copies.append(copy)
    for copy in copies:
        copy.wait()
    for step in range(1, n):
        source = lax.rem(me - step + n, n)
        out_ref[pl.ds(pl.multiple_of(source * chunk, 16), chunk)] = gathered[step - 1]


def axis_sum(values, axis, gather, send_type, out_type, collective_id):
    n = lax.axis_size(axis)
    flat = values.reshape(-1, 128).astype(send_type)
    rows = flat.shape[0]
    padded = -(-rows // (16 * n)) * 16 * n
    flat = jnp.pad(flat, ((0, padded - rows), (0, 0)))
    chunk = padded // n
    out = pl.pallas_call(
        functools.partial(axis_sum_kernel, axis, gather),
        out_shape=jax.ShapeDtypeStruct((padded if gather else chunk, 128), out_type),
        in_specs=[pl.BlockSpec(memory_space=pltpu.VMEM)],
        out_specs=pl.BlockSpec(memory_space=pltpu.VMEM),
        scratch_shapes=[
            pltpu.VMEM((n - 1, chunk, 128), send_type),
            pltpu.VMEM((n - 1, chunk, 128), out_type),
            pltpu.SemaphoreType.DMA((4, n - 1)),
        ],
        compiler_params=pltpu.CompilerParams(collective_id=collective_id, has_side_effects=True),
    )(flat)
    return out


def dp_exchange_kernel(x_ref, out_ref, held, sems):
    n = lax.axis_size("dp")
    me = lax.axis_index("dp")
    col = lax.axis_index("tx")
    row = lax.axis_index("ty")
    barrier = pltpu.get_barrier_semaphore()
    for step in range(1, n):
        pl.semaphore_signal(
            barrier, inc=1, device_id=(lax.rem(me + step, n), col, row), device_id_type=pl.DeviceIdType.MESH
        )
    pl.semaphore_wait(barrier, n - 1)
    copies = []
    for step in range(1, n):
        peer = lax.rem(me + step, n)
        copy = pltpu.make_async_remote_copy(
            src_ref=x_ref.at[peer],
            dst_ref=held.at[step - 1],
            send_sem=sems.at[0, step - 1],
            recv_sem=sems.at[1, step - 1],
            device_id=(peer, col, row),
            device_id_type=pl.DeviceIdType.MESH,
        )
        copy.start()
        copies.append(copy)
    out_ref[me] = x_ref[me]
    for copy in copies:
        copy.wait()
    for step in range(1, n):
        out_ref[lax.rem(me - step + n, n)] = held[step - 1]


def dp_exchange(blocks, collective_id):
    n = lax.axis_size("dp")
    shape = blocks.shape
    tiles = blocks.reshape(n, -1, 128)
    out = pl.pallas_call(
        dp_exchange_kernel,
        out_shape=jax.ShapeDtypeStruct(tiles.shape, tiles.dtype),
        in_specs=[pl.BlockSpec(memory_space=pltpu.VMEM)],
        out_specs=pl.BlockSpec(memory_space=pltpu.VMEM),
        scratch_shapes=[
            pltpu.VMEM((n - 1,) + tiles.shape[1:], tiles.dtype),
            pltpu.SemaphoreType.DMA((2, n - 1)),
        ],
        compiler_params=pltpu.CompilerParams(collective_id=collective_id, has_side_effects=True),
    )(tiles)
    return out.reshape(shape)


def axis_gather_kernel(axis, x_ref, out_ref, gathered, sems):
    n = lax.axis_size(axis)
    me = lax.axis_index(axis)
    chunk = x_ref.shape[0]
    where = {name: lax.axis_index(name) for name in ("dp", "tx", "ty")}

    def device(peer):
        return tuple(peer if name == axis else where[name] for name in ("dp", "tx", "ty"))

    barrier = pltpu.get_barrier_semaphore()
    for step in range(1, n):
        pl.semaphore_signal(
            barrier, inc=1, device_id=device(lax.rem(me + step, n)), device_id_type=pl.DeviceIdType.MESH
        )
    pl.semaphore_wait(barrier, n - 1)
    copies = []
    for step in range(1, n):
        peer = lax.rem(me + step, n)
        copy = pltpu.make_async_remote_copy(
            src_ref=x_ref,
            dst_ref=gathered.at[step - 1],
            send_sem=sems.at[0, step - 1],
            recv_sem=sems.at[1, step - 1],
            device_id=device(peer),
            device_id_type=pl.DeviceIdType.MESH,
        )
        copy.start()
        copies.append(copy)
    out_ref[pl.ds(pl.multiple_of(me * chunk, 16), chunk)] = x_ref[...]
    for copy in copies:
        copy.wait()
    for step in range(1, n):
        source = lax.rem(me - step + n, n)
        out_ref[pl.ds(pl.multiple_of(source * chunk, 16), chunk)] = gathered[step - 1]


def axis_gather(values, axis, collective_id):
    n = lax.axis_size(axis)
    flat = values.reshape(-1, 128)
    chunk = flat.shape[0]
    out = pl.pallas_call(
        functools.partial(axis_gather_kernel, axis),
        out_shape=jax.ShapeDtypeStruct((n * chunk, 128), flat.dtype),
        in_specs=[pl.BlockSpec(memory_space=pltpu.VMEM)],
        out_specs=pl.BlockSpec(memory_space=pltpu.VMEM),
        scratch_shapes=[
            pltpu.VMEM((n - 1, chunk, 128), flat.dtype),
            pltpu.SemaphoreType.DMA((2, n - 1)),
        ],
        compiler_params=pltpu.CompilerParams(collective_id=collective_id, has_side_effects=True),
    )(flat)
    return out.reshape((n * values.shape[0],) + values.shape[1:])


def ty_max(values):
    n = lax.axis_size("ty")
    flat = values.reshape(-1, 128)
    out = pl.pallas_call(
        ty_max_kernel,
        out_shape=jax.ShapeDtypeStruct(flat.shape, flat.dtype),
        in_specs=[pl.BlockSpec(memory_space=pltpu.VMEM)],
        out_specs=pl.BlockSpec(memory_space=pltpu.VMEM),
        scratch_shapes=[
            pltpu.VMEM((n - 1,) + flat.shape, flat.dtype),
            pltpu.SemaphoreType.DMA((n - 1,)),
            pltpu.SemaphoreType.DMA((n - 1,)),
        ],
        compiler_params=pltpu.CompilerParams(collective_id=0, has_side_effects=True),
    )(flat)
    return out.reshape(values.shape)


def shards(
    hidden_in,
    norm_gain,
    w_qkv,
    w_out,
    k_cache,
    v_cache,
    cache_lens,
    home_slot,
    parents,
    tree_sizes,
    leaf_node,
):
    group_count = lax.axis_size("dp")
    group_index = lax.axis_index("dp")
    local_reqs = k_cache.shape[0]
    tree_slots = parents.shape[1]
    capacity = (local_reqs + group_count - 1) // group_count
    head_local = k_cache.shape[2] // HD
    row_count = hidden_in.shape[0]
    float_in = hidden_in.astype(jnp.float32)
    feature_local = hidden_in.shape[1]
    gain_part = lax.dynamic_slice_in_dim(
        norm_gain, lax.axis_index("ty") * feature_local, feature_local
    )
    scaled = (float_in * gain_part.astype(jnp.float32)).astype(jnp.bfloat16)
    partial_proj = jnp.dot(scaled, w_qkv, preferred_element_type=jnp.float32)
    partial_square = jnp.sum(float_in * float_in, axis=1)
    proj_cols = partial_proj.shape[1]
    n_ty = lax.axis_size("ty")
    chunk_rows = row_count // n_ty
    reqs_mine = local_reqs // n_ty
    square_block = jnp.pad(
        partial_square.reshape(n_ty, 1, chunk_rows),
        ((0, 0), (0, 7), (0, proj_cols - chunk_rows)),
    )
    joint = jnp.concatenate(
        [partial_proj.reshape(n_ty, chunk_rows, proj_cols), square_block], axis=1
    )
    mine = axis_sum(joint, "ty", False, jnp.float32, jnp.float32, 1).reshape(-1, proj_cols)
    square_sum = mine[chunk_rows, :chunk_rows]
    rms_inverse = lax.rsqrt(square_sum / D + norm_eps)
    projected = (mine[:chunk_rows] * rms_inverse[:, None]).reshape(
        reqs_mine, tree_slots, head_local, GROUP + 2, HD
    )
    first_request = group_index * local_reqs
    local_ids = jnp.arange(local_reqs, dtype=jnp.int32)
    request_ids = jnp.arange(home_slot.shape[0], dtype=jnp.int32)
    my_parents = lax.dynamic_slice_in_dim(parents, first_request, local_reqs, 0)
    my_slots = lax.dynamic_slice_in_dim(home_slot, first_request, local_reqs, 0)
    ancestors = jax.vmap(ancestry)(my_parents)
    node_depth = jnp.sum(ancestors > 0.5, axis=2) - 1
    slot_match = my_slots[:, None] == request_ids[None, :]
    my_lens = jnp.sum(jnp.where(slot_match, cache_lens[None, :], 0), axis=1)
    positions = my_lens[:, None] + node_depth
    positions_mine = lax.dynamic_slice_in_dim(
        positions, lax.axis_index("ty") * reqs_mine, reqs_mine, 0
    )
    queries_mine = rotated(
        projected[:, :, :, :GROUP, :], positions_mine[:, :, None, None]
    ).astype(jnp.bfloat16)
    keys_mine = rotated(projected[:, :, :, GROUP, :], positions_mine[:, :, None]).astype(
        jnp.bfloat16
    )
    values_mine = projected[:, :, :, GROUP + 1, :].astype(jnp.bfloat16)
    piece = jnp.concatenate(
        [
            queries_mine.reshape(chunk_rows, -1),
            keys_mine.reshape(chunk_rows, -1),
            values_mine.reshape(chunk_rows, -1),
        ],
        axis=1,
    )
    everything = axis_gather(piece, "ty", 6)
    query_cols = head_local * GROUP * HD
    queries = everything[:, :query_cols].reshape(local_reqs, tree_slots, head_local, GROUP, HD)
    keys_new = everything[:, query_cols : query_cols + head_local * HD].reshape(
        local_reqs, tree_slots, head_local, HD
    )
    values_new = everything[:, query_cols + head_local * HD :].reshape(
        local_reqs, tree_slots, head_local, HD
    )
    dest_group, dest_rank = routing(home_slot, group_count, local_reqs)
    send_pos = lax.dynamic_index_in_dim(
        dest_group, group_index, 0, keepdims=False
    ) * capacity + lax.dynamic_index_in_dim(dest_rank, group_index, 0, keepdims=False)
    buffer_ids = jnp.arange(group_count * capacity, dtype=jnp.int32)
    send_hit = send_pos[None, :] == buffer_ids[:, None]
    send_index = jnp.where(
        jnp.any(send_hit, axis=1),
        jnp.sum(jnp.where(send_hit, local_ids[None, :], 0), axis=1),
        local_reqs,
    )
    target_slots = first_request + local_ids
    owner_match = home_slot[None, :] == target_slots[:, None]
    owner_request = jnp.sum(jnp.where(owner_match, request_ids[None, :], 0), axis=1)
    owner_rank = jnp.sum(jnp.where(owner_match, dest_rank.reshape(-1)[None, :], 0), axis=1)
    recv_index = owner_request // local_reqs * capacity + owner_rank
    back_hit = recv_index[None, :] == buffer_ids[:, None]
    back_index = jnp.where(
        jnp.any(back_hit, axis=1),
        jnp.sum(jnp.where(back_hit, local_ids[None, :], 0), axis=1),
        local_reqs,
    )
    home_lens = lax.dynamic_slice_in_dim(cache_lens, first_request, local_reqs, 0)
    arrived = dp_exchange(packed(queries.reshape(local_reqs, -1), send_index), 4)
    slot_queries = packed(arrived, recv_index).reshape(queries.shape)
    top_score, weight_sum, summed = cache_merged(slot_queries, k_cache, v_cache, home_lens)
    normalized = summed / jnp.repeat(weight_sum.transpose(0, 2, 1), HD, axis=2)
    log_total = top_score + jnp.log(weight_sum)
    value_width = normalized.size // local_reqs
    log_flat = log_total.reshape(local_reqs, -1)
    log_high = lax.reduce_precision(log_flat, exponent_bits=8, mantissa_bits=7)
    log_rest = log_flat - log_high
    log_mid = lax.reduce_precision(log_rest, exponent_bits=8, mantissa_bits=7)
    log_low = log_rest - log_mid
    payload = jnp.concatenate(
        [normalized.reshape(local_reqs, -1), log_high, log_mid, log_low], axis=1
    ).astype(jnp.bfloat16)
    back = lax.all_to_all(
        packed(payload, back_index), "dp", split_axis=0, concat_axis=0, tiled=True
    )
    back = packed(back, send_pos).astype(jnp.float32)
    log_width = log_flat.shape[1]
    cache_values = (
        back[:, :value_width]
        .reshape(local_reqs, tree_slots, GROUP, head_local, HD)
        .transpose(0, 1, 3, 2, 4)
    )
    cache_top = (
        (
            back[:, value_width : value_width + log_width]
            + back[:, value_width + log_width : value_width + 2 * log_width]
            + back[:, value_width + 2 * log_width :]
        )
        .reshape(local_reqs, head_local, tree_slots, GROUP)
        .transpose(0, 2, 1, 3)
    )
    tree_stats = tree_part(queries, keys_new, values_new, ancestors)
    top_all, sum_all, summed_all = combine_stats(
        (cache_top, jnp.ones_like(cache_top), cache_values), tree_stats
    )
    attention = (summed_all / sum_all[..., None]).astype(jnp.bfloat16)
    attention_rows = attention.reshape(row_count, -1)
    rows_mine = row_count // lax.axis_size("tx")
    mixed_sum = axis_sum(
        jnp.dot(attention_rows, w_out, preferred_element_type=jnp.float32),
        "tx",
        False,
        jnp.bfloat16,
        jnp.float32,
        3,
    ).reshape(row_count // lax.axis_size("tx"), -1)
    row_start = lax.axis_index("tx") * rows_mine
    residual = lax.dynamic_slice_in_dim(float_in, row_start, rows_mine, 0)
    row_ids = row_start + jnp.arange(rows_mine, dtype=jnp.int32)
    request_of = row_ids // tree_slots
    slot_of = row_ids % tree_slots
    size_of = jnp.sum(
        jnp.where(request_of[:, None] == local_ids[None, :], tree_sizes[None, :], 0), axis=1
    )
    layer_out = jnp.where((slot_of < size_of)[:, None], residual + mixed_sum, 0.0).astype(
        jnp.bfloat16
    )
    node_ids = jnp.arange(tree_slots, dtype=jnp.int32)
    leaf_hit = (leaf_node[:, None] == node_ids[None, :]).astype(jnp.float32)
    path_nodes = jnp.einsum("rt,rtu->ru", leaf_hit, ancestors)
    depth_hit = node_depth[:, None, :] == jnp.arange(ACC, dtype=jnp.int32)[None, :, None]
    chooser = jnp.where(depth_hit, path_nodes[:, None, :], 0.0).astype(jnp.bfloat16)
    stacked = jnp.stack(
        [
            keys_new.reshape(local_reqs, tree_slots, -1),
            values_new.reshape(local_reqs, tree_slots, -1),
        ],
        axis=2,
    )
    accepted_kv = jnp.einsum(
        "rsu,ruwc->rswc", chooser, stacked, preferred_element_type=jnp.float32
    ).astype(jnp.bfloat16)
    return (layer_out, accepted_kv)


def solution(mesh):
    return jax.shard_map(
        shards,
        mesh=mesh,
        in_specs=(
            P("dp", "ty"),
            P(),
            P("ty", "tx"),
            P("tx", "ty"),
            P("dp", "ty", "tx"),
            P("dp", "ty", "tx"),
            P(),
            P(),
            P(),
            P("dp"),
            P("dp"),
        ),
        out_specs=(P(("dp", "tx"), "ty"), P("dp", None, None, "tx")),
        check_vma=False,
    )
```

```python
import functools

import jax
import jax.numpy as jnp
from jax import lax
from jax.experimental import pallas as pl
from jax.experimental.pallas import tpu as pltpu
from jax.sharding import PartitionSpec as P

D = 2048
HD = 64
GROUP = 4
ACC = 8


rope_base = 10000000.0
attn_mult = 0.015625
norm_eps = 1e-05
neg_fill = -1e30


def joined(value, axis, join):
    pieces = jax.tree.map(lambda part: lax.all_gather(part, axis), value)
    head = jax.tree.map(lambda part: part[0], pieces)
    tail = jax.tree.map(lambda part: part[1:], pieces)
    so_far, _ = lax.scan(lambda so_far, slab: (join(so_far, slab), None), head, tail)
    return so_far


def ancestry(parent_rows):
    node_count = parent_rows.shape[-1]
    node_ids = jnp.arange(node_count, dtype=jnp.int32)
    linked = (node_ids[None, :] == parent_rows[:, None]) | (node_ids[None, :] == node_ids[:, None])
    reachable = linked.astype(jnp.float32)
    for repeat in range(max(1, (node_count - 1).bit_length())):
        reachable = jnp.minimum(jnp.dot(reachable, reachable, precision=lax.Precision.HIGHEST), 1.0)
    return reachable


def rotated(values, positions):
    half_size = values.shape[-1] // 2
    frequency = rope_base ** (-2.0 * jnp.arange(half_size, dtype=jnp.float32) / values.shape[-1])
    angles = positions.astype(jnp.float32)[..., None] * frequency
    cosine = jnp.cos(angles)
    sine_part = jnp.sin(angles)
    front_half = values[..., :half_size]
    back_half = values[..., half_size:]
    return jnp.concatenate(
        [front_half * cosine - back_half * sine_part, back_half * cosine + front_half * sine_part],
        axis=-1,
    )


def combine_stats(first_stats, second_stats):
    top_first, sum_first, summed_first = first_stats
    top_second, sum_second, summed_second = second_stats
    top_both = jnp.maximum(top_first, top_second)
    scale_first = jnp.exp(top_first - top_both)
    scale_second = jnp.exp(top_second - top_both)
    return (
        top_both,
        sum_first * scale_first + sum_second * scale_second,
        summed_first * scale_first[..., None] + summed_second * scale_second[..., None],
    )


def packed(values, index):
    return jnp.take(values, index, axis=0, mode="fill", fill_value=0)


def routing(home_slot, group_count, local_reqs):
    dest_group = (home_slot // local_reqs).reshape(group_count, local_reqs)
    local_ids = jnp.arange(local_reqs, dtype=jnp.int32)
    earlier = local_ids[None, :] < local_ids[:, None]
    same_dest = dest_group[:, :, None] == dest_group[:, None, :]
    dest_rank = jnp.sum(same_dest & earlier[None], axis=2)
    return (dest_group, dest_rank)


def tree_part(queries, keys_new, values_new, ancestors):
    scores = attn_mult * jnp.einsum(
        "rtkgd,rukd->rtkgu", queries, keys_new, preferred_element_type=jnp.float32
    )
    valid_keys = (ancestors > 0.5)[:, :, None, None, :]
    masked = jnp.where(valid_keys, scores, neg_fill)
    top_score = jnp.max(masked, axis=-1)
    weights = jnp.where(valid_keys, jnp.exp(masked - top_score[..., None]), 0.0)
    summed = jnp.einsum(
        "rtkgu,rukd->rtkgd",
        weights.astype(jnp.bfloat16),
        values_new,
        preferred_element_type=jnp.float32,
    )
    return (top_score, jnp.sum(weights, axis=-1), summed)


def cache_kernel(lens_ref, start_ref, q_ref, k_ref, v_ref, top_ref, sum_ref, acc_ref):
    slot = pl.program_id(0)
    head_local = top_ref.shape[1]
    cache_local = k_ref.shape[1]
    limit = lens_ref[slot] - start_ref[0]
    valid = lax.broadcasted_iota(jnp.int32, (1, cache_local), 1) < limit
    keys = k_ref[0]
    values = v_ref[0]
    lane = lax.broadcasted_iota(jnp.int32, (1, head_local * HD), 1)
    queries = q_ref[0] * jnp.asarray(attn_mult, q_ref.dtype)
    any_valid = limit > 0
    result = None
    for head in range(head_local):
        mine = (lane >= head * HD) & (lane < (head + 1) * HD)
        own = jnp.where(mine, queries, jnp.zeros((), queries.dtype))
        scores = lax.dot_general(
            own, keys, (((1,), (1,)), ((), ())), preferred_element_type=jnp.float32
        )
        masked = jnp.where(valid, scores, neg_fill)
        top = jnp.max(masked, axis=1, keepdims=True)
        weights = jnp.exp(masked - top)
        summed = jnp.dot(weights.astype(jnp.bfloat16), values, preferred_element_type=jnp.float32)
        total = jnp.where(any_valid, jnp.sum(weights, axis=1, keepdims=True), 0.0)
        top_ref[0, head : head + 1, :] = jnp.broadcast_to(top, (top.shape[0], 128)).T[0:1, :]
        sum_ref[0, head : head + 1, :] = jnp.broadcast_to(total, (total.shape[0], 128)).T[0:1, :]
        result = summed if result is None else jnp.where(mine, summed, result)
    acc_ref[0] = jnp.where(any_valid, result, 0.0)


def cache_merged(slot_queries, k_cache, v_cache, home_lens):
    local_reqs, tree_slots, head_local = slot_queries.shape[:3]
    cache_local = k_cache.shape[1]
    width = head_local * HD
    rows = tree_slots * GROUP
    key_start = (lax.axis_index("ty") * cache_local).astype(jnp.int32).reshape(1)
    spread = slot_queries.transpose(0, 1, 3, 2, 4).reshape(local_reqs, rows, width)
    top, total, summed = pl.pallas_call(
        cache_kernel,
        grid_spec=pltpu.PrefetchScalarGridSpec(
            num_scalar_prefetch=2,
            grid=(local_reqs,),
            in_specs=[
                pl.BlockSpec((1, rows, width), lambda s, lens, start: (s, 0, 0)),
                pl.BlockSpec((1, cache_local, width), lambda s, lens, start: (s, 0, 0)),
                pl.BlockSpec((1, cache_local, width), lambda s, lens, start: (s, 0, 0)),
            ],
            out_specs=[
                pl.BlockSpec((1, head_local, rows), lambda s, lens, start: (s, 0, 0)),
                pl.BlockSpec((1, head_local, rows), lambda s, lens, start: (s, 0, 0)),
                pl.BlockSpec((1, rows, width), lambda s, lens, start: (s, 0, 0)),
            ],
        ),
        out_shape=[
            jax.ShapeDtypeStruct((local_reqs, head_local, rows), jnp.float32),
            jax.ShapeDtypeStruct((local_reqs, head_local, rows), jnp.float32),
            jax.ShapeDtypeStruct((local_reqs, rows, width), jnp.float32),
        ],
        cost_estimate=pl.CostEstimate(
            flops=4 * local_reqs * head_local * rows * cache_local * width,
            transcendentals=local_reqs * head_local * rows * cache_local,
            bytes_accessed=2 * k_cache.size * 2 + spread.size * 2 + local_reqs * rows * width * 4,
        ),
    )(home_lens, key_start, spread, k_cache, v_cache)
    top_all = ty_max(top)
    scale = jnp.exp(top - top_all)
    scale_lanes = jnp.repeat(scale.transpose(0, 2, 1), HD, axis=2)
    count = total.size
    joint = jnp.concatenate(
        [(summed * scale_lanes).reshape(-1, 128), (total * scale).reshape(count // 128, 128)],
        axis=0,
    )
    joint = axis_sum(joint, "ty", True, jnp.bfloat16, jnp.bfloat16, 2)[: joint.shape[0]]
    summed = joint[: summed.size // 128].reshape(summed.shape[0], -1)
    total = joint[summed.size // 128 :].reshape(total.shape[0], -1)
    return (top_all, total, summed)


def ty_max_kernel(x_ref, out_ref, held, send_sem, recv_sem):
    n = lax.axis_size("ty")
    me = lax.axis_index("ty")
    row = lax.axis_index("dp")
    col = lax.axis_index("tx")
    barrier = pltpu.get_barrier_semaphore()
    for step in range(1, n):
        peer = lax.rem(me + step, n)
        pl.semaphore_signal(
            barrier, inc=1, device_id=(row, col, peer), device_id_type=pl.DeviceIdType.MESH
        )
    pl.semaphore_wait(barrier, n - 1)
    copies = []
    for step in range(1, n):
        peer = lax.rem(me + step, n)
        copy = pltpu.make_async_remote_copy(
            src_ref=x_ref,
            dst_ref=held.at[step - 1],
            send_sem=send_sem.at[step - 1],
            recv_sem=recv_sem.at[step - 1],
            device_id=(row, col, peer),
            device_id_type=pl.DeviceIdType.MESH,
        )
        copy.start()
        copies.append(copy)
    for copy in copies:
        copy.wait()
    result = x_ref[...]
    for step in range(1, n):
        result = jnp.maximum(result, held[step - 1])
    out_ref[...] = result


def axis_sum_kernel(axis, gather, x_ref, out_ref, held, gathered, sems):
    n = lax.axis_size(axis)
    me = lax.axis_index(axis)
    chunk = held.shape[1]
    where = {name: lax.axis_index(name) for name in ("dp", "tx", "ty")}

    def device(peer):
        return tuple(peer if name == axis else where[name] for name in ("dp", "tx", "ty"))

    barrier = pltpu.get_barrier_semaphore()
    for step in range(1, n):
        pl.semaphore_signal(
            barrier, inc=1, device_id=device(lax.rem(me + step, n)), device_id_type=pl.DeviceIdType.MESH
        )
    pl.semaphore_wait(barrier, n - 1)
    copies = []
    for step in range(1, n):
        peer = lax.rem(me + step, n)
        copy = pltpu.make_async_remote_copy(
            src_ref=x_ref.at[pl.ds(pl.multiple_of(peer * chunk, 16), chunk)],
            dst_ref=held.at[step - 1],
            send_sem=sems.at[0, step - 1],
            recv_sem=sems.at[1, step - 1],
            device_id=device(peer),
            device_id_type=pl.DeviceIdType.MESH,
        )
        copy.start()
        copies.append(copy)
    for copy in copies:
        copy.wait()
    own = pl.ds(pl.multiple_of(me * chunk, 16), chunk)
    total = x_ref[own].astype(jnp.float32)
    for step in range(1, n):
        total = total + held[step - 1].astype(jnp.float32)
    if not gather:
        out_ref[...] = total.astype(out_ref.dtype)
        return
    out_ref[own] = total.astype(out_ref.dtype)
    copies = []
    for step in range(1, n):
        peer = lax.rem(me + step, n)
        copy = pltpu.make_async_remote_copy(
            src_ref=out_ref.at[own],
            dst_ref=gathered.at[step - 1],
            send_sem=sems.at[2, step - 1],
            recv_sem=sems.at[3, step - 1],
            device_id=device(peer),
            device_id_type=pl.DeviceIdType.MESH,
        )
        copy.start()
        copies.append(copy)
    for copy in copies:
        copy.wait()
    for step in range(1, n):
        source = lax.rem(me - step + n, n)
        out_ref[pl.ds(pl.multiple_of(source * chunk, 16), chunk)] = gathered[step - 1]


def axis_sum(values, axis, gather, send_type, out_type, collective_id):
    n = lax.axis_size(axis)
    flat = values.reshape(-1, 128).astype(send_type)
    rows = flat.shape[0]
    padded = -(-rows // (16 * n)) * 16 * n
    flat = jnp.pad(flat, ((0, padded - rows), (0, 0)))
    chunk = padded // n
    out = pl.pallas_call(
        functools.partial(axis_sum_kernel, axis, gather),
        out_shape=jax.ShapeDtypeStruct((padded if gather else chunk, 128), out_type),
        in_specs=[pl.BlockSpec(memory_space=pltpu.VMEM)],
        out_specs=pl.BlockSpec(memory_space=pltpu.VMEM),
        scratch_shapes=[
            pltpu.VMEM((n - 1, chunk, 128), send_type),
            pltpu.VMEM((n - 1, chunk, 128), out_type),
            pltpu.SemaphoreType.DMA((4, n - 1)),
        ],
        compiler_params=pltpu.CompilerParams(collective_id=collective_id, has_side_effects=True),
    )(flat)
    return out


def dp_exchange_kernel(x_ref, out_ref, held, sems):
    n = lax.axis_size("dp")
    me = lax.axis_index("dp")
    col = lax.axis_index("tx")
    row = lax.axis_index("ty")
    barrier = pltpu.get_barrier_semaphore()
    for step in range(1, n):
        pl.semaphore_signal(
            barrier, inc=1, device_id=(lax.rem(me + step, n), col, row), device_id_type=pl.DeviceIdType.MESH
        )
    pl.semaphore_wait(barrier, n - 1)
    copies = []
    for step in range(1, n):
        peer = lax.rem(me + step, n)
        copy = pltpu.make_async_remote_copy(
            src_ref=x_ref.at[peer],
            dst_ref=held.at[step - 1],
            send_sem=sems.at[0, step - 1],
            recv_sem=sems.at[1, step - 1],
            device_id=(peer, col, row),
            device_id_type=pl.DeviceIdType.MESH,
        )
        copy.start()
        copies.append(copy)
    out_ref[me] = x_ref[me]
    for copy in copies:
        copy.wait()
    for step in range(1, n):
        out_ref[lax.rem(me - step + n, n)] = held[step - 1]


def dp_exchange(blocks, collective_id):
    n = lax.axis_size("dp")
    shape = blocks.shape
    tiles = blocks.reshape(n, -1, 128)
    out = pl.pallas_call(
        dp_exchange_kernel,
        out_shape=jax.ShapeDtypeStruct(tiles.shape, tiles.dtype),
        in_specs=[pl.BlockSpec(memory_space=pltpu.VMEM)],
        out_specs=pl.BlockSpec(memory_space=pltpu.VMEM),
        scratch_shapes=[
            pltpu.VMEM((n - 1,) + tiles.shape[1:], tiles.dtype),
            pltpu.SemaphoreType.DMA((2, n - 1)),
        ],
        compiler_params=pltpu.CompilerParams(collective_id=collective_id, has_side_effects=True),
    )(tiles)
    return out.reshape(shape)


def axis_gather_kernel(axis, x_ref, out_ref, gathered, sems):
    n = lax.axis_size(axis)
    me = lax.axis_index(axis)
    chunk = x_ref.shape[0]
    where = {name: lax.axis_index(name) for name in ("dp", "tx", "ty")}

    def device(peer):
        return tuple(peer if name == axis else where[name] for name in ("dp", "tx", "ty"))

    barrier = pltpu.get_barrier_semaphore()
    for step in range(1, n):
        pl.semaphore_signal(
            barrier, inc=1, device_id=device(lax.rem(me + step, n)), device_id_type=pl.DeviceIdType.MESH
        )
    pl.semaphore_wait(barrier, n - 1)
    copies = []
    for step in range(1, n):
        peer = lax.rem(me + step, n)
        copy = pltpu.make_async_remote_copy(
            src_ref=x_ref,
            dst_ref=gathered.at[step - 1],
            send_sem=sems.at[0, step - 1],
            recv_sem=sems.at[1, step - 1],
            device_id=device(peer),
            device_id_type=pl.DeviceIdType.MESH,
        )
        copy.start()
        copies.append(copy)
    out_ref[pl.ds(pl.multiple_of(me * chunk, 16), chunk)] = x_ref[...]
    for copy in copies:
        copy.wait()
    for step in range(1, n):
        source = lax.rem(me - step + n, n)
        out_ref[pl.ds(pl.multiple_of(source * chunk, 16), chunk)] = gathered[step - 1]


def axis_gather(values, axis, collective_id):
    n = lax.axis_size(axis)
    flat = values.reshape(-1, 128)
    chunk = flat.shape[0]
    out = pl.pallas_call(
        functools.partial(axis_gather_kernel, axis),
        out_shape=jax.ShapeDtypeStruct((n * chunk, 128), flat.dtype),
        in_specs=[pl.BlockSpec(memory_space=pltpu.VMEM)],
        out_specs=pl.BlockSpec(memory_space=pltpu.VMEM),
        scratch_shapes=[
            pltpu.VMEM((n - 1, chunk, 128), flat.dtype),
            pltpu.SemaphoreType.DMA((2, n - 1)),
        ],
        compiler_params=pltpu.CompilerParams(collective_id=collective_id, has_side_effects=True),
    )(flat)
    return out.reshape((n * values.shape[0],) + values.shape[1:])


def ty_max(values):
    n = lax.axis_size("ty")
    flat = values.reshape(-1, 128)
    out = pl.pallas_call(
        ty_max_kernel,
        out_shape=jax.ShapeDtypeStruct(flat.shape, flat.dtype),
        in_specs=[pl.BlockSpec(memory_space=pltpu.VMEM)],
        out_specs=pl.BlockSpec(memory_space=pltpu.VMEM),
        scratch_shapes=[
            pltpu.VMEM((n - 1,) + flat.shape, flat.dtype),
            pltpu.SemaphoreType.DMA((n - 1,)),
            pltpu.SemaphoreType.DMA((n - 1,)),
        ],
        compiler_params=pltpu.CompilerParams(collective_id=0, has_side_effects=True),
    )(flat)
    return out.reshape(values.shape)


def shards(
    hidden_in,
    norm_gain,
    w_qkv,
    w_out,
    k_cache,
    v_cache,
    cache_lens,
    home_slot,
    parents,
    tree_sizes,
    leaf_node,
):
    group_count = lax.axis_size("dp")
    group_index = lax.axis_index("dp")
    local_reqs = k_cache.shape[0]
    tree_slots = parents.shape[1]
    capacity = (local_reqs + group_count - 1) // group_count
    head_local = k_cache.shape[2] // HD
    row_count = hidden_in.shape[0]
    float_in = hidden_in.astype(jnp.float32)
    feature_local = hidden_in.shape[1]
    gain_part = lax.dynamic_slice_in_dim(
        norm_gain, lax.axis_index("ty") * feature_local, feature_local
    )
    scaled = (float_in * gain_part.astype(jnp.float32)).astype(jnp.bfloat16)
    partial_proj = jnp.dot(scaled, w_qkv, preferred_element_type=jnp.float32)
    partial_square = jnp.sum(float_in * float_in, axis=1)
    proj_cols = partial_proj.shape[1]
    n_ty = lax.axis_size("ty")
    chunk_rows = row_count // n_ty
    reqs_mine = local_reqs // n_ty
    square_block = jnp.pad(
        partial_square.reshape(n_ty, 1, chunk_rows),
        ((0, 0), (0, 7), (0, proj_cols - chunk_rows)),
    )
    joint = jnp.concatenate(
        [partial_proj.reshape(n_ty, chunk_rows, proj_cols), square_block], axis=1
    )
    mine = axis_sum(joint, "ty", False, jnp.float32, jnp.float32, 1).reshape(-1, proj_cols)
    square_sum = mine[chunk_rows, :chunk_rows]
    rms_inverse = lax.rsqrt(square_sum / D + norm_eps)
    projected = (mine[:chunk_rows] * rms_inverse[:, None]).reshape(
        reqs_mine, tree_slots, head_local, GROUP + 2, HD
    )
    first_request = group_index * local_reqs
    local_ids = jnp.arange(local_reqs, dtype=jnp.int32)
    request_ids = jnp.arange(home_slot.shape[0], dtype=jnp.int32)
    my_parents = lax.dynamic_slice_in_dim(parents, first_request, local_reqs, 0)
    my_slots = lax.dynamic_slice_in_dim(home_slot, first_request, local_reqs, 0)
    ancestors = jax.vmap(ancestry)(my_parents)
    node_depth = jnp.sum(ancestors > 0.5, axis=2) - 1
    slot_match = my_slots[:, None] == request_ids[None, :]
    my_lens = jnp.sum(jnp.where(slot_match, cache_lens[None, :], 0), axis=1)
    positions = my_lens[:, None] + node_depth
    positions_mine = lax.dynamic_slice_in_dim(
        positions, lax.axis_index("ty") * reqs_mine, reqs_mine, 0
    )
    queries_mine = rotated(
        projected[:, :, :, :GROUP, :], positions_mine[:, :, None, None]
    ).astype(jnp.bfloat16)
    keys_mine = rotated(projected[:, :, :, GROUP, :], positions_mine[:, :, None]).astype(
        jnp.bfloat16
    )
    values_mine = projected[:, :, :, GROUP + 1, :].astype(jnp.bfloat16)
    piece = jnp.concatenate(
        [
            queries_mine.reshape(chunk_rows, -1),
            keys_mine.reshape(chunk_rows, -1),
            values_mine.reshape(chunk_rows, -1),
        ],
        axis=1,
    )
    everything = axis_gather(piece, "ty", 6)
    query_cols = head_local * GROUP * HD
    queries = everything[:, :query_cols].reshape(local_reqs, tree_slots, head_local, GROUP, HD)
    keys_new = everything[:, query_cols : query_cols + head_local * HD].reshape(
        local_reqs, tree_slots, head_local, HD
    )
    values_new = everything[:, query_cols + head_local * HD :].reshape(
        local_reqs, tree_slots, head_local, HD
    )
    dest_group, dest_rank = routing(home_slot, group_count, local_reqs)
    send_pos = lax.dynamic_index_in_dim(
        dest_group, group_index, 0, keepdims=False
    ) * capacity + lax.dynamic_index_in_dim(dest_rank, group_index, 0, keepdims=False)
    buffer_ids = jnp.arange(group_count * capacity, dtype=jnp.int32)
    send_hit = send_pos[None, :] == buffer_ids[:, None]
    send_index = jnp.where(
        jnp.any(send_hit, axis=1),
        jnp.sum(jnp.where(send_hit, local_ids[None, :], 0), axis=1),
        local_reqs,
    )
    target_slots = first_request + local_ids
    owner_match = home_slot[None, :] == target_slots[:, None]
    owner_request = jnp.sum(jnp.where(owner_match, request_ids[None, :], 0), axis=1)
    owner_rank = jnp.sum(jnp.where(owner_match, dest_rank.reshape(-1)[None, :], 0), axis=1)
    recv_index = owner_request // local_reqs * capacity + owner_rank
    back_hit = recv_index[None, :] == buffer_ids[:, None]
    back_index = jnp.where(
        jnp.any(back_hit, axis=1),
        jnp.sum(jnp.where(back_hit, local_ids[None, :], 0), axis=1),
        local_reqs,
    )
    home_lens = lax.dynamic_slice_in_dim(cache_lens, first_request, local_reqs, 0)
    arrived = dp_exchange(packed(queries.reshape(local_reqs, -1), send_index), 4)
    slot_queries = packed(arrived, recv_index).reshape(queries.shape)
    top_score, weight_sum, summed = cache_merged(slot_queries, k_cache, v_cache, home_lens)
    value_width = summed.shape[1]
    sum_width = weight_sum.shape[1]
    log_flat = top_score.reshape(local_reqs, -1)
    log_high = lax.reduce_precision(log_flat, exponent_bits=8, mantissa_bits=7)
    log_rest = log_flat - log_high
    log_mid = lax.reduce_precision(log_rest, exponent_bits=8, mantissa_bits=7)
    log_low = log_rest - log_mid
    payload = jnp.concatenate(
        [
            summed,
            weight_sum,
            log_high.astype(jnp.bfloat16),
            log_mid.astype(jnp.bfloat16),
            log_low.astype(jnp.bfloat16),
        ],
        axis=1,
    )
    back = lax.all_to_all(
        packed(payload, back_index), "dp", split_axis=0, concat_axis=0, tiled=True
    )
    back = packed(back, send_pos).astype(jnp.float32)
    log_width = log_flat.shape[1]
    cache_values = (
        back[:, :value_width]
        .reshape(local_reqs, tree_slots, GROUP, head_local, HD)
        .transpose(0, 1, 3, 2, 4)
    )
    cache_sum = (
        back[:, value_width : value_width + sum_width]
        .reshape(local_reqs, head_local, tree_slots, GROUP)
        .transpose(0, 2, 1, 3)
    )
    logs = value_width + sum_width
    cache_top = (
        (
            back[:, logs : logs + log_width]
            + back[:, logs + log_width : logs + 2 * log_width]
            + back[:, logs + 2 * log_width :]
        )
        .reshape(local_reqs, head_local, tree_slots, GROUP)
        .transpose(0, 2, 1, 3)
    )
    tree_stats = tree_part(queries, keys_new, values_new, ancestors)
    top_all, sum_all, summed_all = combine_stats(
        (cache_top, cache_sum, cache_values), tree_stats
    )
    attention = (summed_all / sum_all[..., None]).astype(jnp.bfloat16)
    attention_rows = attention.reshape(row_count, -1)
    rows_mine = row_count // lax.axis_size("tx")
    mixed_sum = axis_sum(
        jnp.dot(attention_rows, w_out, preferred_element_type=jnp.float32),
        "tx",
        False,
        jnp.bfloat16,
        jnp.float32,
        3,
    ).reshape(row_count // lax.axis_size("tx"), -1)
    row_start = lax.axis_index("tx") * rows_mine
    residual = lax.dynamic_slice_in_dim(float_in, row_start, rows_mine, 0)
    row_ids = row_start + jnp.arange(rows_mine, dtype=jnp.int32)
    request_of = row_ids // tree_slots
    slot_of = row_ids % tree_slots
    size_of = jnp.sum(
        jnp.where(request_of[:, None] == local_ids[None, :], tree_sizes[None, :], 0), axis=1
    )
    layer_out = jnp.where((slot_of < size_of)[:, None], residual + mixed_sum, 0.0).astype(
        jnp.bfloat16
    )
    node_ids = jnp.arange(tree_slots, dtype=jnp.int32)
    leaf_hit = (leaf_node[:, None] == node_ids[None, :]).astype(jnp.float32)
    path_nodes = jnp.einsum("rt,rtu->ru", leaf_hit, ancestors)
    depth_hit = node_depth[:, None, :] == jnp.arange(ACC, dtype=jnp.int32)[None, :, None]
    chooser = jnp.where(depth_hit, path_nodes[:, None, :], 0.0).astype(jnp.bfloat16)
    stacked = jnp.stack(
        [
            keys_new.reshape(local_reqs, tree_slots, -1),
            values_new.reshape(local_reqs, tree_slots, -1),
        ],
        axis=2,
    )
    accepted_kv = jnp.einsum(
        "rsu,ruwc->rswc", chooser, stacked, preferred_element_type=jnp.float32
    ).astype(jnp.bfloat16)
    return (layer_out, accepted_kv)


def solution(mesh):
    return jax.shard_map(
        shards,
        mesh=mesh,
        in_specs=(
            P("dp", "ty"),
            P(),
            P("ty", "tx"),
            P("tx", "ty"),
            P("dp", "ty", "tx"),
            P("dp", "ty", "tx"),
            P(),
            P(),
            P(),
            P("dp"),
            P("dp"),
        ),
        out_specs=(P(("dp", "tx"), "ty"), P("dp", None, None, "tx")),
        check_vma=False,
    )
```

```python
import functools

import jax
import jax.numpy as jnp
from jax import lax
from jax.experimental import pallas as pl
from jax.experimental.pallas import tpu as pltpu
from jax.sharding import PartitionSpec as P

D = 2048
HD = 64
GROUP = 4
ACC = 8


rope_base = 10000000.0
attn_mult = 0.015625
norm_eps = 1e-05
neg_fill = -1e30


def joined(value, axis, join):
    pieces = jax.tree.map(lambda part: lax.all_gather(part, axis), value)
    head = jax.tree.map(lambda part: part[0], pieces)
    tail = jax.tree.map(lambda part: part[1:], pieces)
    so_far, _ = lax.scan(lambda so_far, slab: (join(so_far, slab), None), head, tail)
    return so_far


def ancestry(parent_rows):
    node_count = parent_rows.shape[-1]
    node_ids = jnp.arange(node_count, dtype=jnp.int32)
    linked = (node_ids[None, :] == parent_rows[:, None]) | (node_ids[None, :] == node_ids[:, None])
    reachable = linked.astype(jnp.float32)
    for repeat in range(max(1, (node_count - 1).bit_length())):
        reachable = jnp.minimum(jnp.dot(reachable, reachable, precision=lax.Precision.HIGHEST), 1.0)
    return reachable


def rotated(values, positions):
    half_size = values.shape[-1] // 2
    frequency = rope_base ** (-2.0 * jnp.arange(half_size, dtype=jnp.float32) / values.shape[-1])
    angles = positions.astype(jnp.float32)[..., None] * frequency
    cosine = jnp.cos(angles)
    sine_part = jnp.sin(angles)
    front_half = values[..., :half_size]
    back_half = values[..., half_size:]
    return jnp.concatenate(
        [front_half * cosine - back_half * sine_part, back_half * cosine + front_half * sine_part],
        axis=-1,
    )


def combine_stats(first_stats, second_stats):
    top_first, sum_first, summed_first = first_stats
    top_second, sum_second, summed_second = second_stats
    top_both = jnp.maximum(top_first, top_second)
    scale_first = jnp.exp(top_first - top_both)
    scale_second = jnp.exp(top_second - top_both)
    return (
        top_both,
        sum_first * scale_first + sum_second * scale_second,
        summed_first * scale_first[..., None] + summed_second * scale_second[..., None],
    )


def packed(values, index):
    return jnp.take(values, index, axis=0, mode="fill", fill_value=0)


def routing(home_slot, group_count, local_reqs):
    dest_group = (home_slot // local_reqs).reshape(group_count, local_reqs)
    local_ids = jnp.arange(local_reqs, dtype=jnp.int32)
    earlier = local_ids[None, :] < local_ids[:, None]
    same_dest = dest_group[:, :, None] == dest_group[:, None, :]
    dest_rank = jnp.sum(same_dest & earlier[None], axis=2)
    return (dest_group, dest_rank)


def tree_part(queries, keys_new, values_new, ancestors):
    scores = attn_mult * jnp.einsum(
        "rtkgd,rukd->rtgku", queries, keys_new, preferred_element_type=jnp.float32
    )
    valid_keys = (ancestors > 0.5)[:, :, None, None, :]
    masked = jnp.where(valid_keys, scores, neg_fill)
    top_score = jnp.max(masked, axis=-1)
    weights = jnp.where(valid_keys, jnp.exp(masked - top_score[..., None]), 0.0)
    summed = jnp.einsum(
        "rtgku,rukd->rtgkd",
        weights.astype(jnp.bfloat16),
        values_new,
        preferred_element_type=jnp.float32,
    )
    summed = summed.reshape(summed.shape[:3] + (-1,))
    return (top_score, jnp.sum(weights, axis=-1), summed)


def cache_kernel(lens_ref, start_ref, q_ref, k_ref, v_ref, top_ref, sum_ref, acc_ref):
    slot = pl.program_id(0)
    head_local = top_ref.shape[1]
    cache_local = k_ref.shape[1]
    limit = lens_ref[slot] - start_ref[0]
    valid = lax.broadcasted_iota(jnp.int32, (1, cache_local), 1) < limit
    keys = k_ref[0]
    values = v_ref[0]
    lane = lax.broadcasted_iota(jnp.int32, (1, head_local * HD), 1)
    queries = q_ref[0] * jnp.asarray(attn_mult, q_ref.dtype)
    any_valid = limit > 0
    result = None
    for head in range(head_local):
        mine = (lane >= head * HD) & (lane < (head + 1) * HD)
        own = jnp.where(mine, queries, jnp.zeros((), queries.dtype))
        scores = lax.dot_general(
            own, keys, (((1,), (1,)), ((), ())), preferred_element_type=jnp.float32
        )
        masked = jnp.where(valid, scores, neg_fill)
        top = jnp.max(masked, axis=1, keepdims=True)
        weights = jnp.exp(masked - top)
        summed = jnp.dot(weights.astype(jnp.bfloat16), values, preferred_element_type=jnp.float32)
        total = jnp.where(any_valid, jnp.sum(weights, axis=1, keepdims=True), 0.0)
        top_ref[0, head : head + 1, :] = jnp.broadcast_to(top, (top.shape[0], 128)).T[0:1, :]
        sum_ref[0, head : head + 1, :] = jnp.broadcast_to(total, (total.shape[0], 128)).T[0:1, :]
        result = summed if result is None else jnp.where(mine, summed, result)
    acc_ref[0] = jnp.where(any_valid, result, 0.0)


def cache_merged(slot_queries, k_cache, v_cache, home_lens):
    local_reqs, tree_slots, head_local = slot_queries.shape[:3]
    cache_local = k_cache.shape[1]
    width = head_local * HD
    rows = tree_slots * GROUP
    key_start = (lax.axis_index("ty") * cache_local).astype(jnp.int32).reshape(1)
    spread = slot_queries.transpose(0, 1, 3, 2, 4).reshape(local_reqs, rows, width)
    top, total, summed = pl.pallas_call(
        cache_kernel,
        grid_spec=pltpu.PrefetchScalarGridSpec(
            num_scalar_prefetch=2,
            grid=(local_reqs,),
            in_specs=[
                pl.BlockSpec((1, rows, width), lambda s, lens, start: (s, 0, 0)),
                pl.BlockSpec((1, cache_local, width), lambda s, lens, start: (s, 0, 0)),
                pl.BlockSpec((1, cache_local, width), lambda s, lens, start: (s, 0, 0)),
            ],
            out_specs=[
                pl.BlockSpec((1, head_local, rows), lambda s, lens, start: (s, 0, 0)),
                pl.BlockSpec((1, head_local, rows), lambda s, lens, start: (s, 0, 0)),
                pl.BlockSpec((1, rows, width), lambda s, lens, start: (s, 0, 0)),
            ],
        ),
        out_shape=[
            jax.ShapeDtypeStruct((local_reqs, head_local, rows), jnp.float32),
            jax.ShapeDtypeStruct((local_reqs, head_local, rows), jnp.float32),
            jax.ShapeDtypeStruct((local_reqs, rows, width), jnp.float32),
        ],
        cost_estimate=pl.CostEstimate(
            flops=4 * local_reqs * head_local * rows * cache_local * width,
            transcendentals=local_reqs * head_local * rows * cache_local,
            bytes_accessed=2 * k_cache.size * 2 + spread.size * 2 + local_reqs * rows * width * 4,
        ),
    )(home_lens, key_start, spread, k_cache, v_cache)
    top_all = ty_max(top)
    scale = jnp.exp(top - top_all)
    scale_lanes = jnp.repeat(scale.transpose(0, 2, 1), HD, axis=2)
    count = total.size
    joint = jnp.concatenate(
        [(summed * scale_lanes).reshape(-1, 128), (total * scale).reshape(count // 128, 128)],
        axis=0,
    )
    joint = axis_sum(joint, "ty", True, jnp.bfloat16, jnp.bfloat16, 2)[: joint.shape[0]]
    summed = joint[: summed.size // 128].reshape(summed.shape[0], -1)
    total = joint[summed.size // 128 :].reshape(total.shape[0], -1)
    return (top_all, total, summed)


def ty_max_kernel(x_ref, out_ref, held, send_sem, recv_sem):
    n = lax.axis_size("ty")
    me = lax.axis_index("ty")
    row = lax.axis_index("dp")
    col = lax.axis_index("tx")
    barrier = pltpu.get_barrier_semaphore()
    for step in range(1, n):
        peer = lax.rem(me + step, n)
        pl.semaphore_signal(
            barrier, inc=1, device_id=(row, col, peer), device_id_type=pl.DeviceIdType.MESH
        )
    pl.semaphore_wait(barrier, n - 1)
    copies = []
    for step in range(1, n):
        peer = lax.rem(me + step, n)
        copy = pltpu.make_async_remote_copy(
            src_ref=x_ref,
            dst_ref=held.at[step - 1],
            send_sem=send_sem.at[step - 1],
            recv_sem=recv_sem.at[step - 1],
            device_id=(row, col, peer),
            device_id_type=pl.DeviceIdType.MESH,
        )
        copy.start()
        copies.append(copy)
    for copy in copies:
        copy.wait()
    result = x_ref[...]
    for step in range(1, n):
        result = jnp.maximum(result, held[step - 1])
    out_ref[...] = result


def axis_sum_kernel(axis, gather, x_ref, out_ref, held, gathered, sems):
    n = lax.axis_size(axis)
    me = lax.axis_index(axis)
    chunk = held.shape[1]
    where = {name: lax.axis_index(name) for name in ("dp", "tx", "ty")}

    def device(peer):
        return tuple(peer if name == axis else where[name] for name in ("dp", "tx", "ty"))

    barrier = pltpu.get_barrier_semaphore()
    for step in range(1, n):
        pl.semaphore_signal(
            barrier, inc=1, device_id=device(lax.rem(me + step, n)), device_id_type=pl.DeviceIdType.MESH
        )
    pl.semaphore_wait(barrier, n - 1)
    copies = []
    for step in range(1, n):
        peer = lax.rem(me + step, n)
        copy = pltpu.make_async_remote_copy(
            src_ref=x_ref.at[pl.ds(pl.multiple_of(peer * chunk, 16), chunk)],
            dst_ref=held.at[step - 1],
            send_sem=sems.at[0, step - 1],
            recv_sem=sems.at[1, step - 1],
            device_id=device(peer),
            device_id_type=pl.DeviceIdType.MESH,
        )
        copy.start()
        copies.append(copy)
    for copy in copies:
        copy.wait()
    own = pl.ds(pl.multiple_of(me * chunk, 16), chunk)
    total = x_ref[own].astype(jnp.float32)
    for step in range(1, n):
        total = total + held[step - 1].astype(jnp.float32)
    if not gather:
        out_ref[...] = total.astype(out_ref.dtype)
        return
    out_ref[own] = total.astype(out_ref.dtype)
    copies = []
    for step in range(1, n):
        peer = lax.rem(me + step, n)
        copy = pltpu.make_async_remote_copy(
            src_ref=out_ref.at[own],
            dst_ref=gathered.at[step - 1],
            send_sem=sems.at[2, step - 1],
            recv_sem=sems.at[3, step - 1],
            device_id=device(peer),
            device_id_type=pl.DeviceIdType.MESH,
        )
        copy.start()
        copies.append(copy)
    for copy in copies:
        copy.wait()
    for step in range(1, n):
        source = lax.rem(me - step + n, n)
        out_ref[pl.ds(pl.multiple_of(source * chunk, 16), chunk)] = gathered[step - 1]


def axis_sum(values, axis, gather, send_type, out_type, collective_id):
    n = lax.axis_size(axis)
    flat = values.reshape(-1, 128).astype(send_type)
    rows = flat.shape[0]
    padded = -(-rows // (16 * n)) * 16 * n
    flat = jnp.pad(flat, ((0, padded - rows), (0, 0)))
    chunk = padded // n
    out = pl.pallas_call(
        functools.partial(axis_sum_kernel, axis, gather),
        out_shape=jax.ShapeDtypeStruct((padded if gather else chunk, 128), out_type),
        in_specs=[pl.BlockSpec(memory_space=pltpu.VMEM)],
        out_specs=pl.BlockSpec(memory_space=pltpu.VMEM),
        scratch_shapes=[
            pltpu.VMEM((n - 1, chunk, 128), send_type),
            pltpu.VMEM((n - 1, chunk, 128), out_type),
            pltpu.SemaphoreType.DMA((4, n - 1)),
        ],
        compiler_params=pltpu.CompilerParams(collective_id=collective_id, has_side_effects=True),
    )(flat)
    return out


def dp_exchange_kernel(x_ref, out_ref, held, sems):
    n = lax.axis_size("dp")
    me = lax.axis_index("dp")
    col = lax.axis_index("tx")
    row = lax.axis_index("ty")
    barrier = pltpu.get_barrier_semaphore()
    for step in range(1, n):
        pl.semaphore_signal(
            barrier, inc=1, device_id=(lax.rem(me + step, n), col, row), device_id_type=pl.DeviceIdType.MESH
        )
    pl.semaphore_wait(barrier, n - 1)
    copies = []
    for step in range(1, n):
        peer = lax.rem(me + step, n)
        copy = pltpu.make_async_remote_copy(
            src_ref=x_ref.at[peer],
            dst_ref=held.at[step - 1],
            send_sem=sems.at[0, step - 1],
            recv_sem=sems.at[1, step - 1],
            device_id=(peer, col, row),
            device_id_type=pl.DeviceIdType.MESH,
        )
        copy.start()
        copies.append(copy)
    out_ref[me] = x_ref[me]
    for copy in copies:
        copy.wait()
    for step in range(1, n):
        out_ref[lax.rem(me - step + n, n)] = held[step - 1]


def dp_exchange(blocks, collective_id):
    n = lax.axis_size("dp")
    shape = blocks.shape
    tiles = blocks.reshape(n, -1, 128)
    out = pl.pallas_call(
        dp_exchange_kernel,
        out_shape=jax.ShapeDtypeStruct(tiles.shape, tiles.dtype),
        in_specs=[pl.BlockSpec(memory_space=pltpu.VMEM)],
        out_specs=pl.BlockSpec(memory_space=pltpu.VMEM),
        scratch_shapes=[
            pltpu.VMEM((n - 1,) + tiles.shape[1:], tiles.dtype),
            pltpu.SemaphoreType.DMA((2, n - 1)),
        ],
        compiler_params=pltpu.CompilerParams(collective_id=collective_id, has_side_effects=True),
    )(tiles)
    return out.reshape(shape)


def axis_gather_kernel(axis, x_ref, out_ref, gathered, sems):
    n = lax.axis_size(axis)
    me = lax.axis_index(axis)
    chunk = x_ref.shape[0]
    where = {name: lax.axis_index(name) for name in ("dp", "tx", "ty")}

    def device(peer):
        return tuple(peer if name == axis else where[name] for name in ("dp", "tx", "ty"))

    barrier = pltpu.get_barrier_semaphore()
    for step in range(1, n):
        pl.semaphore_signal(
            barrier, inc=1, device_id=device(lax.rem(me + step, n)), device_id_type=pl.DeviceIdType.MESH
        )
    pl.semaphore_wait(barrier, n - 1)
    copies = []
    for step in range(1, n):
        peer = lax.rem(me + step, n)
        copy = pltpu.make_async_remote_copy(
            src_ref=x_ref,
            dst_ref=gathered.at[step - 1],
            send_sem=sems.at[0, step - 1],
            recv_sem=sems.at[1, step - 1],
            device_id=device(peer),
            device_id_type=pl.DeviceIdType.MESH,
        )
        copy.start()
        copies.append(copy)
    out_ref[pl.ds(pl.multiple_of(me * chunk, 16), chunk)] = x_ref[...]
    for copy in copies:
        copy.wait()
    for step in range(1, n):
        source = lax.rem(me - step + n, n)
        out_ref[pl.ds(pl.multiple_of(source * chunk, 16), chunk)] = gathered[step - 1]


def axis_gather(values, axis, collective_id):
    n = lax.axis_size(axis)
    flat = values.reshape(-1, 128)
    chunk = flat.shape[0]
    out = pl.pallas_call(
        functools.partial(axis_gather_kernel, axis),
        out_shape=jax.ShapeDtypeStruct((n * chunk, 128), flat.dtype),
        in_specs=[pl.BlockSpec(memory_space=pltpu.VMEM)],
        out_specs=pl.BlockSpec(memory_space=pltpu.VMEM),
        scratch_shapes=[
            pltpu.VMEM((n - 1, chunk, 128), flat.dtype),
            pltpu.SemaphoreType.DMA((2, n - 1)),
        ],
        compiler_params=pltpu.CompilerParams(collective_id=collective_id, has_side_effects=True),
    )(flat)
    return out.reshape((n * values.shape[0],) + values.shape[1:])


def ty_max(values):
    n = lax.axis_size("ty")
    flat = values.reshape(-1, 128)
    out = pl.pallas_call(
        ty_max_kernel,
        out_shape=jax.ShapeDtypeStruct(flat.shape, flat.dtype),
        in_specs=[pl.BlockSpec(memory_space=pltpu.VMEM)],
        out_specs=pl.BlockSpec(memory_space=pltpu.VMEM),
        scratch_shapes=[
            pltpu.VMEM((n - 1,) + flat.shape, flat.dtype),
            pltpu.SemaphoreType.DMA((n - 1,)),
            pltpu.SemaphoreType.DMA((n - 1,)),
        ],
        compiler_params=pltpu.CompilerParams(collective_id=0, has_side_effects=True),
    )(flat)
    return out.reshape(values.shape)


def shards(
    hidden_in,
    norm_gain,
    w_qkv,
    w_out,
    k_cache,
    v_cache,
    cache_lens,
    home_slot,
    parents,
    tree_sizes,
    leaf_node,
):
    group_count = lax.axis_size("dp")
    group_index = lax.axis_index("dp")
    local_reqs = k_cache.shape[0]
    tree_slots = parents.shape[1]
    capacity = (local_reqs + group_count - 1) // group_count
    head_local = k_cache.shape[2] // HD
    row_count = hidden_in.shape[0]
    float_in = hidden_in.astype(jnp.float32)
    feature_local = hidden_in.shape[1]
    gain_part = lax.dynamic_slice_in_dim(
        norm_gain, lax.axis_index("ty") * feature_local, feature_local
    )
    scaled = (float_in * gain_part.astype(jnp.float32)).astype(jnp.bfloat16)
    partial_proj = jnp.dot(scaled, w_qkv, preferred_element_type=jnp.float32)
    partial_square = jnp.sum(float_in * float_in, axis=1)
    proj_cols = partial_proj.shape[1]
    n_ty = lax.axis_size("ty")
    chunk_rows = row_count // n_ty
    reqs_mine = local_reqs // n_ty
    square_block = jnp.pad(
        partial_square.reshape(n_ty, 1, chunk_rows),
        ((0, 0), (0, 7), (0, proj_cols - chunk_rows)),
    )
    joint = jnp.concatenate(
        [partial_proj.reshape(n_ty, chunk_rows, proj_cols), square_block], axis=1
    )
    mine = axis_sum(joint, "ty", False, jnp.float32, jnp.float32, 1).reshape(-1, proj_cols)
    square_sum = mine[chunk_rows, :chunk_rows]
    rms_inverse = lax.rsqrt(square_sum / D + norm_eps)
    projected = (mine[:chunk_rows] * rms_inverse[:, None]).reshape(
        reqs_mine, tree_slots, head_local, GROUP + 2, HD
    )
    first_request = group_index * local_reqs
    local_ids = jnp.arange(local_reqs, dtype=jnp.int32)
    request_ids = jnp.arange(home_slot.shape[0], dtype=jnp.int32)
    my_parents = lax.dynamic_slice_in_dim(parents, first_request, local_reqs, 0)
    my_slots = lax.dynamic_slice_in_dim(home_slot, first_request, local_reqs, 0)
    ancestors = jax.vmap(ancestry)(my_parents)
    node_depth = jnp.sum(ancestors > 0.5, axis=2) - 1
    slot_match = my_slots[:, None] == request_ids[None, :]
    my_lens = jnp.sum(jnp.where(slot_match, cache_lens[None, :], 0), axis=1)
    positions = my_lens[:, None] + node_depth
    positions_mine = lax.dynamic_slice_in_dim(
        positions, lax.axis_index("ty") * reqs_mine, reqs_mine, 0
    )
    queries_mine = rotated(
        projected[:, :, :, :GROUP, :], positions_mine[:, :, None, None]
    ).astype(jnp.bfloat16)
    keys_mine = rotated(projected[:, :, :, GROUP, :], positions_mine[:, :, None]).astype(
        jnp.bfloat16
    )
    values_mine = projected[:, :, :, GROUP + 1, :].astype(jnp.bfloat16)
    piece = jnp.concatenate(
        [
            queries_mine.reshape(chunk_rows, -1),
            keys_mine.reshape(chunk_rows, -1),
            values_mine.reshape(chunk_rows, -1),
        ],
        axis=1,
    )
    everything = axis_gather(piece, "ty", 6)
    query_cols = head_local * GROUP * HD
    queries = everything[:, :query_cols].reshape(local_reqs, tree_slots, head_local, GROUP, HD)
    keys_new = everything[:, query_cols : query_cols + head_local * HD].reshape(
        local_reqs, tree_slots, head_local, HD
    )
    values_new = everything[:, query_cols + head_local * HD :].reshape(
        local_reqs, tree_slots, head_local, HD
    )
    dest_group, dest_rank = routing(home_slot, group_count, local_reqs)
    send_pos = lax.dynamic_index_in_dim(
        dest_group, group_index, 0, keepdims=False
    ) * capacity + lax.dynamic_index_in_dim(dest_rank, group_index, 0, keepdims=False)
    buffer_ids = jnp.arange(group_count * capacity, dtype=jnp.int32)
    send_hit = send_pos[None, :] == buffer_ids[:, None]
    send_index = jnp.where(
        jnp.any(send_hit, axis=1),
        jnp.sum(jnp.where(send_hit, local_ids[None, :], 0), axis=1),
        local_reqs,
    )
    target_slots = first_request + local_ids
    owner_match = home_slot[None, :] == target_slots[:, None]
    owner_request = jnp.sum(jnp.where(owner_match, request_ids[None, :], 0), axis=1)
    owner_rank = jnp.sum(jnp.where(owner_match, dest_rank.reshape(-1)[None, :], 0), axis=1)
    recv_index = owner_request // local_reqs * capacity + owner_rank
    back_hit = recv_index[None, :] == buffer_ids[:, None]
    back_index = jnp.where(
        jnp.any(back_hit, axis=1),
        jnp.sum(jnp.where(back_hit, local_ids[None, :], 0), axis=1),
        local_reqs,
    )
    home_lens = lax.dynamic_slice_in_dim(cache_lens, first_request, local_reqs, 0)
    arrived = dp_exchange(packed(queries.reshape(local_reqs, -1), send_index), 4)
    slot_queries = packed(arrived, recv_index).reshape(queries.shape)
    top_score, weight_sum, summed = cache_merged(slot_queries, k_cache, v_cache, home_lens)
    value_width = summed.shape[1]
    sum_width = weight_sum.shape[1]
    log_flat = top_score.reshape(local_reqs, -1)
    log_high = lax.reduce_precision(log_flat, exponent_bits=8, mantissa_bits=7)
    log_rest = log_flat - log_high
    log_mid = lax.reduce_precision(log_rest, exponent_bits=8, mantissa_bits=7)
    log_low = log_rest - log_mid
    payload = jnp.concatenate(
        [
            summed,
            weight_sum,
            log_high.astype(jnp.bfloat16),
            log_mid.astype(jnp.bfloat16),
            log_low.astype(jnp.bfloat16),
        ],
        axis=1,
    )
    back = lax.all_to_all(
        packed(payload, back_index), "dp", split_axis=0, concat_axis=0, tiled=True
    )
    back = packed(back, send_pos).astype(jnp.float32)
    log_width = log_flat.shape[1]
    cache_values = back[:, :value_width].reshape(local_reqs, tree_slots, GROUP, head_local * HD)
    cache_sum = (
        back[:, value_width : value_width + sum_width]
        .reshape(local_reqs, head_local, tree_slots, GROUP)
        .transpose(0, 2, 3, 1)
    )
    logs = value_width + sum_width
    cache_top = (
        (
            back[:, logs : logs + log_width]
            + back[:, logs + log_width : logs + 2 * log_width]
            + back[:, logs + 2 * log_width :]
        )
        .reshape(local_reqs, head_local, tree_slots, GROUP)
        .transpose(0, 2, 3, 1)
    )
    tree_top, tree_sum, tree_summed = tree_part(queries, keys_new, values_new, ancestors)
    top_all = jnp.maximum(cache_top, tree_top)
    scale_cache = jnp.exp(cache_top - top_all)
    scale_tree = jnp.exp(tree_top - top_all)
    sum_all = cache_sum * scale_cache + tree_sum * scale_tree
    summed_all = cache_values * jnp.repeat(scale_cache, HD, axis=-1) + tree_summed * jnp.repeat(
        scale_tree, HD, axis=-1
    )
    attention = (summed_all / jnp.repeat(sum_all, HD, axis=-1)).astype(jnp.bfloat16)
    attention_rows = attention.reshape(row_count, -1)
    w_out = (
        w_out.reshape(head_local, GROUP, HD, -1)
        .transpose(1, 0, 2, 3)
        .reshape(head_local * GROUP * HD, -1)
    )
    rows_mine = row_count // lax.axis_size("tx")
    mixed_sum = axis_sum(
        jnp.dot(attention_rows, w_out, preferred_element_type=jnp.float32),
        "tx",
        False,
        jnp.bfloat16,
        jnp.float32,
        3,
    ).reshape(row_count // lax.axis_size("tx"), -1)
    row_start = lax.axis_index("tx") * rows_mine
    residual = lax.dynamic_slice_in_dim(float_in, row_start, rows_mine, 0)
    row_ids = row_start + jnp.arange(rows_mine, dtype=jnp.int32)
    request_of = row_ids // tree_slots
    slot_of = row_ids % tree_slots
    size_of = jnp.sum(
        jnp.where(request_of[:, None] == local_ids[None, :], tree_sizes[None, :], 0), axis=1
    )
    layer_out = jnp.where((slot_of < size_of)[:, None], residual + mixed_sum, 0.0).astype(
        jnp.bfloat16
    )
    node_ids = jnp.arange(tree_slots, dtype=jnp.int32)
    leaf_hit = (leaf_node[:, None] == node_ids[None, :]).astype(jnp.float32)
    path_nodes = jnp.einsum("rt,rtu->ru", leaf_hit, ancestors)
    depth_hit = node_depth[:, None, :] == jnp.arange(ACC, dtype=jnp.int32)[None, :, None]
    chooser = jnp.where(depth_hit, path_nodes[:, None, :], 0.0).astype(jnp.bfloat16)
    stacked = jnp.stack(
        [
            keys_new.reshape(local_reqs, tree_slots, -1),
            values_new.reshape(local_reqs, tree_slots, -1),
        ],
        axis=2,
    )
    accepted_kv = jnp.einsum(
        "rsu,ruwc->rswc", chooser, stacked, preferred_element_type=jnp.float32
    ).astype(jnp.bfloat16)
    return (layer_out, accepted_kv)


def solution(mesh):
    return jax.shard_map(
        shards,
        mesh=mesh,
        in_specs=(
            P("dp", "ty"),
            P(),
            P("ty", "tx"),
            P("tx", "ty"),
            P("dp", "ty", "tx"),
            P("dp", "ty", "tx"),
            P(),
            P(),
            P(),
            P("dp"),
            P("dp"),
        ),
        out_specs=(P(("dp", "tx"), "ty"), P("dp", None, None, "tx")),
        check_vma=False,
    )
```

```python
import functools

import jax
import jax.numpy as jnp
from jax import lax
from jax.experimental import pallas as pl
from jax.experimental.pallas import tpu as pltpu
from jax.sharding import PartitionSpec as P

D = 2048
HD = 64
GROUP = 4
ACC = 8


rope_base = 10000000.0
attn_mult = 0.015625
norm_eps = 1e-05
neg_fill = -1e30


def joined(value, axis, join):
    pieces = jax.tree.map(lambda part: lax.all_gather(part, axis), value)
    head = jax.tree.map(lambda part: part[0], pieces)
    tail = jax.tree.map(lambda part: part[1:], pieces)
    so_far, _ = lax.scan(lambda so_far, slab: (join(so_far, slab), None), head, tail)
    return so_far


def ancestry(parent_rows):
    node_count = parent_rows.shape[-1]
    node_ids = jnp.arange(node_count, dtype=jnp.int32)
    linked = (node_ids[None, :] == parent_rows[:, None]) | (node_ids[None, :] == node_ids[:, None])
    reachable = linked.astype(jnp.float32)
    for repeat in range(max(1, (node_count - 1).bit_length())):
        reachable = jnp.minimum(jnp.dot(reachable, reachable, precision=lax.Precision.HIGHEST), 1.0)
    return reachable


def rotated(values, positions):
    half_size = values.shape[-1] // 2
    frequency = rope_base ** (-2.0 * jnp.arange(half_size, dtype=jnp.float32) / values.shape[-1])
    angles = positions.astype(jnp.float32)[..., None] * frequency
    cosine = jnp.cos(angles)
    sine_part = jnp.sin(angles)
    front_half = values[..., :half_size]
    back_half = values[..., half_size:]
    return jnp.concatenate(
        [front_half * cosine - back_half * sine_part, back_half * cosine + front_half * sine_part],
        axis=-1,
    )


def combine_stats(first_stats, second_stats):
    top_first, sum_first, summed_first = first_stats
    top_second, sum_second, summed_second = second_stats
    top_both = jnp.maximum(top_first, top_second)
    scale_first = jnp.exp(top_first - top_both)
    scale_second = jnp.exp(top_second - top_both)
    return (
        top_both,
        sum_first * scale_first + sum_second * scale_second,
        summed_first * scale_first[..., None] + summed_second * scale_second[..., None],
    )


def packed(values, index):
    chooser = (index[:, None] == jnp.arange(values.shape[0], dtype=index.dtype)[None, :]).astype(
        values.dtype
    )
    return jnp.dot(chooser, values, preferred_element_type=jnp.float32).astype(values.dtype)


def routing(home_slot, group_count, local_reqs):
    dest_group = (home_slot // local_reqs).reshape(group_count, local_reqs)
    local_ids = jnp.arange(local_reqs, dtype=jnp.int32)
    earlier = local_ids[None, :] < local_ids[:, None]
    same_dest = dest_group[:, :, None] == dest_group[:, None, :]
    dest_rank = jnp.sum(same_dest & earlier[None], axis=2)
    return (dest_group, dest_rank)


def tree_part(queries, keys_new, values_new, ancestors):
    scores = attn_mult * jnp.einsum(
        "rtkgd,rukd->rtkgu", queries, keys_new, preferred_element_type=jnp.float32
    )
    valid_keys = (ancestors > 0.5)[:, :, None, None, :]
    masked = jnp.where(valid_keys, scores, neg_fill)
    top_score = jnp.max(masked, axis=-1)
    weights = jnp.where(valid_keys, jnp.exp(masked - top_score[..., None]), 0.0)
    summed = jnp.einsum(
        "rtkgu,rukd->rtkgd",
        weights.astype(jnp.bfloat16),
        values_new,
        preferred_element_type=jnp.float32,
    )
    return (top_score, jnp.sum(weights, axis=-1), summed)


def cache_kernel(lens_ref, start_ref, q_ref, k_ref, v_ref, top_ref, sum_ref, acc_ref):
    slot = pl.program_id(0)
    head_local = top_ref.shape[1]
    cache_local = k_ref.shape[1]
    limit = lens_ref[slot] - start_ref[0]
    valid = lax.broadcasted_iota(jnp.int32, (1, cache_local), 1) < limit
    keys = k_ref[0]
    values = v_ref[0]
    lane = lax.broadcasted_iota(jnp.int32, (1, head_local * HD), 1)
    queries = q_ref[0] * jnp.asarray(attn_mult, q_ref.dtype)
    any_valid = limit > 0
    result = None
    for head in range(head_local):
        mine = (lane >= head * HD) & (lane < (head + 1) * HD)
        own = jnp.where(mine, queries, jnp.zeros((), queries.dtype))
        scores = lax.dot_general(
            own, keys, (((1,), (1,)), ((), ())), preferred_element_type=jnp.float32
        )
        masked = jnp.where(valid, scores, neg_fill)
        top = jnp.max(masked, axis=1, keepdims=True)
        weights = jnp.exp(masked - top)
        summed = jnp.dot(weights.astype(jnp.bfloat16), values, preferred_element_type=jnp.float32)
        total = jnp.where(any_valid, jnp.sum(weights, axis=1, keepdims=True), 0.0)
        top_ref[0, head : head + 1, :] = jnp.broadcast_to(top, (top.shape[0], 128)).T[0:1, :]
        sum_ref[0, head : head + 1, :] = jnp.broadcast_to(total, (total.shape[0], 128)).T[0:1, :]
        result = summed if result is None else jnp.where(mine, summed, result)
    acc_ref[0] = jnp.where(any_valid, result, 0.0)


def cache_merged(slot_queries, k_cache, v_cache, home_lens):
    local_reqs, tree_slots, head_local = slot_queries.shape[:3]
    cache_local = k_cache.shape[1]
    width = head_local * HD
    rows = tree_slots * GROUP
    key_start = (lax.axis_index("ty") * cache_local).astype(jnp.int32).reshape(1)
    spread = slot_queries.transpose(0, 1, 3, 2, 4).reshape(local_reqs, rows, width)
    top, total, summed = pl.pallas_call(
        cache_kernel,
        grid_spec=pltpu.PrefetchScalarGridSpec(
            num_scalar_prefetch=2,
            grid=(local_reqs,),
            in_specs=[
                pl.BlockSpec((1, rows, width), lambda s, lens, start: (s, 0, 0)),
                pl.BlockSpec((1, cache_local, width), lambda s, lens, start: (s, 0, 0)),
                pl.BlockSpec((1, cache_local, width), lambda s, lens, start: (s, 0, 0)),
            ],
            out_specs=[
                pl.BlockSpec((1, head_local, rows), lambda s, lens, start: (s, 0, 0)),
                pl.BlockSpec((1, head_local, rows), lambda s, lens, start: (s, 0, 0)),
                pl.BlockSpec((1, rows, width), lambda s, lens, start: (s, 0, 0)),
            ],
        ),
        out_shape=[
            jax.ShapeDtypeStruct((local_reqs, head_local, rows), jnp.float32),
            jax.ShapeDtypeStruct((local_reqs, head_local, rows), jnp.float32),
            jax.ShapeDtypeStruct((local_reqs, rows, width), jnp.float32),
        ],
        cost_estimate=pl.CostEstimate(
            flops=4 * local_reqs * head_local * rows * cache_local * width,
            transcendentals=local_reqs * head_local * rows * cache_local,
            bytes_accessed=2 * k_cache.size * 2 + spread.size * 2 + local_reqs * rows * width * 4,
        ),
    )(home_lens, key_start, spread, k_cache, v_cache)
    top_all = ty_max(top)
    scale = jnp.exp(top - top_all)
    scale_lanes = jnp.repeat(scale.transpose(0, 2, 1), HD, axis=2)
    count = total.size
    joint = jnp.concatenate(
        [(summed * scale_lanes).reshape(-1, 128), (total * scale).reshape(count // 128, 128)],
        axis=0,
    )
    joint = axis_sum(joint, "ty", True, jnp.bfloat16, jnp.bfloat16, 2)[: joint.shape[0]]
    summed = joint[: summed.size // 128].reshape(summed.shape[0], -1)
    total = joint[summed.size // 128 :].reshape(total.shape[0], -1)
    return (top_all, total, summed)


def ty_max_kernel(x_ref, out_ref, held, send_sem, recv_sem):
    n = lax.axis_size("ty")
    me = lax.axis_index("ty")
    row = lax.axis_index("dp")
    col = lax.axis_index("tx")
    barrier = pltpu.get_barrier_semaphore()
    for step in range(1, n):
        peer = lax.rem(me + step, n)
        pl.semaphore_signal(
            barrier, inc=1, device_id=(row, col, peer), device_id_type=pl.DeviceIdType.MESH
        )
    pl.semaphore_wait(barrier, n - 1)
    copies = []
    for step in range(1, n):
        peer = lax.rem(me + step, n)
        copy = pltpu.make_async_remote_copy(
            src_ref=x_ref,
            dst_ref=held.at[step - 1],
            send_sem=send_sem.at[step - 1],
            recv_sem=recv_sem.at[step - 1],
            device_id=(row, col, peer),
            device_id_type=pl.DeviceIdType.MESH,
        )
        copy.start()
        copies.append(copy)
    for copy in copies:
        copy.wait()
    result = x_ref[...]
    for step in range(1, n):
        result = jnp.maximum(result, held[step - 1])
    out_ref[...] = result


def axis_sum_kernel(axis, gather, x_ref, out_ref, held, gathered, sems):
    n = lax.axis_size(axis)
    me = lax.axis_index(axis)
    chunk = held.shape[1]
    where = {name: lax.axis_index(name) for name in ("dp", "tx", "ty")}

    def device(peer):
        return tuple(peer if name == axis else where[name] for name in ("dp", "tx", "ty"))

    barrier = pltpu.get_barrier_semaphore()
    for step in range(1, n):
        pl.semaphore_signal(
            barrier, inc=1, device_id=device(lax.rem(me + step, n)), device_id_type=pl.DeviceIdType.MESH
        )
    pl.semaphore_wait(barrier, n - 1)
    copies = []
    for step in range(1, n):
        peer = lax.rem(me + step, n)
        copy = pltpu.make_async_remote_copy(
            src_ref=x_ref.at[pl.ds(pl.multiple_of(peer * chunk, 16), chunk)],
            dst_ref=held.at[step - 1],
            send_sem=sems.at[0, step - 1],
            recv_sem=sems.at[1, step - 1],
            device_id=device(peer),
            device_id_type=pl.DeviceIdType.MESH,
        )
        copy.start()
        copies.append(copy)
    for copy in copies:
        copy.wait()
    own = pl.ds(pl.multiple_of(me * chunk, 16), chunk)
    total = x_ref[own].astype(jnp.float32)
    for step in range(1, n):
        total = total + held[step - 1].astype(jnp.float32)
    if not gather:
        out_ref[...] = total.astype(out_ref.dtype)
        return
    out_ref[own] = total.astype(out_ref.dtype)
    copies = []
    for step in range(1, n):
        peer = lax.rem(me + step, n)
        copy = pltpu.make_async_remote_copy(
            src_ref=out_ref.at[own],
            dst_ref=gathered.at[step - 1],
            send_sem=sems.at[2, step - 1],
            recv_sem=sems.at[3, step - 1],
            device_id=device(peer),
            device_id_type=pl.DeviceIdType.MESH,
        )
        copy.start()
        copies.append(copy)
    for copy in copies:
        copy.wait()
    for step in range(1, n):
        source = lax.rem(me - step + n, n)
        out_ref[pl.ds(pl.multiple_of(source * chunk, 16), chunk)] = gathered[step - 1]


def axis_sum(values, axis, gather, send_type, out_type, collective_id):
    n = lax.axis_size(axis)
    flat = values.reshape(-1, 128).astype(send_type)
    rows = flat.shape[0]
    padded = -(-rows // (16 * n)) * 16 * n
    flat = jnp.pad(flat, ((0, padded - rows), (0, 0)))
    chunk = padded // n
    out = pl.pallas_call(
        functools.partial(axis_sum_kernel, axis, gather),
        out_shape=jax.ShapeDtypeStruct((padded if gather else chunk, 128), out_type),
        in_specs=[pl.BlockSpec(memory_space=pltpu.VMEM)],
        out_specs=pl.BlockSpec(memory_space=pltpu.VMEM),
        scratch_shapes=[
            pltpu.VMEM((n - 1, chunk, 128), send_type),
            pltpu.VMEM((n - 1, chunk, 128), out_type),
            pltpu.SemaphoreType.DMA((4, n - 1)),
        ],
        compiler_params=pltpu.CompilerParams(collective_id=collective_id, has_side_effects=True),
    )(flat)
    return out


def dp_exchange_kernel(x_ref, out_ref, held, sems):
    n = lax.axis_size("dp")
    me = lax.axis_index("dp")
    col = lax.axis_index("tx")
    row = lax.axis_index("ty")
    barrier = pltpu.get_barrier_semaphore()
    for step in range(1, n):
        pl.semaphore_signal(
            barrier, inc=1, device_id=(lax.rem(me + step, n), col, row), device_id_type=pl.DeviceIdType.MESH
        )
    pl.semaphore_wait(barrier, n - 1)
    copies = []
    for step in range(1, n):
        peer = lax.rem(me + step, n)
        copy = pltpu.make_async_remote_copy(
            src_ref=x_ref.at[peer],
            dst_ref=held.at[step - 1],
            send_sem=sems.at[0, step - 1],
            recv_sem=sems.at[1, step - 1],
            device_id=(peer, col, row),
            device_id_type=pl.DeviceIdType.MESH,
        )
        copy.start()
        copies.append(copy)
    out_ref[me] = x_ref[me]
    for copy in copies:
        copy.wait()
    for step in range(1, n):
        out_ref[lax.rem(me - step + n, n)] = held[step - 1]


def dp_exchange(blocks, collective_id):
    n = lax.axis_size("dp")
    shape = blocks.shape
    tiles = blocks.reshape(n, -1, 128)
    out = pl.pallas_call(
        dp_exchange_kernel,
        out_shape=jax.ShapeDtypeStruct(tiles.shape, tiles.dtype),
        in_specs=[pl.BlockSpec(memory_space=pltpu.VMEM)],
        out_specs=pl.BlockSpec(memory_space=pltpu.VMEM),
        scratch_shapes=[
            pltpu.VMEM((n - 1,) + tiles.shape[1:], tiles.dtype),
            pltpu.SemaphoreType.DMA((2, n - 1)),
        ],
        compiler_params=pltpu.CompilerParams(collective_id=collective_id, has_side_effects=True),
    )(tiles)
    return out.reshape(shape)


def axis_gather_kernel(axis, x_ref, out_ref, gathered, sems):
    n = lax.axis_size(axis)
    me = lax.axis_index(axis)
    chunk = x_ref.shape[0]
    where = {name: lax.axis_index(name) for name in ("dp", "tx", "ty")}

    def device(peer):
        return tuple(peer if name == axis else where[name] for name in ("dp", "tx", "ty"))

    barrier = pltpu.get_barrier_semaphore()
    for step in range(1, n):
        pl.semaphore_signal(
            barrier, inc=1, device_id=device(lax.rem(me + step, n)), device_id_type=pl.DeviceIdType.MESH
        )
    pl.semaphore_wait(barrier, n - 1)
    copies = []
    for step in range(1, n):
        peer = lax.rem(me + step, n)
        copy = pltpu.make_async_remote_copy(
            src_ref=x_ref,
            dst_ref=gathered.at[step - 1],
            send_sem=sems.at[0, step - 1],
            recv_sem=sems.at[1, step - 1],
            device_id=device(peer),
            device_id_type=pl.DeviceIdType.MESH,
        )
        copy.start()
        copies.append(copy)
    out_ref[pl.ds(pl.multiple_of(me * chunk, 16), chunk)] = x_ref[...]
    for copy in copies:
        copy.wait()
    for step in range(1, n):
        source = lax.rem(me - step + n, n)
        out_ref[pl.ds(pl.multiple_of(source * chunk, 16), chunk)] = gathered[step - 1]


def axis_gather(values, axis, collective_id):
    n = lax.axis_size(axis)
    flat = values.reshape(-1, 128)
    chunk = flat.shape[0]
    out = pl.pallas_call(
        functools.partial(axis_gather_kernel, axis),
        out_shape=jax.ShapeDtypeStruct((n * chunk, 128), flat.dtype),
        in_specs=[pl.BlockSpec(memory_space=pltpu.VMEM)],
        out_specs=pl.BlockSpec(memory_space=pltpu.VMEM),
        scratch_shapes=[
            pltpu.VMEM((n - 1, chunk, 128), flat.dtype),
            pltpu.SemaphoreType.DMA((2, n - 1)),
        ],
        compiler_params=pltpu.CompilerParams(collective_id=collective_id, has_side_effects=True),
    )(flat)
    return out.reshape((n * values.shape[0],) + values.shape[1:])


def ty_max(values):
    n = lax.axis_size("ty")
    flat = values.reshape(-1, 128)
    out = pl.pallas_call(
        ty_max_kernel,
        out_shape=jax.ShapeDtypeStruct(flat.shape, flat.dtype),
        in_specs=[pl.BlockSpec(memory_space=pltpu.VMEM)],
        out_specs=pl.BlockSpec(memory_space=pltpu.VMEM),
        scratch_shapes=[
            pltpu.VMEM((n - 1,) + flat.shape, flat.dtype),
            pltpu.SemaphoreType.DMA((n - 1,)),
            pltpu.SemaphoreType.DMA((n - 1,)),
        ],
        compiler_params=pltpu.CompilerParams(collective_id=0, has_side_effects=True),
    )(flat)
    return out.reshape(values.shape)


def shards(
    hidden_in,
    norm_gain,
    w_qkv,
    w_out,
    k_cache,
    v_cache,
    cache_lens,
    home_slot,
    parents,
    tree_sizes,
    leaf_node,
):
    group_count = lax.axis_size("dp")
    group_index = lax.axis_index("dp")
    local_reqs = k_cache.shape[0]
    tree_slots = parents.shape[1]
    capacity = (local_reqs + group_count - 1) // group_count
    head_local = k_cache.shape[2] // HD
    row_count = hidden_in.shape[0]
    float_in = hidden_in.astype(jnp.float32)
    feature_local = hidden_in.shape[1]
    gain_part = lax.dynamic_slice_in_dim(
        norm_gain, lax.axis_index("ty") * feature_local, feature_local
    )
    scaled = (float_in * gain_part.astype(jnp.float32)).astype(jnp.bfloat16)
    partial_proj = jnp.dot(scaled, w_qkv, preferred_element_type=jnp.float32)
    partial_square = jnp.sum(float_in * float_in, axis=1)
    proj_cols = partial_proj.shape[1]
    n_ty = lax.axis_size("ty")
    chunk_rows = row_count // n_ty
    reqs_mine = local_reqs // n_ty
    square_block = jnp.pad(
        partial_square.reshape(n_ty, 1, chunk_rows),
        ((0, 0), (0, 7), (0, proj_cols - chunk_rows)),
    )
    joint = jnp.concatenate(
        [partial_proj.reshape(n_ty, chunk_rows, proj_cols), square_block], axis=1
    )
    mine = axis_sum(joint, "ty", False, jnp.float32, jnp.float32, 1).reshape(-1, proj_cols)
    square_sum = mine[chunk_rows, :chunk_rows]
    rms_inverse = lax.rsqrt(square_sum / D + norm_eps)
    projected = (mine[:chunk_rows] * rms_inverse[:, None]).reshape(
        reqs_mine, tree_slots, head_local, GROUP + 2, HD
    )
    first_request = group_index * local_reqs
    local_ids = jnp.arange(local_reqs, dtype=jnp.int32)
    request_ids = jnp.arange(home_slot.shape[0], dtype=jnp.int32)
    my_parents = lax.dynamic_slice_in_dim(parents, first_request, local_reqs, 0)
    my_slots = lax.dynamic_slice_in_dim(home_slot, first_request, local_reqs, 0)
    ancestors = jax.vmap(ancestry)(my_parents)
    node_depth = jnp.sum(ancestors > 0.5, axis=2) - 1
    slot_match = my_slots[:, None] == request_ids[None, :]
    my_lens = jnp.sum(jnp.where(slot_match, cache_lens[None, :], 0), axis=1)
    positions = my_lens[:, None] + node_depth
    positions_mine = lax.dynamic_slice_in_dim(
        positions, lax.axis_index("ty") * reqs_mine, reqs_mine, 0
    )
    queries_mine = rotated(
        projected[:, :, :, :GROUP, :], positions_mine[:, :, None, None]
    ).astype(jnp.bfloat16)
    keys_mine = rotated(projected[:, :, :, GROUP, :], positions_mine[:, :, None]).astype(
        jnp.bfloat16
    )
    values_mine = projected[:, :, :, GROUP + 1, :].astype(jnp.bfloat16)
    piece = jnp.concatenate(
        [
            queries_mine.reshape(chunk_rows, -1),
            keys_mine.reshape(chunk_rows, -1),
            values_mine.reshape(chunk_rows, -1),
        ],
        axis=1,
    )
    everything = axis_gather(piece, "ty", 6)
    query_cols = head_local * GROUP * HD
    queries = everything[:, :query_cols].reshape(local_reqs, tree_slots, head_local, GROUP, HD)
    keys_new = everything[:, query_cols : query_cols + head_local * HD].reshape(
        local_reqs, tree_slots, head_local, HD
    )
    values_new = everything[:, query_cols + head_local * HD :].reshape(
        local_reqs, tree_slots, head_local, HD
    )
    dest_group, dest_rank = routing(home_slot, group_count, local_reqs)
    send_pos = lax.dynamic_index_in_dim(
        dest_group, group_index, 0, keepdims=False
    ) * capacity + lax.dynamic_index_in_dim(dest_rank, group_index, 0, keepdims=False)
    buffer_ids = jnp.arange(group_count * capacity, dtype=jnp.int32)
    send_hit = send_pos[None, :] == buffer_ids[:, None]
    send_index = jnp.where(
        jnp.any(send_hit, axis=1),
        jnp.sum(jnp.where(send_hit, local_ids[None, :], 0), axis=1),
        local_reqs,
    )
    target_slots = first_request + local_ids
    owner_match = home_slot[None, :] == target_slots[:, None]
    owner_request = jnp.sum(jnp.where(owner_match, request_ids[None, :], 0), axis=1)
    owner_rank = jnp.sum(jnp.where(owner_match, dest_rank.reshape(-1)[None, :], 0), axis=1)
    recv_index = owner_request // local_reqs * capacity + owner_rank
    back_hit = recv_index[None, :] == buffer_ids[:, None]
    back_index = jnp.where(
        jnp.any(back_hit, axis=1),
        jnp.sum(jnp.where(back_hit, local_ids[None, :], 0), axis=1),
        local_reqs,
    )
    home_lens = lax.dynamic_slice_in_dim(cache_lens, first_request, local_reqs, 0)
    arrived = dp_exchange(packed(queries.reshape(local_reqs, -1), send_index), 4)
    slot_queries = packed(arrived, recv_index).reshape(queries.shape)
    top_score, weight_sum, summed = cache_merged(slot_queries, k_cache, v_cache, home_lens)
    value_width = summed.shape[1]
    sum_width = weight_sum.shape[1]
    log_flat = top_score.reshape(local_reqs, -1)
    log_high = lax.reduce_precision(log_flat, exponent_bits=8, mantissa_bits=7)
    log_rest = log_flat - log_high
    log_mid = lax.reduce_precision(log_rest, exponent_bits=8, mantissa_bits=7)
    log_low = log_rest - log_mid
    payload = jnp.concatenate(
        [
            summed,
            weight_sum,
            log_high.astype(jnp.bfloat16),
            log_mid.astype(jnp.bfloat16),
            log_low.astype(jnp.bfloat16),
        ],
        axis=1,
    )
    outgoing = packed(payload, back_index)
    back = lax.all_to_all(
        outgoing.reshape(outgoing.shape[0], -1, 128), "dp", split_axis=0, concat_axis=0, tiled=True
    ).reshape(outgoing.shape)
    back = packed(back, send_pos).astype(jnp.float32)
    log_width = log_flat.shape[1]
    cache_values = (
        back[:, :value_width]
        .reshape(local_reqs, tree_slots, GROUP, head_local, HD)
        .transpose(0, 1, 3, 2, 4)
    )
    cache_sum = (
        back[:, value_width : value_width + sum_width]
        .reshape(local_reqs, head_local, tree_slots, GROUP)
        .transpose(0, 2, 1, 3)
    )
    logs = value_width + sum_width
    cache_top = (
        (
            back[:, logs : logs + log_width]
            + back[:, logs + log_width : logs + 2 * log_width]
            + back[:, logs + 2 * log_width :]
        )
        .reshape(local_reqs, head_local, tree_slots, GROUP)
        .transpose(0, 2, 1, 3)
    )
    tree_stats = tree_part(queries, keys_new, values_new, ancestors)
    top_all, sum_all, summed_all = combine_stats(
        (cache_top, cache_sum, cache_values), tree_stats
    )
    attention = (summed_all / sum_all[..., None]).astype(jnp.bfloat16)
    attention_rows = attention.reshape(row_count, -1)
    rows_mine = row_count // lax.axis_size("tx")
    mixed_sum = axis_sum(
        jnp.dot(attention_rows, w_out, preferred_element_type=jnp.float32),
        "tx",
        False,
        jnp.bfloat16,
        jnp.float32,
        3,
    ).reshape(row_count // lax.axis_size("tx"), -1)
    row_start = lax.axis_index("tx") * rows_mine
    residual = lax.dynamic_slice_in_dim(float_in, row_start, rows_mine, 0)
    row_ids = row_start + jnp.arange(rows_mine, dtype=jnp.int32)
    request_of = row_ids // tree_slots
    slot_of = row_ids % tree_slots
    size_of = jnp.sum(
        jnp.where(request_of[:, None] == local_ids[None, :], tree_sizes[None, :], 0), axis=1
    )
    layer_out = jnp.where((slot_of < size_of)[:, None], residual + mixed_sum, 0.0).astype(
        jnp.bfloat16
    )
    node_ids = jnp.arange(tree_slots, dtype=jnp.int32)
    leaf_hit = (leaf_node[:, None] == node_ids[None, :]).astype(jnp.float32)
    path_nodes = jnp.einsum("rt,rtu->ru", leaf_hit, ancestors)
    depth_hit = node_depth[:, None, :] == jnp.arange(ACC, dtype=jnp.int32)[None, :, None]
    chooser = jnp.where(depth_hit, path_nodes[:, None, :], 0.0).astype(jnp.bfloat16)
    stacked = jnp.stack(
        [
            keys_new.reshape(local_reqs, tree_slots, -1),
            values_new.reshape(local_reqs, tree_slots, -1),
        ],
        axis=2,
    )
    accepted_kv = jnp.einsum(
        "rsu,ruwc->rswc", chooser, stacked, preferred_element_type=jnp.float32
    ).astype(jnp.bfloat16)
    return (layer_out, accepted_kv)


def solution(mesh):
    return jax.shard_map(
        shards,
        mesh=mesh,
        in_specs=(
            P("dp", "ty"),
            P(),
            P("ty", "tx"),
            P("tx", "ty"),
            P("dp", "ty", "tx"),
            P("dp", "ty", "tx"),
            P(),
            P(),
            P(),
            P("dp"),
            P("dp"),
        ),
        out_specs=(P(("dp", "tx"), "ty"), P("dp", None, None, "tx")),
        check_vma=False,
    )
```

```python
import functools

import jax
import jax.numpy as jnp
from jax import lax
from jax.experimental import pallas as pl
from jax.experimental.pallas import tpu as pltpu
from jax.sharding import PartitionSpec as P

D = 2048
HD = 64
GROUP = 4
ACC = 8


rope_base = 10000000.0
attn_mult = 0.015625
norm_eps = 1e-05
neg_fill = -1e30


def joined(value, axis, join):
    pieces = jax.tree.map(lambda part: lax.all_gather(part, axis), value)
    head = jax.tree.map(lambda part: part[0], pieces)
    tail = jax.tree.map(lambda part: part[1:], pieces)
    so_far, _ = lax.scan(lambda so_far, slab: (join(so_far, slab), None), head, tail)
    return so_far


def ancestry(parent_rows):
    node_count = parent_rows.shape[-1]
    node_ids = jnp.arange(node_count, dtype=jnp.int32)
    linked = (node_ids[None, :] == parent_rows[:, None]) | (node_ids[None, :] == node_ids[:, None])
    reachable = linked.astype(jnp.float32)
    for repeat in range(max(1, (node_count - 1).bit_length())):
        reachable = jnp.minimum(jnp.dot(reachable, reachable, precision=lax.Precision.HIGHEST), 1.0)
    return reachable


def rotated(values, positions):
    half_size = values.shape[-1] // 2
    frequency = rope_base ** (-2.0 * jnp.arange(half_size, dtype=jnp.float32) / values.shape[-1])
    angles = positions.astype(jnp.float32)[..., None] * frequency
    cosine = jnp.cos(angles)
    sine_part = jnp.sin(angles)
    front_half = values[..., :half_size]
    back_half = values[..., half_size:]
    return jnp.concatenate(
        [front_half * cosine - back_half * sine_part, back_half * cosine + front_half * sine_part],
        axis=-1,
    )


def combine_stats(first_stats, second_stats):
    top_first, sum_first, summed_first = first_stats
    top_second, sum_second, summed_second = second_stats
    top_both = jnp.maximum(top_first, top_second)
    scale_first = jnp.exp(top_first - top_both)
    scale_second = jnp.exp(top_second - top_both)
    return (
        top_both,
        sum_first * scale_first + sum_second * scale_second,
        summed_first * scale_first[..., None] + summed_second * scale_second[..., None],
    )


def packed(values, index):
    chooser = (index[:, None] == jnp.arange(values.shape[0], dtype=index.dtype)[None, :]).astype(
        values.dtype
    )
    return jnp.dot(chooser, values, preferred_element_type=jnp.float32).astype(values.dtype)


def routing(home_slot, group_count, local_reqs):
    dest_group = (home_slot // local_reqs).reshape(group_count, local_reqs)
    local_ids = jnp.arange(local_reqs, dtype=jnp.int32)
    earlier = local_ids[None, :] < local_ids[:, None]
    same_dest = dest_group[:, :, None] == dest_group[:, None, :]
    dest_rank = jnp.sum(same_dest & earlier[None], axis=2)
    return (dest_group, dest_rank)


def tree_part(queries, keys_new, values_new, ancestors):
    scores = attn_mult * jnp.einsum(
        "rtkgd,rukd->rtkgu", queries, keys_new, preferred_element_type=jnp.float32
    )
    valid_keys = (ancestors > 0.5)[:, :, None, None, :]
    masked = jnp.where(valid_keys, scores, neg_fill)
    top_score = jnp.max(masked, axis=-1)
    weights = jnp.where(valid_keys, jnp.exp(masked - top_score[..., None]), 0.0)
    summed = jnp.einsum(
        "rtkgu,rukd->rtkgd",
        weights.astype(jnp.bfloat16),
        values_new,
        preferred_element_type=jnp.float32,
    )
    return (top_score, jnp.sum(weights, axis=-1), summed)


def cache_kernel(lens_ref, start_ref, q_ref, k_ref, v_ref, top_ref, sum_ref, acc_ref):
    slot = pl.program_id(0)
    head_local = top_ref.shape[1]
    cache_local = k_ref.shape[1]
    limit = lens_ref[slot] - start_ref[0]
    valid = lax.broadcasted_iota(jnp.int32, (1, cache_local), 1) < limit
    keys = k_ref[0]
    values = v_ref[0]
    lane = lax.broadcasted_iota(jnp.int32, (1, head_local * HD), 1)
    queries = q_ref[0] * jnp.asarray(attn_mult, q_ref.dtype)
    any_valid = limit > 0
    result = None
    for head in range(head_local):
        mine = (lane >= head * HD) & (lane < (head + 1) * HD)
        own = jnp.where(mine, queries, jnp.zeros((), queries.dtype))
        scores = lax.dot_general(
            own, keys, (((1,), (1,)), ((), ())), preferred_element_type=jnp.float32
        )
        masked = jnp.where(valid, scores, neg_fill)
        top = jnp.max(masked, axis=1, keepdims=True)
        weights = jnp.exp(masked - top)
        summed = jnp.dot(weights.astype(jnp.bfloat16), values, preferred_element_type=jnp.float32)
        total = jnp.where(any_valid, jnp.sum(weights, axis=1, keepdims=True), 0.0)
        top_ref[0, head : head + 1, :] = jnp.broadcast_to(top, (top.shape[0], 128)).T[0:1, :]
        sum_ref[0, head : head + 1, :] = jnp.broadcast_to(total, (total.shape[0], 128)).T[0:1, :]
        result = summed if result is None else jnp.where(mine, summed, result)
    acc_ref[0] = jnp.where(any_valid, result, 0.0)


def cache_merged(slot_queries, k_cache, v_cache, home_lens):
    local_reqs, tree_slots, head_local = slot_queries.shape[:3]
    cache_local = k_cache.shape[1]
    width = head_local * HD
    rows = tree_slots * GROUP
    key_start = (lax.axis_index("ty") * cache_local).astype(jnp.int32).reshape(1)
    spread = slot_queries.transpose(0, 1, 3, 2, 4).reshape(local_reqs, rows, width)
    top, total, summed = pl.pallas_call(
        cache_kernel,
        grid_spec=pltpu.PrefetchScalarGridSpec(
            num_scalar_prefetch=2,
            grid=(local_reqs,),
            in_specs=[
                pl.BlockSpec((1, rows, width), lambda s, lens, start: (s, 0, 0)),
                pl.BlockSpec((1, cache_local, width), lambda s, lens, start: (s, 0, 0)),
                pl.BlockSpec((1, cache_local, width), lambda s, lens, start: (s, 0, 0)),
            ],
            out_specs=[
                pl.BlockSpec((1, head_local, rows), lambda s, lens, start: (s, 0, 0)),
                pl.BlockSpec((1, head_local, rows), lambda s, lens, start: (s, 0, 0)),
                pl.BlockSpec((1, rows, width), lambda s, lens, start: (s, 0, 0)),
            ],
        ),
        out_shape=[
            jax.ShapeDtypeStruct((local_reqs, head_local, rows), jnp.float32),
            jax.ShapeDtypeStruct((local_reqs, head_local, rows), jnp.float32),
            jax.ShapeDtypeStruct((local_reqs, rows, width), jnp.float32),
        ],
        cost_estimate=pl.CostEstimate(
            flops=4 * local_reqs * head_local * rows * cache_local * width,
            transcendentals=local_reqs * head_local * rows * cache_local,
            bytes_accessed=2 * k_cache.size * 2 + spread.size * 2 + local_reqs * rows * width * 4,
        ),
    )(home_lens, key_start, spread, k_cache, v_cache)
    top_all = ty_max(top)
    scale = jnp.exp(top - top_all)
    scale_lanes = jnp.repeat(scale.transpose(0, 2, 1), HD, axis=2)
    count = total.size
    joint = jnp.concatenate(
        [(summed * scale_lanes).reshape(-1, 128), (total * scale).reshape(count // 128, 128)],
        axis=0,
    )
    joint = axis_sum(joint, "ty", True, jnp.bfloat16, jnp.bfloat16, 2)[: joint.shape[0]]
    summed = joint[: summed.size // 128].reshape(summed.shape[0], -1)
    total = joint[summed.size // 128 :].reshape(total.shape[0], -1)
    return (top_all, total, summed)


def ty_max_kernel(x_ref, out_ref, held, send_sem, recv_sem):
    n = lax.axis_size("ty")
    me = lax.axis_index("ty")
    row = lax.axis_index("dp")
    col = lax.axis_index("tx")
    barrier = pltpu.get_barrier_semaphore()
    for step in range(1, n):
        peer = lax.rem(me + step, n)
        pl.semaphore_signal(
            barrier, inc=1, device_id=(row, col, peer), device_id_type=pl.DeviceIdType.MESH
        )
    pl.semaphore_wait(barrier, n - 1)
    copies = []
    for step in range(1, n):
        peer = lax.rem(me + step, n)
        copy = pltpu.make_async_remote_copy(
            src_ref=x_ref,
            dst_ref=held.at[step - 1],
            send_sem=send_sem.at[step - 1],
            recv_sem=recv_sem.at[step - 1],
            device_id=(row, col, peer),
            device_id_type=pl.DeviceIdType.MESH,
        )
        copy.start()
        copies.append(copy)
    for copy in copies:
        copy.wait()
    result = x_ref[...]
    for step in range(1, n):
        result = jnp.maximum(result, held[step - 1])
    out_ref[...] = result


def axis_sum_kernel(axis, gather, x_ref, out_ref, held, gathered, sems):
    n = lax.axis_size(axis)
    me = lax.axis_index(axis)
    chunk = held.shape[1]
    where = {name: lax.axis_index(name) for name in ("dp", "tx", "ty")}

    def device(peer):
        return tuple(peer if name == axis else where[name] for name in ("dp", "tx", "ty"))

    barrier = pltpu.get_barrier_semaphore()
    for step in range(1, n):
        pl.semaphore_signal(
            barrier, inc=1, device_id=device(lax.rem(me + step, n)), device_id_type=pl.DeviceIdType.MESH
        )
    pl.semaphore_wait(barrier, n - 1)
    copies = []
    for step in range(1, n):
        peer = lax.rem(me + step, n)
        copy = pltpu.make_async_remote_copy(
            src_ref=x_ref.at[pl.ds(pl.multiple_of(peer * chunk, 16), chunk)],
            dst_ref=held.at[step - 1],
            send_sem=sems.at[0, step - 1],
            recv_sem=sems.at[1, step - 1],
            device_id=device(peer),
            device_id_type=pl.DeviceIdType.MESH,
        )
        copy.start()
        copies.append(copy)
    for copy in copies:
        copy.wait()
    own = pl.ds(pl.multiple_of(me * chunk, 16), chunk)
    total = x_ref[own].astype(jnp.float32)
    for step in range(1, n):
        total = total + held[step - 1].astype(jnp.float32)
    if not gather:
        out_ref[...] = total.astype(out_ref.dtype)
        return
    out_ref[own] = total.astype(out_ref.dtype)
    copies = []
    for step in range(1, n):
        peer = lax.rem(me + step, n)
        copy = pltpu.make_async_remote_copy(
            src_ref=out_ref.at[own],
            dst_ref=gathered.at[step - 1],
            send_sem=sems.at[2, step - 1],
            recv_sem=sems.at[3, step - 1],
            device_id=device(peer),
            device_id_type=pl.DeviceIdType.MESH,
        )
        copy.start()
        copies.append(copy)
    for copy in copies:
        copy.wait()
    for step in range(1, n):
        source = lax.rem(me - step + n, n)
        out_ref[pl.ds(pl.multiple_of(source * chunk, 16), chunk)] = gathered[step - 1]


def axis_sum(values, axis, gather, send_type, out_type, collective_id):
    n = lax.axis_size(axis)
    flat = values.reshape(-1, 128).astype(send_type)
    rows = flat.shape[0]
    padded = -(-rows // (16 * n)) * 16 * n
    flat = jnp.pad(flat, ((0, padded - rows), (0, 0)))
    chunk = padded // n
    out = pl.pallas_call(
        functools.partial(axis_sum_kernel, axis, gather),
        out_shape=jax.ShapeDtypeStruct((padded if gather else chunk, 128), out_type),
        in_specs=[pl.BlockSpec(memory_space=pltpu.VMEM)],
        out_specs=pl.BlockSpec(memory_space=pltpu.VMEM),
        scratch_shapes=[
            pltpu.VMEM((n - 1, chunk, 128), send_type),
            pltpu.VMEM((n - 1, chunk, 128), out_type),
            pltpu.SemaphoreType.DMA((4, n - 1)),
        ],
        compiler_params=pltpu.CompilerParams(collective_id=collective_id, has_side_effects=True),
    )(flat)
    return out


def dp_exchange_kernel(x_ref, out_ref, held, sems):
    n = lax.axis_size("dp")
    me = lax.axis_index("dp")
    col = lax.axis_index("tx")
    row = lax.axis_index("ty")
    barrier = pltpu.get_barrier_semaphore()
    for step in range(1, n):
        pl.semaphore_signal(
            barrier, inc=1, device_id=(lax.rem(me + step, n), col, row), device_id_type=pl.DeviceIdType.MESH
        )
    pl.semaphore_wait(barrier, n - 1)
    copies = []
    for step in range(1, n):
        peer = lax.rem(me + step, n)
        copy = pltpu.make_async_remote_copy(
            src_ref=x_ref.at[peer],
            dst_ref=held.at[step - 1],
            send_sem=sems.at[0, step - 1],
            recv_sem=sems.at[1, step - 1],
            device_id=(peer, col, row),
            device_id_type=pl.DeviceIdType.MESH,
        )
        copy.start()
        copies.append(copy)
    out_ref[me] = x_ref[me]
    for copy in copies:
        copy.wait()
    for step in range(1, n):
        out_ref[lax.rem(me - step + n, n)] = held[step - 1]


def dp_exchange(blocks, collective_id):
    n = lax.axis_size("dp")
    shape = blocks.shape
    tiles = blocks.reshape(n, -1, 128)
    out = pl.pallas_call(
        dp_exchange_kernel,
        out_shape=jax.ShapeDtypeStruct(tiles.shape, tiles.dtype),
        in_specs=[pl.BlockSpec(memory_space=pltpu.VMEM)],
        out_specs=pl.BlockSpec(memory_space=pltpu.VMEM),
        scratch_shapes=[
            pltpu.VMEM((n - 1,) + tiles.shape[1:], tiles.dtype),
            pltpu.SemaphoreType.DMA((2, n - 1)),
        ],
        compiler_params=pltpu.CompilerParams(collective_id=collective_id, has_side_effects=True),
    )(tiles)
    return out.reshape(shape)


def axis_gather_kernel(axis, x_ref, out_ref, gathered, sems):
    n = lax.axis_size(axis)
    me = lax.axis_index(axis)
    chunk = x_ref.shape[0]
    where = {name: lax.axis_index(name) for name in ("dp", "tx", "ty")}

    def device(peer):
        return tuple(peer if name == axis else where[name] for name in ("dp", "tx", "ty"))

    barrier = pltpu.get_barrier_semaphore()
    for step in range(1, n):
        pl.semaphore_signal(
            barrier, inc=1, device_id=device(lax.rem(me + step, n)), device_id_type=pl.DeviceIdType.MESH
        )
    pl.semaphore_wait(barrier, n - 1)
    copies = []
    for step in range(1, n):
        peer = lax.rem(me + step, n)
        copy = pltpu.make_async_remote_copy(
            src_ref=x_ref,
            dst_ref=gathered.at[step - 1],
            send_sem=sems.at[0, step - 1],
            recv_sem=sems.at[1, step - 1],
            device_id=device(peer),
            device_id_type=pl.DeviceIdType.MESH,
        )
        copy.start()
        copies.append(copy)
    out_ref[pl.ds(pl.multiple_of(me * chunk, 16), chunk)] = x_ref[...]
    for copy in copies:
        copy.wait()
    for step in range(1, n):
        source = lax.rem(me - step + n, n)
        out_ref[pl.ds(pl.multiple_of(source * chunk, 16), chunk)] = gathered[step - 1]


def axis_gather(values, axis, collective_id):
    n = lax.axis_size(axis)
    flat = values.reshape(-1, 128)
    chunk = flat.shape[0]
    out = pl.pallas_call(
        functools.partial(axis_gather_kernel, axis),
        out_shape=jax.ShapeDtypeStruct((n * chunk, 128), flat.dtype),
        in_specs=[pl.BlockSpec(memory_space=pltpu.VMEM)],
        out_specs=pl.BlockSpec(memory_space=pltpu.VMEM),
        scratch_shapes=[
            pltpu.VMEM((n - 1, chunk, 128), flat.dtype),
            pltpu.SemaphoreType.DMA((2, n - 1)),
        ],
        compiler_params=pltpu.CompilerParams(collective_id=collective_id, has_side_effects=True),
    )(flat)
    return out.reshape((n * values.shape[0],) + values.shape[1:])


def ty_max(values):
    n = lax.axis_size("ty")
    flat = values.reshape(-1, 128)
    out = pl.pallas_call(
        ty_max_kernel,
        out_shape=jax.ShapeDtypeStruct(flat.shape, flat.dtype),
        in_specs=[pl.BlockSpec(memory_space=pltpu.VMEM)],
        out_specs=pl.BlockSpec(memory_space=pltpu.VMEM),
        scratch_shapes=[
            pltpu.VMEM((n - 1,) + flat.shape, flat.dtype),
            pltpu.SemaphoreType.DMA((n - 1,)),
            pltpu.SemaphoreType.DMA((n - 1,)),
        ],
        compiler_params=pltpu.CompilerParams(collective_id=0, has_side_effects=True),
    )(flat)
    return out.reshape(values.shape)


def shards(
    hidden_in,
    norm_gain,
    w_qkv,
    w_out,
    k_cache,
    v_cache,
    cache_lens,
    home_slot,
    parents,
    tree_sizes,
    leaf_node,
):
    group_count = lax.axis_size("dp")
    group_index = lax.axis_index("dp")
    local_reqs = k_cache.shape[0]
    tree_slots = parents.shape[1]
    capacity = (local_reqs + group_count - 1) // group_count
    head_local = k_cache.shape[2] // HD
    row_count = hidden_in.shape[0]
    float_in = hidden_in.astype(jnp.float32)
    feature_local = hidden_in.shape[1]
    gain_part = lax.dynamic_slice_in_dim(
        norm_gain, lax.axis_index("ty") * feature_local, feature_local
    )
    scaled = (float_in * gain_part.astype(jnp.float32)).astype(jnp.bfloat16)
    partial_proj = jnp.dot(scaled, w_qkv, preferred_element_type=jnp.float32)
    partial_square = jnp.sum(float_in * float_in, axis=1)
    proj_cols = partial_proj.shape[1]
    n_ty = lax.axis_size("ty")
    chunk_rows = row_count // n_ty
    reqs_mine = local_reqs // n_ty
    square_block = jnp.pad(
        partial_square.reshape(n_ty, 1, chunk_rows),
        ((0, 0), (0, 7), (0, proj_cols - chunk_rows)),
    )
    joint = jnp.concatenate(
        [partial_proj.reshape(n_ty, chunk_rows, proj_cols), square_block], axis=1
    )
    mine = axis_sum(joint, "ty", False, jnp.float32, jnp.float32, 1).reshape(-1, proj_cols)
    square_sum = mine[chunk_rows, :chunk_rows]
    rms_inverse = lax.rsqrt(square_sum / D + norm_eps)
    projected = (mine[:chunk_rows] * rms_inverse[:, None]).reshape(
        reqs_mine, tree_slots, head_local, GROUP + 2, HD
    )
    first_request = group_index * local_reqs
    local_ids = jnp.arange(local_reqs, dtype=jnp.int32)
    request_ids = jnp.arange(home_slot.shape[0], dtype=jnp.int32)
    my_parents = lax.dynamic_slice_in_dim(parents, first_request, local_reqs, 0)
    my_slots = lax.dynamic_slice_in_dim(home_slot, first_request, local_reqs, 0)
    ancestors = jax.vmap(ancestry)(my_parents)
    node_depth = jnp.sum(ancestors > 0.5, axis=2) - 1
    slot_match = my_slots[:, None] == request_ids[None, :]
    my_lens = jnp.sum(jnp.where(slot_match, cache_lens[None, :], 0), axis=1)
    positions = my_lens[:, None] + node_depth
    positions_mine = lax.dynamic_slice_in_dim(
        positions, lax.axis_index("ty") * reqs_mine, reqs_mine, 0
    )
    queries_mine = rotated(
        projected[:, :, :, :GROUP, :], positions_mine[:, :, None, None]
    ).astype(jnp.bfloat16)
    keys_mine = rotated(projected[:, :, :, GROUP, :], positions_mine[:, :, None]).astype(
        jnp.bfloat16
    )
    values_mine = projected[:, :, :, GROUP + 1, :].astype(jnp.bfloat16)
    piece = jnp.concatenate(
        [
            queries_mine.reshape(chunk_rows, -1),
            keys_mine.reshape(chunk_rows, -1),
            values_mine.reshape(chunk_rows, -1),
        ],
        axis=1,
    )
    everything = axis_gather(piece, "ty", 6)
    query_cols = head_local * GROUP * HD
    queries = everything[:, :query_cols].reshape(local_reqs, tree_slots, head_local, GROUP, HD)
    keys_new = everything[:, query_cols : query_cols + head_local * HD].reshape(
        local_reqs, tree_slots, head_local, HD
    )
    values_new = everything[:, query_cols + head_local * HD :].reshape(
        local_reqs, tree_slots, head_local, HD
    )
    dest_group, dest_rank = routing(home_slot, group_count, local_reqs)
    send_pos = lax.dynamic_index_in_dim(
        dest_group, group_index, 0, keepdims=False
    ) * capacity + lax.dynamic_index_in_dim(dest_rank, group_index, 0, keepdims=False)
    buffer_ids = jnp.arange(group_count * capacity, dtype=jnp.int32)
    send_hit = send_pos[None, :] == buffer_ids[:, None]
    send_index = jnp.where(
        jnp.any(send_hit, axis=1),
        jnp.sum(jnp.where(send_hit, local_ids[None, :], 0), axis=1),
        local_reqs,
    )
    target_slots = first_request + local_ids
    owner_match = home_slot[None, :] == target_slots[:, None]
    owner_request = jnp.sum(jnp.where(owner_match, request_ids[None, :], 0), axis=1)
    owner_rank = jnp.sum(jnp.where(owner_match, dest_rank.reshape(-1)[None, :], 0), axis=1)
    recv_index = owner_request // local_reqs * capacity + owner_rank
    back_hit = recv_index[None, :] == buffer_ids[:, None]
    back_index = jnp.where(
        jnp.any(back_hit, axis=1),
        jnp.sum(jnp.where(back_hit, local_ids[None, :], 0), axis=1),
        local_reqs,
    )
    home_lens = lax.dynamic_slice_in_dim(cache_lens, first_request, local_reqs, 0)
    arrived = dp_exchange(packed(queries.reshape(local_reqs, -1), send_index), 4)
    slot_queries = packed(arrived, recv_index).reshape(queries.shape)
    top_score, weight_sum, summed = cache_merged(slot_queries, k_cache, v_cache, home_lens)
    value_width = summed.shape[1]
    sum_width = weight_sum.shape[1]
    log_flat = top_score.reshape(local_reqs, -1)
    log_high = lax.reduce_precision(log_flat, exponent_bits=8, mantissa_bits=7)
    log_rest = log_flat - log_high
    log_mid = lax.reduce_precision(log_rest, exponent_bits=8, mantissa_bits=7)
    log_low = log_rest - log_mid
    payload = jnp.concatenate(
        [
            summed.reshape(local_reqs, tree_slots, GROUP, head_local, HD)
            .transpose(0, 1, 3, 2, 4)
            .reshape(local_reqs, -1),
            weight_sum,
            log_high.astype(jnp.bfloat16),
            log_mid.astype(jnp.bfloat16),
            log_low.astype(jnp.bfloat16),
        ],
        axis=1,
    )
    outgoing = packed(payload, back_index)
    back = lax.all_to_all(
        outgoing.reshape(outgoing.shape[0], -1, 128), "dp", split_axis=0, concat_axis=0, tiled=True
    ).reshape(outgoing.shape)
    back = packed(back, send_pos).astype(jnp.float32)
    log_width = log_flat.shape[1]
    cache_values = back[:, :value_width].reshape(local_reqs, tree_slots, head_local, GROUP, HD)
    cache_sum = (
        back[:, value_width : value_width + sum_width]
        .reshape(local_reqs, head_local, tree_slots, GROUP)
        .transpose(0, 2, 1, 3)
    )
    logs = value_width + sum_width
    cache_top = (
        (
            back[:, logs : logs + log_width]
            + back[:, logs + log_width : logs + 2 * log_width]
            + back[:, logs + 2 * log_width :]
        )
        .reshape(local_reqs, head_local, tree_slots, GROUP)
        .transpose(0, 2, 1, 3)
    )
    tree_stats = tree_part(queries, keys_new, values_new, ancestors)
    top_all, sum_all, summed_all = combine_stats(
        (cache_top, cache_sum, cache_values), tree_stats
    )
    attention = (summed_all / sum_all[..., None]).astype(jnp.bfloat16)
    attention_rows = attention.reshape(row_count, -1)
    rows_mine = row_count // lax.axis_size("tx")
    mixed_sum = axis_sum(
        jnp.dot(attention_rows, w_out, preferred_element_type=jnp.float32),
        "tx",
        False,
        jnp.bfloat16,
        jnp.float32,
        3,
    ).reshape(row_count // lax.axis_size("tx"), -1)
    row_start = lax.axis_index("tx") * rows_mine
    residual = lax.dynamic_slice_in_dim(float_in, row_start, rows_mine, 0)
    row_ids = row_start + jnp.arange(rows_mine, dtype=jnp.int32)
    request_of = row_ids // tree_slots
    slot_of = row_ids % tree_slots
    size_of = jnp.sum(
        jnp.where(request_of[:, None] == local_ids[None, :], tree_sizes[None, :], 0), axis=1
    )
    layer_out = jnp.where((slot_of < size_of)[:, None], residual + mixed_sum, 0.0).astype(
        jnp.bfloat16
    )
    node_ids = jnp.arange(tree_slots, dtype=jnp.int32)
    leaf_hit = (leaf_node[:, None] == node_ids[None, :]).astype(jnp.float32)
    path_nodes = jnp.einsum("rt,rtu->ru", leaf_hit, ancestors)
    depth_hit = node_depth[:, None, :] == jnp.arange(ACC, dtype=jnp.int32)[None, :, None]
    chooser = jnp.where(depth_hit, path_nodes[:, None, :], 0.0).astype(jnp.bfloat16)
    stacked = jnp.stack(
        [
            keys_new.reshape(local_reqs, tree_slots, -1),
            values_new.reshape(local_reqs, tree_slots, -1),
        ],
        axis=2,
    )
    accepted_kv = jnp.einsum(
        "rsu,ruwc->rswc", chooser, stacked, preferred_element_type=jnp.float32
    ).astype(jnp.bfloat16)
    return (layer_out, accepted_kv)


def solution(mesh):
    return jax.shard_map(
        shards,
        mesh=mesh,
        in_specs=(
            P("dp", "ty"),
            P(),
            P("ty", "tx"),
            P("tx", "ty"),
            P("dp", "ty", "tx"),
            P("dp", "ty", "tx"),
            P(),
            P(),
            P(),
            P("dp"),
            P("dp"),
        ),
        out_specs=(P(("dp", "tx"), "ty"), P("dp", None, None, "tx")),
        check_vma=False,
    )
```

```python
import functools

import jax
import jax.numpy as jnp
from jax import lax
from jax.experimental import pallas as pl
from jax.experimental.pallas import tpu as pltpu
from jax.sharding import PartitionSpec as P

D = 2048
HD = 64
GROUP = 4
ACC = 8


rope_base = 10000000.0
attn_mult = 0.015625
norm_eps = 1e-05
neg_fill = -1e30


def joined(value, axis, join):
    pieces = jax.tree.map(lambda part: lax.all_gather(part, axis), value)
    head = jax.tree.map(lambda part: part[0], pieces)
    tail = jax.tree.map(lambda part: part[1:], pieces)
    so_far, _ = lax.scan(lambda so_far, slab: (join(so_far, slab), None), head, tail)
    return so_far


def ancestry(parent_rows):
    node_count = parent_rows.shape[-1]
    node_ids = jnp.arange(node_count, dtype=jnp.int32)
    linked = (node_ids[None, :] == parent_rows[:, None]) | (node_ids[None, :] == node_ids[:, None])
    reachable = linked.astype(jnp.float32)
    for repeat in range(max(1, (node_count - 1).bit_length())):
        reachable = jnp.minimum(jnp.dot(reachable, reachable, precision=lax.Precision.HIGHEST), 1.0)
    return reachable


def rotated(values, positions):
    half_size = values.shape[-1] // 2
    frequency = rope_base ** (-2.0 * jnp.arange(half_size, dtype=jnp.float32) / values.shape[-1])
    angles = positions.astype(jnp.float32)[..., None] * frequency
    cosine = jnp.cos(angles)
    sine_part = jnp.sin(angles)
    front_half = values[..., :half_size]
    back_half = values[..., half_size:]
    return jnp.concatenate(
        [front_half * cosine - back_half * sine_part, back_half * cosine + front_half * sine_part],
        axis=-1,
    )


def combine_stats(first_stats, second_stats):
    top_first, sum_first, summed_first = first_stats
    top_second, sum_second, summed_second = second_stats
    top_both = jnp.maximum(top_first, top_second)
    scale_first = jnp.exp(top_first - top_both)
    scale_second = jnp.exp(top_second - top_both)
    return (
        top_both,
        sum_first * scale_first + sum_second * scale_second,
        summed_first * scale_first[..., None] + summed_second * scale_second[..., None],
    )


def packed(values, index):
    chooser = (index[:, None] == jnp.arange(values.shape[0], dtype=index.dtype)[None, :]).astype(
        values.dtype
    )
    return jnp.dot(chooser, values, preferred_element_type=jnp.float32).astype(values.dtype)


def routing(home_slot, group_count, local_reqs):
    dest_group = (home_slot // local_reqs).reshape(group_count, local_reqs)
    local_ids = jnp.arange(local_reqs, dtype=jnp.int32)
    earlier = local_ids[None, :] < local_ids[:, None]
    same_dest = dest_group[:, :, None] == dest_group[:, None, :]
    dest_rank = jnp.sum(same_dest & earlier[None], axis=2)
    return (dest_group, dest_rank)


def tree_part(queries, keys_new, values_new, ancestors):
    scores = attn_mult * jnp.einsum(
        "rtkgd,rukd->rtkgu", queries, keys_new, preferred_element_type=jnp.float32
    )
    valid_keys = (ancestors > 0.5)[:, :, None, None, :]
    masked = jnp.where(valid_keys, scores, neg_fill)
    top_score = jnp.max(masked, axis=-1)
    weights = jnp.where(valid_keys, jnp.exp(masked - top_score[..., None]), 0.0)
    summed = jnp.einsum(
        "rtkgu,rukd->rtkgd",
        weights.astype(jnp.bfloat16),
        values_new,
        preferred_element_type=jnp.float32,
    )
    return (top_score, jnp.sum(weights, axis=-1), summed)


def cache_kernel(lens_ref, start_ref, q_ref, k_ref, v_ref, top_ref, sum_ref, acc_ref):
    slot = pl.program_id(0)
    head_local = top_ref.shape[1]
    cache_local = k_ref.shape[1]
    limit = lens_ref[slot] - start_ref[0]
    valid = lax.broadcasted_iota(jnp.int32, (1, cache_local), 1) < limit
    keys = k_ref[0]
    values = v_ref[0]
    lane = lax.broadcasted_iota(jnp.int32, (1, head_local * HD), 1)
    queries = q_ref[0] * jnp.asarray(attn_mult, q_ref.dtype)
    any_valid = limit > 0
    result = None
    for head in range(head_local):
        mine = (lane >= head * HD) & (lane < (head + 1) * HD)
        own = jnp.where(mine, queries, jnp.zeros((), queries.dtype))
        scores = lax.dot_general(
            own, keys, (((1,), (1,)), ((), ())), preferred_element_type=jnp.float32
        )
        masked = jnp.where(valid, scores, neg_fill)
        top = jnp.max(masked, axis=1, keepdims=True)
        weights = jnp.exp(masked - top)
        summed = jnp.dot(weights.astype(jnp.bfloat16), values, preferred_element_type=jnp.float32)
        total = jnp.where(any_valid, jnp.sum(weights, axis=1, keepdims=True), 0.0)
        top_ref[0, head : head + 1, :] = jnp.broadcast_to(top, (top.shape[0], 128)).T[0:1, :]
        sum_ref[0, head : head + 1, :] = jnp.broadcast_to(total, (total.shape[0], 128)).T[0:1, :]
        result = summed if result is None else jnp.where(mine, summed, result)
    acc_ref[0] = jnp.where(any_valid, result, 0.0)


def cache_merged(slot_queries, k_cache, v_cache, home_lens):
    local_reqs, tree_slots, head_local = slot_queries.shape[:3]
    cache_local = k_cache.shape[1]
    width = head_local * HD
    rows = tree_slots * GROUP
    key_start = (lax.axis_index("ty") * cache_local).astype(jnp.int32).reshape(1)
    spread = slot_queries.transpose(0, 1, 3, 2, 4).reshape(local_reqs, rows, width)
    top, total, summed = pl.pallas_call(
        cache_kernel,
        grid_spec=pltpu.PrefetchScalarGridSpec(
            num_scalar_prefetch=2,
            grid=(local_reqs,),
            in_specs=[
                pl.BlockSpec((1, rows, width), lambda s, lens, start: (s, 0, 0)),
                pl.BlockSpec((1, cache_local, width), lambda s, lens, start: (s, 0, 0)),
                pl.BlockSpec((1, cache_local, width), lambda s, lens, start: (s, 0, 0)),
            ],
            out_specs=[
                pl.BlockSpec((1, head_local, rows), lambda s, lens, start: (s, 0, 0)),
                pl.BlockSpec((1, head_local, rows), lambda s, lens, start: (s, 0, 0)),
                pl.BlockSpec((1, rows, width), lambda s, lens, start: (s, 0, 0)),
            ],
        ),
        out_shape=[
            jax.ShapeDtypeStruct((local_reqs, head_local, rows), jnp.float32),
            jax.ShapeDtypeStruct((local_reqs, head_local, rows), jnp.float32),
            jax.ShapeDtypeStruct((local_reqs, rows, width), jnp.float32),
        ],
        cost_estimate=pl.CostEstimate(
            flops=4 * local_reqs * head_local * rows * cache_local * width,
            transcendentals=local_reqs * head_local * rows * cache_local,
            bytes_accessed=2 * k_cache.size * 2 + spread.size * 2 + local_reqs * rows * width * 4,
        ),
    )(home_lens, key_start, spread, k_cache, v_cache)
    top_all = ty_max(top)
    scale = jnp.exp(top - top_all)
    scale_lanes = jnp.repeat(scale.transpose(0, 2, 1), HD, axis=2)
    count = total.size
    joint = jnp.concatenate(
        [(summed * scale_lanes).reshape(-1, 128), (total * scale).reshape(count // 128, 128)],
        axis=0,
    )
    joint = axis_sum(joint, "ty", True, jnp.bfloat16, jnp.bfloat16, 2)[: joint.shape[0]]
    summed = joint[: summed.size // 128].reshape(summed.shape[0], -1)
    total = joint[summed.size // 128 :].reshape(total.shape[0], -1)
    return (top_all, total, summed)


def ty_max_kernel(x_ref, out_ref, held, send_sem, recv_sem):
    n = lax.axis_size("ty")
    me = lax.axis_index("ty")
    row = lax.axis_index("dp")
    col = lax.axis_index("tx")
    barrier = pltpu.get_barrier_semaphore()
    for step in range(1, n):
        peer = lax.rem(me + step, n)
        pl.semaphore_signal(
            barrier, inc=1, device_id=(row, col, peer), device_id_type=pl.DeviceIdType.MESH
        )
    pl.semaphore_wait(barrier, n - 1)
    copies = []
    for step in range(1, n):
        peer = lax.rem(me + step, n)
        copy = pltpu.make_async_remote_copy(
            src_ref=x_ref,
            dst_ref=held.at[step - 1],
            send_sem=send_sem.at[step - 1],
            recv_sem=recv_sem.at[step - 1],
            device_id=(row, col, peer),
            device_id_type=pl.DeviceIdType.MESH,
        )
        copy.start()
        copies.append(copy)
    for copy in copies:
        copy.wait()
    result = x_ref[...]
    for step in range(1, n):
        result = jnp.maximum(result, held[step - 1])
    out_ref[...] = result


def axis_sum_kernel(axis, gather, x_ref, out_ref, held, gathered, sems):
    n = lax.axis_size(axis)
    me = lax.axis_index(axis)
    chunk = held.shape[1]
    where = {name: lax.axis_index(name) for name in ("dp", "tx", "ty")}

    def device(peer):
        return tuple(peer if name == axis else where[name] for name in ("dp", "tx", "ty"))

    barrier = pltpu.get_barrier_semaphore()
    for step in range(1, n):
        pl.semaphore_signal(
            barrier, inc=1, device_id=device(lax.rem(me + step, n)), device_id_type=pl.DeviceIdType.MESH
        )
    pl.semaphore_wait(barrier, n - 1)
    copies = []
    for step in range(1, n):
        peer = lax.rem(me + step, n)
        copy = pltpu.make_async_remote_copy(
            src_ref=x_ref.at[pl.ds(pl.multiple_of(peer * chunk, 16), chunk)],
            dst_ref=held.at[step - 1],
            send_sem=sems.at[0, step - 1],
            recv_sem=sems.at[1, step - 1],
            device_id=device(peer),
            device_id_type=pl.DeviceIdType.MESH,
        )
        copy.start()
        copies.append(copy)
    for copy in copies:
        copy.wait()
    own = pl.ds(pl.multiple_of(me * chunk, 16), chunk)
    total = x_ref[own].astype(jnp.float32)
    for step in range(1, n):
        total = total + held[step - 1].astype(jnp.float32)
    if not gather:
        out_ref[...] = total.astype(out_ref.dtype)
        return
    out_ref[own] = total.astype(out_ref.dtype)
    copies = []
    for step in range(1, n):
        peer = lax.rem(me + step, n)
        copy = pltpu.make_async_remote_copy(
            src_ref=out_ref.at[own],
            dst_ref=gathered.at[step - 1],
            send_sem=sems.at[2, step - 1],
            recv_sem=sems.at[3, step - 1],
            device_id=device(peer),
            device_id_type=pl.DeviceIdType.MESH,
        )
        copy.start()
        copies.append(copy)
    for copy in copies:
        copy.wait()
    for step in range(1, n):
        source = lax.rem(me - step + n, n)
        out_ref[pl.ds(pl.multiple_of(source * chunk, 16), chunk)] = gathered[step - 1]


def axis_sum(values, axis, gather, send_type, out_type, collective_id):
    n = lax.axis_size(axis)
    flat = values.reshape(-1, 128).astype(send_type)
    rows = flat.shape[0]
    padded = -(-rows // (16 * n)) * 16 * n
    flat = jnp.pad(flat, ((0, padded - rows), (0, 0)))
    chunk = padded // n
    out = pl.pallas_call(
        functools.partial(axis_sum_kernel, axis, gather),
        out_shape=jax.ShapeDtypeStruct((padded if gather else chunk, 128), out_type),
        in_specs=[pl.BlockSpec(memory_space=pltpu.VMEM)],
        out_specs=pl.BlockSpec(memory_space=pltpu.VMEM),
        scratch_shapes=[
            pltpu.VMEM((n - 1, chunk, 128), send_type),
            pltpu.VMEM((n - 1, chunk, 128), out_type),
            pltpu.SemaphoreType.DMA((4, n - 1)),
        ],
        compiler_params=pltpu.CompilerParams(collective_id=collective_id, has_side_effects=True),
    )(flat)
    return out


def dp_exchange_kernel(x_ref, out_ref, held, sems):
    n = lax.axis_size("dp")
    me = lax.axis_index("dp")
    col = lax.axis_index("tx")
    row = lax.axis_index("ty")
    barrier = pltpu.get_barrier_semaphore()
    for step in range(1, n):
        pl.semaphore_signal(
            barrier, inc=1, device_id=(lax.rem(me + step, n), col, row), device_id_type=pl.DeviceIdType.MESH
        )
    pl.semaphore_wait(barrier, n - 1)
    copies = []
    for step in range(1, n):
        peer = lax.rem(me + step, n)
        copy = pltpu.make_async_remote_copy(
            src_ref=x_ref.at[peer],
            dst_ref=held.at[step - 1],
            send_sem=sems.at[0, step - 1],
            recv_sem=sems.at[1, step - 1],
            device_id=(peer, col, row),
            device_id_type=pl.DeviceIdType.MESH,
        )
        copy.start()
        copies.append(copy)
    out_ref[me] = x_ref[me]
    for copy in copies:
        copy.wait()
    for step in range(1, n):
        out_ref[lax.rem(me - step + n, n)] = held[step - 1]


def dp_exchange(blocks, collective_id):
    n = lax.axis_size("dp")
    shape = blocks.shape
    tiles = blocks.reshape(n, -1, 128)
    out = pl.pallas_call(
        dp_exchange_kernel,
        out_shape=jax.ShapeDtypeStruct(tiles.shape, tiles.dtype),
        in_specs=[pl.BlockSpec(memory_space=pltpu.VMEM)],
        out_specs=pl.BlockSpec(memory_space=pltpu.VMEM),
        scratch_shapes=[
            pltpu.VMEM((n - 1,) + tiles.shape[1:], tiles.dtype),
            pltpu.SemaphoreType.DMA((2, n - 1)),
        ],
        compiler_params=pltpu.CompilerParams(collective_id=collective_id, has_side_effects=True),
    )(tiles)
    return out.reshape(shape)


def axis_gather_kernel(axis, x_ref, out_ref, gathered, sems):
    n = lax.axis_size(axis)
    me = lax.axis_index(axis)
    chunk = x_ref.shape[0]
    where = {name: lax.axis_index(name) for name in ("dp", "tx", "ty")}

    def device(peer):
        return tuple(peer if name == axis else where[name] for name in ("dp", "tx", "ty"))

    barrier = pltpu.get_barrier_semaphore()
    for step in range(1, n):
        pl.semaphore_signal(
            barrier, inc=1, device_id=device(lax.rem(me + step, n)), device_id_type=pl.DeviceIdType.MESH
        )
    pl.semaphore_wait(barrier, n - 1)
    copies = []
    for step in range(1, n):
        peer = lax.rem(me + step, n)
        copy = pltpu.make_async_remote_copy(
            src_ref=x_ref,
            dst_ref=gathered.at[step - 1],
            send_sem=sems.at[0, step - 1],
            recv_sem=sems.at[1, step - 1],
            device_id=device(peer),
            device_id_type=pl.DeviceIdType.MESH,
        )
        copy.start()
        copies.append(copy)
    out_ref[pl.ds(pl.multiple_of(me * chunk, 16), chunk)] = x_ref[...]
    for copy in copies:
        copy.wait()
    for step in range(1, n):
        source = lax.rem(me - step + n, n)
        out_ref[pl.ds(pl.multiple_of(source * chunk, 16), chunk)] = gathered[step - 1]


def axis_gather(values, axis, collective_id):
    n = lax.axis_size(axis)
    flat = values.reshape(-1, 128)
    chunk = flat.shape[0]
    out = pl.pallas_call(
        functools.partial(axis_gather_kernel, axis),
        out_shape=jax.ShapeDtypeStruct((n * chunk, 128), flat.dtype),
        in_specs=[pl.BlockSpec(memory_space=pltpu.VMEM)],
        out_specs=pl.BlockSpec(memory_space=pltpu.VMEM),
        scratch_shapes=[
            pltpu.VMEM((n - 1, chunk, 128), flat.dtype),
            pltpu.SemaphoreType.DMA((2, n - 1)),
        ],
        compiler_params=pltpu.CompilerParams(collective_id=collective_id, has_side_effects=True),
    )(flat)
    return out.reshape((n * values.shape[0],) + values.shape[1:])


def ty_max(values):
    n = lax.axis_size("ty")
    flat = values.reshape(-1, 128)
    out = pl.pallas_call(
        ty_max_kernel,
        out_shape=jax.ShapeDtypeStruct(flat.shape, flat.dtype),
        in_specs=[pl.BlockSpec(memory_space=pltpu.VMEM)],
        out_specs=pl.BlockSpec(memory_space=pltpu.VMEM),
        scratch_shapes=[
            pltpu.VMEM((n - 1,) + flat.shape, flat.dtype),
            pltpu.SemaphoreType.DMA((n - 1,)),
            pltpu.SemaphoreType.DMA((n - 1,)),
        ],
        compiler_params=pltpu.CompilerParams(collective_id=0, has_side_effects=True),
    )(flat)
    return out.reshape(values.shape)


def shards(
    hidden_in,
    norm_gain,
    w_qkv,
    w_out,
    k_cache,
    v_cache,
    cache_lens,
    home_slot,
    parents,
    tree_sizes,
    leaf_node,
):
    group_count = lax.axis_size("dp")
    group_index = lax.axis_index("dp")
    local_reqs = k_cache.shape[0]
    tree_slots = parents.shape[1]
    capacity = (local_reqs + group_count - 1) // group_count
    head_local = k_cache.shape[2] // HD
    row_count = hidden_in.shape[0]
    float_in = hidden_in.astype(jnp.float32)
    feature_local = hidden_in.shape[1]
    gain_part = lax.dynamic_slice_in_dim(
        norm_gain, lax.axis_index("ty") * feature_local, feature_local
    )
    scaled = (float_in * gain_part.astype(jnp.float32)).astype(jnp.bfloat16)
    partial_proj = jnp.dot(scaled, w_qkv, preferred_element_type=jnp.float32)
    partial_square = jnp.sum(float_in * float_in, axis=1)
    proj_cols = partial_proj.shape[1]
    n_ty = lax.axis_size("ty")
    chunk_rows = row_count // n_ty
    reqs_mine = local_reqs // n_ty
    square_block = jnp.pad(
        partial_square.reshape(n_ty, 1, chunk_rows),
        ((0, 0), (0, 7), (0, proj_cols - chunk_rows)),
    )
    joint = jnp.concatenate(
        [partial_proj.reshape(n_ty, chunk_rows, proj_cols), square_block], axis=1
    )
    mine = axis_sum(joint, "ty", False, jnp.float32, jnp.float32, 1).reshape(-1, proj_cols)
    square_sum = mine[chunk_rows, :chunk_rows]
    rms_inverse = lax.rsqrt(square_sum / D + norm_eps)
    projected = (mine[:chunk_rows] * rms_inverse[:, None]).reshape(
        reqs_mine, tree_slots, head_local, GROUP + 2, HD
    )
    first_request = group_index * local_reqs
    local_ids = jnp.arange(local_reqs, dtype=jnp.int32)
    request_ids = jnp.arange(home_slot.shape[0], dtype=jnp.int32)
    my_parents = lax.dynamic_slice_in_dim(parents, first_request, local_reqs, 0)
    my_slots = lax.dynamic_slice_in_dim(home_slot, first_request, local_reqs, 0)
    ancestors = jax.vmap(ancestry)(my_parents)
    node_depth = jnp.sum(ancestors > 0.5, axis=2) - 1
    slot_match = my_slots[:, None] == request_ids[None, :]
    my_lens = jnp.sum(jnp.where(slot_match, cache_lens[None, :], 0), axis=1)
    positions = my_lens[:, None] + node_depth
    positions_mine = lax.dynamic_slice_in_dim(
        positions, lax.axis_index("ty") * reqs_mine, reqs_mine, 0
    )
    queries_mine = rotated(
        projected[:, :, :, :GROUP, :], positions_mine[:, :, None, None]
    ).astype(jnp.bfloat16)
    keys_mine = rotated(projected[:, :, :, GROUP, :], positions_mine[:, :, None]).astype(
        jnp.bfloat16
    )
    values_mine = projected[:, :, :, GROUP + 1, :].astype(jnp.bfloat16)
    piece = jnp.concatenate(
        [
            queries_mine.reshape(chunk_rows, -1),
            keys_mine.reshape(chunk_rows, -1),
            values_mine.reshape(chunk_rows, -1),
        ],
        axis=1,
    )
    everything = axis_gather(piece, "ty", 6)
    query_cols = head_local * GROUP * HD
    queries = everything[:, :query_cols].reshape(local_reqs, tree_slots, head_local, GROUP, HD)
    keys_new = everything[:, query_cols : query_cols + head_local * HD].reshape(
        local_reqs, tree_slots, head_local, HD
    )
    values_new = everything[:, query_cols + head_local * HD :].reshape(
        local_reqs, tree_slots, head_local, HD
    )
    dest_group, dest_rank = routing(home_slot, group_count, local_reqs)
    send_pos = lax.dynamic_index_in_dim(
        dest_group, group_index, 0, keepdims=False
    ) * capacity + lax.dynamic_index_in_dim(dest_rank, group_index, 0, keepdims=False)
    buffer_ids = jnp.arange(group_count * capacity, dtype=jnp.int32)
    send_hit = send_pos[None, :] == buffer_ids[:, None]
    send_index = jnp.where(
        jnp.any(send_hit, axis=1),
        jnp.sum(jnp.where(send_hit, local_ids[None, :], 0), axis=1),
        local_reqs,
    )
    target_slots = first_request + local_ids
    owner_match = home_slot[None, :] == target_slots[:, None]
    owner_request = jnp.sum(jnp.where(owner_match, request_ids[None, :], 0), axis=1)
    owner_rank = jnp.sum(jnp.where(owner_match, dest_rank.reshape(-1)[None, :], 0), axis=1)
    recv_index = owner_request // local_reqs * capacity + owner_rank
    back_hit = recv_index[None, :] == buffer_ids[:, None]
    back_index = jnp.where(
        jnp.any(back_hit, axis=1),
        jnp.sum(jnp.where(back_hit, local_ids[None, :], 0), axis=1),
        local_reqs,
    )
    home_lens = lax.dynamic_slice_in_dim(cache_lens, first_request, local_reqs, 0)
    sending = packed(queries.reshape(local_reqs, -1), send_index)
    arrived = lax.all_to_all(
        sending.reshape(sending.shape[0], -1, 128), "dp", split_axis=0, concat_axis=0, tiled=True
    ).reshape(sending.shape)
    slot_queries = packed(arrived, recv_index).reshape(queries.shape)
    top_score, weight_sum, summed = cache_merged(slot_queries, k_cache, v_cache, home_lens)
    value_width = summed.shape[1]
    sum_width = weight_sum.shape[1]
    log_flat = top_score.reshape(local_reqs, -1)
    log_high = lax.reduce_precision(log_flat, exponent_bits=8, mantissa_bits=7)
    log_rest = log_flat - log_high
    log_mid = lax.reduce_precision(log_rest, exponent_bits=8, mantissa_bits=7)
    log_low = log_rest - log_mid
    payload = jnp.concatenate(
        [
            summed,
            weight_sum,
            log_high.astype(jnp.bfloat16),
            log_mid.astype(jnp.bfloat16),
            log_low.astype(jnp.bfloat16),
        ],
        axis=1,
    )
    outgoing = packed(payload, back_index)
    back = lax.all_to_all(
        outgoing.reshape(outgoing.shape[0], -1, 128), "dp", split_axis=0, concat_axis=0, tiled=True
    ).reshape(outgoing.shape)
    back = packed(back, send_pos).astype(jnp.float32)
    log_width = log_flat.shape[1]
    cache_values = (
        back[:, :value_width]
        .reshape(local_reqs, tree_slots, GROUP, head_local, HD)
        .transpose(0, 1, 3, 2, 4)
    )
    cache_sum = (
        back[:, value_width : value_width + sum_width]
        .reshape(local_reqs, head_local, tree_slots, GROUP)
        .transpose(0, 2, 1, 3)
    )
    logs = value_width + sum_width
    cache_top = (
        (
            back[:, logs : logs + log_width]
            + back[:, logs + log_width : logs + 2 * log_width]
            + back[:, logs + 2 * log_width :]
        )
        .reshape(local_reqs, head_local, tree_slots, GROUP)
        .transpose(0, 2, 1, 3)
    )
    tree_stats = tree_part(queries, keys_new, values_new, ancestors)
    top_all, sum_all, summed_all = combine_stats(
        (cache_top, cache_sum, cache_values), tree_stats
    )
    attention = (summed_all / sum_all[..., None]).astype(jnp.bfloat16)
    attention_rows = attention.reshape(row_count, -1)
    rows_mine = row_count // lax.axis_size("tx")
    mixed_sum = axis_sum(
        jnp.dot(attention_rows, w_out, preferred_element_type=jnp.float32),
        "tx",
        False,
        jnp.bfloat16,
        jnp.float32,
        3,
    ).reshape(row_count // lax.axis_size("tx"), -1)
    row_start = lax.axis_index("tx") * rows_mine
    residual = lax.dynamic_slice_in_dim(float_in, row_start, rows_mine, 0)
    row_ids = row_start + jnp.arange(rows_mine, dtype=jnp.int32)
    request_of = row_ids // tree_slots
    slot_of = row_ids % tree_slots
    size_of = jnp.sum(
        jnp.where(request_of[:, None] == local_ids[None, :], tree_sizes[None, :], 0), axis=1
    )
    layer_out = jnp.where((slot_of < size_of)[:, None], residual + mixed_sum, 0.0).astype(
        jnp.bfloat16
    )
    node_ids = jnp.arange(tree_slots, dtype=jnp.int32)
    leaf_hit = (leaf_node[:, None] == node_ids[None, :]).astype(jnp.float32)
    path_nodes = jnp.einsum("rt,rtu->ru", leaf_hit, ancestors)
    depth_hit = node_depth[:, None, :] == jnp.arange(ACC, dtype=jnp.int32)[None, :, None]
    chooser = jnp.where(depth_hit, path_nodes[:, None, :], 0.0).astype(jnp.bfloat16)
    stacked = jnp.stack(
        [
            keys_new.reshape(local_reqs, tree_slots, -1),
            values_new.reshape(local_reqs, tree_slots, -1),
        ],
        axis=2,
    )
    accepted_kv = jnp.einsum(
        "rsu,ruwc->rswc", chooser, stacked, preferred_element_type=jnp.float32
    ).astype(jnp.bfloat16)
    return (layer_out, accepted_kv)


def solution(mesh):
    return jax.shard_map(
        shards,
        mesh=mesh,
        in_specs=(
            P("dp", "ty"),
            P(),
            P("ty", "tx"),
            P("tx", "ty"),
            P("dp", "ty", "tx"),
            P("dp", "ty", "tx"),
            P(),
            P(),
            P(),
            P("dp"),
            P("dp"),
        ),
        out_specs=(P(("dp", "tx"), "ty"), P("dp", None, None, "tx")),
        check_vma=False,
    )
```

```python
import functools

import jax
import jax.numpy as jnp
from jax import lax
from jax.experimental import pallas as pl
from jax.experimental.pallas import tpu as pltpu
from jax.sharding import PartitionSpec as P

D = 2048
HD = 64
GROUP = 4
ACC = 8


rope_base = 10000000.0
attn_mult = 0.015625
norm_eps = 1e-05
neg_fill = -1e30


def joined(value, axis, join):
    pieces = jax.tree.map(lambda part: lax.all_gather(part, axis), value)
    head = jax.tree.map(lambda part: part[0], pieces)
    tail = jax.tree.map(lambda part: part[1:], pieces)
    so_far, _ = lax.scan(lambda so_far, slab: (join(so_far, slab), None), head, tail)
    return so_far


def ancestry(parent_rows):
    node_count = parent_rows.shape[-1]
    node_ids = jnp.arange(node_count, dtype=jnp.int32)
    linked = (node_ids[None, :] == parent_rows[:, None]) | (node_ids[None, :] == node_ids[:, None])
    reachable = linked.astype(jnp.float32)
    for repeat in range(max(1, (node_count - 1).bit_length())):
        reachable = jnp.minimum(jnp.dot(reachable, reachable, precision=lax.Precision.HIGHEST), 1.0)
    return reachable


def rotated(values, positions):
    half_size = values.shape[-1] // 2
    frequency = rope_base ** (-2.0 * jnp.arange(half_size, dtype=jnp.float32) / values.shape[-1])
    angles = positions.astype(jnp.float32)[..., None] * frequency
    cosine = jnp.cos(angles)
    sine_part = jnp.sin(angles)
    front_half = values[..., :half_size]
    back_half = values[..., half_size:]
    return jnp.concatenate(
        [front_half * cosine - back_half * sine_part, back_half * cosine + front_half * sine_part],
        axis=-1,
    )


def combine_stats(first_stats, second_stats):
    top_first, sum_first, summed_first = first_stats
    top_second, sum_second, summed_second = second_stats
    top_both = jnp.maximum(top_first, top_second)
    scale_first = jnp.exp(top_first - top_both)
    scale_second = jnp.exp(top_second - top_both)
    return (
        top_both,
        sum_first * scale_first + sum_second * scale_second,
        summed_first * scale_first[..., None] + summed_second * scale_second[..., None],
    )


def packed(values, index):
    chooser = (index[:, None] == jnp.arange(values.shape[0], dtype=index.dtype)[None, :]).astype(
        values.dtype
    )
    return jnp.dot(chooser, values, preferred_element_type=jnp.float32).astype(values.dtype)


def routing(home_slot, group_count, local_reqs):
    dest_group = (home_slot // local_reqs).reshape(group_count, local_reqs)
    local_ids = jnp.arange(local_reqs, dtype=jnp.int32)
    earlier = local_ids[None, :] < local_ids[:, None]
    same_dest = dest_group[:, :, None] == dest_group[:, None, :]
    dest_rank = jnp.sum(same_dest & earlier[None], axis=2)
    return (dest_group, dest_rank)


def tree_part(queries, keys_new, values_new, ancestors):
    scores = attn_mult * jnp.einsum(
        "rtkgd,rukd->rtkgu", queries, keys_new, preferred_element_type=jnp.float32
    )
    valid_keys = (ancestors > 0.5)[:, :, None, None, :]
    masked = jnp.where(valid_keys, scores, neg_fill)
    top_score = jnp.max(masked, axis=-1)
    weights = jnp.where(valid_keys, jnp.exp(masked - top_score[..., None]), 0.0)
    summed = jnp.einsum(
        "rtkgu,rukd->rtkgd",
        weights.astype(jnp.bfloat16),
        values_new,
        preferred_element_type=jnp.float32,
    )
    return (top_score, jnp.sum(weights, axis=-1), summed)


def cache_kernel(lens_ref, start_ref, q_ref, k_ref, v_ref, top_ref, sum_ref, acc_ref):
    slot = pl.program_id(0)
    head_local = top_ref.shape[1]
    cache_local = k_ref.shape[1]
    limit = lens_ref[slot] - start_ref[0]
    valid = lax.broadcasted_iota(jnp.int32, (1, cache_local), 1) < limit
    keys = k_ref[0]
    values = v_ref[0]
    lane = lax.broadcasted_iota(jnp.int32, (1, head_local * HD), 1)
    queries = q_ref[0] * jnp.asarray(attn_mult, q_ref.dtype)
    any_valid = limit > 0
    result = None
    for head in range(head_local):
        mine = (lane >= head * HD) & (lane < (head + 1) * HD)
        own = jnp.where(mine, queries, jnp.zeros((), queries.dtype))
        scores = lax.dot_general(
            own, keys, (((1,), (1,)), ((), ())), preferred_element_type=jnp.float32
        )
        masked = jnp.where(valid, scores, neg_fill)
        top = jnp.max(masked, axis=1, keepdims=True)
        weights = jnp.exp(masked - top)
        summed = jnp.dot(weights.astype(jnp.bfloat16), values, preferred_element_type=jnp.float32)
        total = jnp.where(any_valid, jnp.sum(weights, axis=1, keepdims=True), 0.0)
        top_ref[0, head : head + 1, :] = jnp.broadcast_to(top, (top.shape[0], 128)).T[0:1, :]
        sum_ref[0, head : head + 1, :] = jnp.broadcast_to(total, (total.shape[0], 128)).T[0:1, :]
        result = summed if result is None else jnp.where(mine, summed, result)
    acc_ref[0] = jnp.where(any_valid, result, 0.0)


def cache_merged(slot_queries, k_cache, v_cache, home_lens):
    local_reqs, tree_slots, head_local = slot_queries.shape[:3]
    cache_local = k_cache.shape[1]
    width = head_local * HD
    rows = tree_slots * GROUP
    key_start = (lax.axis_index("ty") * cache_local).astype(jnp.int32).reshape(1)
    spread = slot_queries.transpose(0, 1, 3, 2, 4).reshape(local_reqs, rows, width)
    top, total, summed = pl.pallas_call(
        cache_kernel,
        grid_spec=pltpu.PrefetchScalarGridSpec(
            num_scalar_prefetch=2,
            grid=(local_reqs,),
            in_specs=[
                pl.BlockSpec((1, rows, width), lambda s, lens, start: (s, 0, 0)),
                pl.BlockSpec((1, cache_local, width), lambda s, lens, start: (s, 0, 0)),
                pl.BlockSpec((1, cache_local, width), lambda s, lens, start: (s, 0, 0)),
            ],
            out_specs=[
                pl.BlockSpec((1, head_local, rows), lambda s, lens, start: (s, 0, 0)),
                pl.BlockSpec((1, head_local, rows), lambda s, lens, start: (s, 0, 0)),
                pl.BlockSpec((1, rows, width), lambda s, lens, start: (s, 0, 0)),
            ],
        ),
        out_shape=[
            jax.ShapeDtypeStruct((local_reqs, head_local, rows), jnp.float32),
            jax.ShapeDtypeStruct((local_reqs, head_local, rows), jnp.float32),
            jax.ShapeDtypeStruct((local_reqs, rows, width), jnp.float32),
        ],
        cost_estimate=pl.CostEstimate(
            flops=4 * local_reqs * head_local * rows * cache_local * width,
            transcendentals=local_reqs * head_local * rows * cache_local,
            bytes_accessed=2 * k_cache.size * 2 + spread.size * 2 + local_reqs * rows * width * 4,
        ),
    )(home_lens, key_start, spread, k_cache, v_cache)
    top_all = ty_max(top)
    scale = jnp.exp(top - top_all)
    scale_lanes = jnp.repeat(scale.transpose(0, 2, 1), HD, axis=2)
    count = total.size
    joint = jnp.concatenate(
        [(summed * scale_lanes).reshape(-1, 128), (total * scale).reshape(count // 128, 128)],
        axis=0,
    )
    joint = axis_sum(joint, "ty", True, jnp.bfloat16, jnp.bfloat16, 2)[: joint.shape[0]]
    summed = joint[: summed.size // 128].reshape(summed.shape[0], -1)
    total = joint[summed.size // 128 :].reshape(total.shape[0], -1)
    return (top_all, total, summed)


def ty_max_kernel(x_ref, out_ref, held, send_sem, recv_sem):
    n = lax.axis_size("ty")
    me = lax.axis_index("ty")
    row = lax.axis_index("dp")
    col = lax.axis_index("tx")
    barrier = pltpu.get_barrier_semaphore()
    for step in range(1, n):
        peer = lax.rem(me + step, n)
        pl.semaphore_signal(
            barrier, inc=1, device_id=(row, col, peer), device_id_type=pl.DeviceIdType.MESH
        )
    pl.semaphore_wait(barrier, n - 1)
    copies = []
    for step in range(1, n):
        peer = lax.rem(me + step, n)
        copy = pltpu.make_async_remote_copy(
            src_ref=x_ref,
            dst_ref=held.at[step - 1],
            send_sem=send_sem.at[step - 1],
            recv_sem=recv_sem.at[step - 1],
            device_id=(row, col, peer),
            device_id_type=pl.DeviceIdType.MESH,
        )
        copy.start()
        copies.append(copy)
    for copy in copies:
        copy.wait()
    result = x_ref[...]
    for step in range(1, n):
        result = jnp.maximum(result, held[step - 1])
    out_ref[...] = result


def axis_sum_kernel(axis, gather, x_ref, out_ref, held, gathered, sems):
    n = lax.axis_size(axis)
    me = lax.axis_index(axis)
    chunk = held.shape[1]
    where = {name: lax.axis_index(name) for name in ("dp", "tx", "ty")}

    def device(peer):
        return tuple(peer if name == axis else where[name] for name in ("dp", "tx", "ty"))

    barrier = pltpu.get_barrier_semaphore()
    for step in range(1, n):
        pl.semaphore_signal(
            barrier, inc=1, device_id=device(lax.rem(me + step, n)), device_id_type=pl.DeviceIdType.MESH
        )
    pl.semaphore_wait(barrier, n - 1)
    copies = []
    for step in range(1, n):
        peer = lax.rem(me + step, n)
        copy = pltpu.make_async_remote_copy(
            src_ref=x_ref.at[pl.ds(pl.multiple_of(peer * chunk, 16), chunk)],
            dst_ref=held.at[step - 1],
            send_sem=sems.at[0, step - 1],
            recv_sem=sems.at[1, step - 1],
            device_id=device(peer),
            device_id_type=pl.DeviceIdType.MESH,
        )
        copy.start()
        copies.append(copy)
    for copy in copies:
        copy.wait()
    own = pl.ds(pl.multiple_of(me * chunk, 16), chunk)
    total = x_ref[own].astype(jnp.float32)
    for step in range(1, n):
        total = total + held[step - 1].astype(jnp.float32)
    if not gather:
        out_ref[...] = total.astype(out_ref.dtype)
        return
    out_ref[own] = total.astype(out_ref.dtype)
    copies = []
    for step in range(1, n):
        peer = lax.rem(me + step, n)
        copy = pltpu.make_async_remote_copy(
            src_ref=out_ref.at[own],
            dst_ref=gathered.at[step - 1],
            send_sem=sems.at[2, step - 1],
            recv_sem=sems.at[3, step - 1],
            device_id=device(peer),
            device_id_type=pl.DeviceIdType.MESH,
        )
        copy.start()
        copies.append(copy)
    for copy in copies:
        copy.wait()
    for step in range(1, n):
        source = lax.rem(me - step + n, n)
        out_ref[pl.ds(pl.multiple_of(source * chunk, 16), chunk)] = gathered[step - 1]


def relay_sum_kernel(axis, x_ref, out_ref, held, halves, forwarded, sems):
    n = lax.axis_size(axis)
    me = lax.axis_index(axis)
    chunk = held.shape[1]
    half = chunk // 2
    where = {name: lax.axis_index(name) for name in ("dp", "tx", "ty")}

    def device(peer):
        return tuple(peer if name == axis else where[name] for name in ("dp", "tx", "ty"))

    right = lax.rem(me + 1, n)
    left = lax.rem(me + n - 1, n)
    across = lax.rem(me + 2, n)

    def rows(index, start, size):
        return pl.ds(pl.multiple_of(index * chunk + start, 8), size)

    def remote(src, dst, slot, peer):
        return pltpu.make_async_remote_copy(
            src_ref=src,
            dst_ref=dst,
            send_sem=sems.at[0, slot],
            recv_sem=sems.at[1, slot],
            device_id=device(peer),
            device_id_type=pl.DeviceIdType.MESH,
        )

    barrier = pltpu.get_barrier_semaphore()
    for peer in (left, right):
        pl.semaphore_signal(barrier, inc=1, device_id=device(peer), device_id_type=pl.DeviceIdType.MESH)
    pl.semaphore_wait(barrier, 2)
    direct_right = remote(x_ref.at[rows(right, 0, chunk)], held.at[0], 0, right)
    direct_left = remote(x_ref.at[rows(left, 0, chunk)], held.at[1], 1, left)
    relay_right = remote(x_ref.at[rows(across, 0, half)], halves.at[0], 2, right)
    relay_left = remote(x_ref.at[rows(across, half, half)], halves.at[1], 3, left)
    for copy in (direct_right, direct_left, relay_right, relay_left):
        copy.start()
    relay_right.wait()
    onward_right = remote(halves.at[0], forwarded.at[0], 4, right)
    onward_right.start()
    relay_left.wait()
    onward_left = remote(halves.at[1], forwarded.at[1], 5, left)
    onward_left.start()
    for copy in (direct_right, direct_left, onward_right, onward_left):
        copy.wait()
    for part in range(2):
        mine = x_ref[rows(me, part * half, half)].astype(jnp.float32)
        total = (
            mine
            + held[0, pl.ds(part * half, half)].astype(jnp.float32)
            + held[1, pl.ds(part * half, half)].astype(jnp.float32)
            + forwarded[part].astype(jnp.float32)
        )
        out_ref[pl.ds(part * half, half)] = total.astype(out_ref.dtype)


def axis_sum(values, axis, gather, send_type, out_type, collective_id):
    n = lax.axis_size(axis)
    flat = values.reshape(-1, 128).astype(send_type)
    rows = flat.shape[0]
    padded = -(-rows // (16 * n)) * 16 * n
    flat = jnp.pad(flat, ((0, padded - rows), (0, 0)))
    chunk = padded // n
    if not gather and n == 4:
        return pl.pallas_call(
            functools.partial(relay_sum_kernel, axis),
            out_shape=jax.ShapeDtypeStruct((chunk, 128), out_type),
            in_specs=[pl.BlockSpec(memory_space=pltpu.VMEM)],
            out_specs=pl.BlockSpec(memory_space=pltpu.VMEM),
            scratch_shapes=[
                pltpu.VMEM((2, chunk, 128), send_type),
                pltpu.VMEM((2, chunk // 2, 128), send_type),
                pltpu.VMEM((2, chunk // 2, 128), send_type),
                pltpu.SemaphoreType.DMA((2, 6)),
            ],
            compiler_params=pltpu.CompilerParams(collective_id=collective_id, has_side_effects=True),
        )(flat)
    out = pl.pallas_call(
        functools.partial(axis_sum_kernel, axis, gather),
        out_shape=jax.ShapeDtypeStruct((padded if gather else chunk, 128), out_type),
        in_specs=[pl.BlockSpec(memory_space=pltpu.VMEM)],
        out_specs=pl.BlockSpec(memory_space=pltpu.VMEM),
        scratch_shapes=[
            pltpu.VMEM((n - 1, chunk, 128), send_type),
            pltpu.VMEM((n - 1, chunk, 128), out_type),
            pltpu.SemaphoreType.DMA((4, n - 1)),
        ],
        compiler_params=pltpu.CompilerParams(collective_id=collective_id, has_side_effects=True),
    )(flat)
    return out


def dp_exchange_kernel(x_ref, out_ref, held, sems):
    n = lax.axis_size("dp")
    me = lax.axis_index("dp")
    col = lax.axis_index("tx")
    row = lax.axis_index("ty")
    barrier = pltpu.get_barrier_semaphore()
    for step in range(1, n):
        pl.semaphore_signal(
            barrier, inc=1, device_id=(lax.rem(me + step, n), col, row), device_id_type=pl.DeviceIdType.MESH
        )
    pl.semaphore_wait(barrier, n - 1)
    copies = []
    for step in range(1, n):
        peer = lax.rem(me + step, n)
        copy = pltpu.make_async_remote_copy(
            src_ref=x_ref.at[peer],
            dst_ref=held.at[step - 1],
            send_sem=sems.at[0, step - 1],
            recv_sem=sems.at[1, step - 1],
            device_id=(peer, col, row),
            device_id_type=pl.DeviceIdType.MESH,
        )
        copy.start()
        copies.append(copy)
    out_ref[me] = x_ref[me]
    for copy in copies:
        copy.wait()
    for step in range(1, n):
        out_ref[lax.rem(me - step + n, n)] = held[step - 1]


def dp_exchange(blocks, collective_id):
    n = lax.axis_size("dp")
    shape = blocks.shape
    tiles = blocks.reshape(n, -1, 128)
    out = pl.pallas_call(
        dp_exchange_kernel,
        out_shape=jax.ShapeDtypeStruct(tiles.shape, tiles.dtype),
        in_specs=[pl.BlockSpec(memory_space=pltpu.VMEM)],
        out_specs=pl.BlockSpec(memory_space=pltpu.VMEM),
        scratch_shapes=[
            pltpu.VMEM((n - 1,) + tiles.shape[1:], tiles.dtype),
            pltpu.SemaphoreType.DMA((2, n - 1)),
        ],
        compiler_params=pltpu.CompilerParams(collective_id=collective_id, has_side_effects=True),
    )(tiles)
    return out.reshape(shape)


def axis_gather_kernel(axis, x_ref, out_ref, gathered, sems):
    n = lax.axis_size(axis)
    me = lax.axis_index(axis)
    chunk = x_ref.shape[0]
    where = {name: lax.axis_index(name) for name in ("dp", "tx", "ty")}

    def device(peer):
        return tuple(peer if name == axis else where[name] for name in ("dp", "tx", "ty"))

    barrier = pltpu.get_barrier_semaphore()
    for step in range(1, n):
        pl.semaphore_signal(
            barrier, inc=1, device_id=device(lax.rem(me + step, n)), device_id_type=pl.DeviceIdType.MESH
        )
    pl.semaphore_wait(barrier, n - 1)
    copies = []
    for step in range(1, n):
        peer = lax.rem(me + step, n)
        copy = pltpu.make_async_remote_copy(
            src_ref=x_ref,
            dst_ref=gathered.at[step - 1],
            send_sem=sems.at[0, step - 1],
            recv_sem=sems.at[1, step - 1],
            device_id=device(peer),
            device_id_type=pl.DeviceIdType.MESH,
        )
        copy.start()
        copies.append(copy)
    out_ref[pl.ds(pl.multiple_of(me * chunk, 16), chunk)] = x_ref[...]
    for copy in copies:
        copy.wait()
    for step in range(1, n):
        source = lax.rem(me - step + n, n)
        out_ref[pl.ds(pl.multiple_of(source * chunk, 16), chunk)] = gathered[step - 1]


def axis_gather(values, axis, collective_id):
    n = lax.axis_size(axis)
    flat = values.reshape(-1, 128)
    chunk = flat.shape[0]
    out = pl.pallas_call(
        functools.partial(axis_gather_kernel, axis),
        out_shape=jax.ShapeDtypeStruct((n * chunk, 128), flat.dtype),
        in_specs=[pl.BlockSpec(memory_space=pltpu.VMEM)],
        out_specs=pl.BlockSpec(memory_space=pltpu.VMEM),
        scratch_shapes=[
            pltpu.VMEM((n - 1, chunk, 128), flat.dtype),
            pltpu.SemaphoreType.DMA((2, n - 1)),
        ],
        compiler_params=pltpu.CompilerParams(collective_id=collective_id, has_side_effects=True),
    )(flat)
    return out.reshape((n * values.shape[0],) + values.shape[1:])


def ty_max(values):
    n = lax.axis_size("ty")
    flat = values.reshape(-1, 128)
    out = pl.pallas_call(
        ty_max_kernel,
        out_shape=jax.ShapeDtypeStruct(flat.shape, flat.dtype),
        in_specs=[pl.BlockSpec(memory_space=pltpu.VMEM)],
        out_specs=pl.BlockSpec(memory_space=pltpu.VMEM),
        scratch_shapes=[
            pltpu.VMEM((n - 1,) + flat.shape, flat.dtype),
            pltpu.SemaphoreType.DMA((n - 1,)),
            pltpu.SemaphoreType.DMA((n - 1,)),
        ],
        compiler_params=pltpu.CompilerParams(collective_id=0, has_side_effects=True),
    )(flat)
    return out.reshape(values.shape)


def shards(
    hidden_in,
    norm_gain,
    w_qkv,
    w_out,
    k_cache,
    v_cache,
    cache_lens,
    home_slot,
    parents,
    tree_sizes,
    leaf_node,
):
    group_count = lax.axis_size("dp")
    group_index = lax.axis_index("dp")
    local_reqs = k_cache.shape[0]
    tree_slots = parents.shape[1]
    capacity = (local_reqs + group_count - 1) // group_count
    head_local = k_cache.shape[2] // HD
    row_count = hidden_in.shape[0]
    float_in = hidden_in.astype(jnp.float32)
    feature_local = hidden_in.shape[1]
    gain_part = lax.dynamic_slice_in_dim(
        norm_gain, lax.axis_index("ty") * feature_local, feature_local
    )
    scaled = (float_in * gain_part.astype(jnp.float32)).astype(jnp.bfloat16)
    partial_proj = jnp.dot(scaled, w_qkv, preferred_element_type=jnp.float32)
    partial_square = jnp.sum(float_in * float_in, axis=1)
    proj_cols = partial_proj.shape[1]
    n_ty = lax.axis_size("ty")
    chunk_rows = row_count // n_ty
    reqs_mine = local_reqs // n_ty
    square_block = jnp.pad(
        partial_square.reshape(n_ty, 1, chunk_rows),
        ((0, 0), (0, 7), (0, proj_cols - chunk_rows)),
    )
    joint = jnp.concatenate(
        [partial_proj.reshape(n_ty, chunk_rows, proj_cols), square_block], axis=1
    )
    mine = axis_sum(joint, "ty", False, jnp.float32, jnp.float32, 1).reshape(-1, proj_cols)
    square_sum = mine[chunk_rows, :chunk_rows]
    rms_inverse = lax.rsqrt(square_sum / D + norm_eps)
    projected = (mine[:chunk_rows] * rms_inverse[:, None]).reshape(
        reqs_mine, tree_slots, head_local, GROUP + 2, HD
    )
    first_request = group_index * local_reqs
    local_ids = jnp.arange(local_reqs, dtype=jnp.int32)
    request_ids = jnp.arange(home_slot.shape[0], dtype=jnp.int32)
    my_parents = lax.dynamic_slice_in_dim(parents, first_request, local_reqs, 0)
    my_slots = lax.dynamic_slice_in_dim(home_slot, first_request, local_reqs, 0)
    ancestors = jax.vmap(ancestry)(my_parents)
    node_depth = jnp.sum(ancestors > 0.5, axis=2) - 1
    slot_match = my_slots[:, None] == request_ids[None, :]
    my_lens = jnp.sum(jnp.where(slot_match, cache_lens[None, :], 0), axis=1)
    positions = my_lens[:, None] + node_depth
    positions_mine = lax.dynamic_slice_in_dim(
        positions, lax.axis_index("ty") * reqs_mine, reqs_mine, 0
    )
    queries_mine = rotated(
        projected[:, :, :, :GROUP, :], positions_mine[:, :, None, None]
    ).astype(jnp.bfloat16)
    keys_mine = rotated(projected[:, :, :, GROUP, :], positions_mine[:, :, None]).astype(
        jnp.bfloat16
    )
    values_mine = projected[:, :, :, GROUP + 1, :].astype(jnp.bfloat16)
    piece = jnp.concatenate(
        [
            queries_mine.reshape(chunk_rows, -1),
            keys_mine.reshape(chunk_rows, -1),
            values_mine.reshape(chunk_rows, -1),
        ],
        axis=1,
    )
    everything = axis_gather(piece, "ty", 6)
    query_cols = head_local * GROUP * HD
    queries = everything[:, :query_cols].reshape(local_reqs, tree_slots, head_local, GROUP, HD)
    keys_new = everything[:, query_cols : query_cols + head_local * HD].reshape(
        local_reqs, tree_slots, head_local, HD
    )
    values_new = everything[:, query_cols + head_local * HD :].reshape(
        local_reqs, tree_slots, head_local, HD
    )
    dest_group, dest_rank = routing(home_slot, group_count, local_reqs)
    send_pos = lax.dynamic_index_in_dim(
        dest_group, group_index, 0, keepdims=False
    ) * capacity + lax.dynamic_index_in_dim(dest_rank, group_index, 0, keepdims=False)
    buffer_ids = jnp.arange(group_count * capacity, dtype=jnp.int32)
    send_hit = send_pos[None, :] == buffer_ids[:, None]
    send_index = jnp.where(
        jnp.any(send_hit, axis=1),
        jnp.sum(jnp.where(send_hit, local_ids[None, :], 0), axis=1),
        local_reqs,
    )
    target_slots = first_request + local_ids
    owner_match = home_slot[None, :] == target_slots[:, None]
    owner_request = jnp.sum(jnp.where(owner_match, request_ids[None, :], 0), axis=1)
    owner_rank = jnp.sum(jnp.where(owner_match, dest_rank.reshape(-1)[None, :], 0), axis=1)
    recv_index = owner_request // local_reqs * capacity + owner_rank
    back_hit = recv_index[None, :] == buffer_ids[:, None]
    back_index = jnp.where(
        jnp.any(back_hit, axis=1),
        jnp.sum(jnp.where(back_hit, local_ids[None, :], 0), axis=1),
        local_reqs,
    )
    home_lens = lax.dynamic_slice_in_dim(cache_lens, first_request, local_reqs, 0)
    arrived = dp_exchange(packed(queries.reshape(local_reqs, -1), send_index), 4)
    slot_queries = packed(arrived, recv_index).reshape(queries.shape)
    top_score, weight_sum, summed = cache_merged(slot_queries, k_cache, v_cache, home_lens)
    value_width = summed.shape[1]
    sum_width = weight_sum.shape[1]
    log_flat = top_score.reshape(local_reqs, -1)
    log_high = lax.reduce_precision(log_flat, exponent_bits=8, mantissa_bits=7)
    log_rest = log_flat - log_high
    log_mid = lax.reduce_precision(log_rest, exponent_bits=8, mantissa_bits=7)
    log_low = log_rest - log_mid
    payload = jnp.concatenate(
        [
            summed,
            weight_sum,
            log_high.astype(jnp.bfloat16),
            log_mid.astype(jnp.bfloat16),
            log_low.astype(jnp.bfloat16),
        ],
        axis=1,
    )
    outgoing = packed(payload, back_index)
    back = lax.all_to_all(
        outgoing.reshape(outgoing.shape[0], -1, 128), "dp", split_axis=0, concat_axis=0, tiled=True
    ).reshape(outgoing.shape)
    back = packed(back, send_pos).astype(jnp.float32)
    log_width = log_flat.shape[1]
    cache_values = (
        back[:, :value_width]
        .reshape(local_reqs, tree_slots, GROUP, head_local, HD)
        .transpose(0, 1, 3, 2, 4)
    )
    cache_sum = (
        back[:, value_width : value_width + sum_width]
        .reshape(local_reqs, head_local, tree_slots, GROUP)
        .transpose(0, 2, 1, 3)
    )
    logs = value_width + sum_width
    cache_top = (
        (
            back[:, logs : logs + log_width]
            + back[:, logs + log_width : logs + 2 * log_width]
            + back[:, logs + 2 * log_width :]
        )
        .reshape(local_reqs, head_local, tree_slots, GROUP)
        .transpose(0, 2, 1, 3)
    )
    tree_stats = tree_part(queries, keys_new, values_new, ancestors)
    top_all, sum_all, summed_all = combine_stats(
        (cache_top, cache_sum, cache_values), tree_stats
    )
    attention = (summed_all / sum_all[..., None]).astype(jnp.bfloat16)
    attention_rows = attention.reshape(row_count, -1)
    rows_mine = row_count // lax.axis_size("tx")
    mixed_sum = axis_sum(
        jnp.dot(attention_rows, w_out, preferred_element_type=jnp.float32),
        "tx",
        False,
        jnp.bfloat16,
        jnp.float32,
        3,
    ).reshape(row_count // lax.axis_size("tx"), -1)
    row_start = lax.axis_index("tx") * rows_mine
    residual = lax.dynamic_slice_in_dim(float_in, row_start, rows_mine, 0)
    row_ids = row_start + jnp.arange(rows_mine, dtype=jnp.int32)
    request_of = row_ids // tree_slots
    slot_of = row_ids % tree_slots
    size_of = jnp.sum(
        jnp.where(request_of[:, None] == local_ids[None, :], tree_sizes[None, :], 0), axis=1
    )
    layer_out = jnp.where((slot_of < size_of)[:, None], residual + mixed_sum, 0.0).astype(
        jnp.bfloat16
    )
    node_ids = jnp.arange(tree_slots, dtype=jnp.int32)
    leaf_hit = (leaf_node[:, None] == node_ids[None, :]).astype(jnp.float32)
    path_nodes = jnp.einsum("rt,rtu->ru", leaf_hit, ancestors)
    depth_hit = node_depth[:, None, :] == jnp.arange(ACC, dtype=jnp.int32)[None, :, None]
    chooser = jnp.where(depth_hit, path_nodes[:, None, :], 0.0).astype(jnp.bfloat16)
    stacked = jnp.stack(
        [
            keys_new.reshape(local_reqs, tree_slots, -1),
            values_new.reshape(local_reqs, tree_slots, -1),
        ],
        axis=2,
    )
    accepted_kv = jnp.einsum(
        "rsu,ruwc->rswc", chooser, stacked, preferred_element_type=jnp.float32
    ).astype(jnp.bfloat16)
    return (layer_out, accepted_kv)


def solution(mesh):
    return jax.shard_map(
        shards,
        mesh=mesh,
        in_specs=(
            P("dp", "ty"),
            P(),
            P("ty", "tx"),
            P("tx", "ty"),
            P("dp", "ty", "tx"),
            P("dp", "ty", "tx"),
            P(),
            P(),
            P(),
            P("dp"),
            P("dp"),
        ),
        out_specs=(P(("dp", "tx"), "ty"), P("dp", None, None, "tx")),
        check_vma=False,
    )
```

```python
import functools

import jax
import jax.numpy as jnp
from jax import lax
from jax.experimental import pallas as pl
from jax.experimental.pallas import tpu as pltpu
from jax.sharding import PartitionSpec as P

D = 2048
HD = 64
GROUP = 4
ACC = 8


rope_base = 10000000.0
attn_mult = 0.015625
norm_eps = 1e-05
neg_fill = -1e30


def joined(value, axis, join):
    pieces = jax.tree.map(lambda part: lax.all_gather(part, axis), value)
    head = jax.tree.map(lambda part: part[0], pieces)
    tail = jax.tree.map(lambda part: part[1:], pieces)
    so_far, _ = lax.scan(lambda so_far, slab: (join(so_far, slab), None), head, tail)
    return so_far


def ancestry(parent_rows):
    node_count = parent_rows.shape[-1]
    node_ids = jnp.arange(node_count, dtype=jnp.int32)
    linked = (node_ids[None, :] == parent_rows[:, None]) | (node_ids[None, :] == node_ids[:, None])
    reachable = linked.astype(jnp.float32)
    for repeat in range(max(1, (node_count - 1).bit_length())):
        reachable = jnp.minimum(jnp.dot(reachable, reachable, precision=lax.Precision.HIGHEST), 1.0)
    return reachable


def rotated(values, positions):
    half_size = values.shape[-1] // 2
    frequency = rope_base ** (-2.0 * jnp.arange(half_size, dtype=jnp.float32) / values.shape[-1])
    angles = positions.astype(jnp.float32)[..., None] * frequency
    cosine = jnp.cos(angles)
    sine_part = jnp.sin(angles)
    front_half = values[..., :half_size]
    back_half = values[..., half_size:]
    return jnp.concatenate(
        [front_half * cosine - back_half * sine_part, back_half * cosine + front_half * sine_part],
        axis=-1,
    )


def combine_stats(first_stats, second_stats):
    top_first, sum_first, summed_first = first_stats
    top_second, sum_second, summed_second = second_stats
    top_both = jnp.maximum(top_first, top_second)
    scale_first = jnp.exp(top_first - top_both)
    scale_second = jnp.exp(top_second - top_both)
    return (
        top_both,
        sum_first * scale_first + sum_second * scale_second,
        summed_first * scale_first[..., None] + summed_second * scale_second[..., None],
    )


def packed(values, index):
    chooser = (index[:, None] == jnp.arange(values.shape[0], dtype=index.dtype)[None, :]).astype(
        values.dtype
    )
    return jnp.dot(chooser, values, preferred_element_type=jnp.float32).astype(values.dtype)


def routing(home_slot, group_count, local_reqs):
    dest_group = (home_slot // local_reqs).reshape(group_count, local_reqs)
    local_ids = jnp.arange(local_reqs, dtype=jnp.int32)
    earlier = local_ids[None, :] < local_ids[:, None]
    same_dest = dest_group[:, :, None] == dest_group[:, None, :]
    dest_rank = jnp.sum(same_dest & earlier[None], axis=2)
    return (dest_group, dest_rank)


def tree_part(queries, keys_new, values_new, ancestors):
    scores = attn_mult * jnp.einsum(
        "rtkgd,rukd->rtkgu", queries, keys_new, preferred_element_type=jnp.float32
    )
    valid_keys = (ancestors > 0.5)[:, :, None, None, :]
    masked = jnp.where(valid_keys, scores, neg_fill)
    top_score = jnp.max(masked, axis=-1)
    weights = jnp.where(valid_keys, jnp.exp(masked - top_score[..., None]), 0.0)
    summed = jnp.einsum(
        "rtkgu,rukd->rtkgd",
        weights.astype(jnp.bfloat16),
        values_new,
        preferred_element_type=jnp.float32,
    )
    return (top_score, jnp.sum(weights, axis=-1), summed)


def cache_kernel(lens_ref, start_ref, q_ref, k_ref, v_ref, top_ref, sum_ref, acc_ref):
    slot = pl.program_id(0)
    head_local = top_ref.shape[1]
    cache_local = k_ref.shape[1]
    limit = lens_ref[slot] - start_ref[0]
    valid = lax.broadcasted_iota(jnp.int32, (1, cache_local), 1) < limit
    keys = k_ref[0]
    values = v_ref[0]
    lane = lax.broadcasted_iota(jnp.int32, (1, head_local * HD), 1)
    queries = q_ref[0] * jnp.asarray(attn_mult, q_ref.dtype)
    any_valid = limit > 0
    result = None
    for head in range(head_local):
        mine = (lane >= head * HD) & (lane < (head + 1) * HD)
        own = jnp.where(mine, queries, jnp.zeros((), queries.dtype))
        scores = lax.dot_general(
            own, keys, (((1,), (1,)), ((), ())), preferred_element_type=jnp.float32
        )
        masked = jnp.where(valid, scores, neg_fill)
        top = jnp.max(masked, axis=1, keepdims=True)
        weights = jnp.exp(masked - top)
        summed = jnp.dot(weights.astype(jnp.bfloat16), values, preferred_element_type=jnp.float32)
        total = jnp.where(any_valid, jnp.sum(weights, axis=1, keepdims=True), 0.0)
        top_ref[0, head : head + 1, :] = jnp.broadcast_to(top, (top.shape[0], 128)).T[0:1, :]
        sum_ref[0, head : head + 1, :] = jnp.broadcast_to(total, (total.shape[0], 128)).T[0:1, :]
        result = summed if result is None else jnp.where(mine, summed, result)
    acc_ref[0] = jnp.where(any_valid, result, 0.0)


def cache_merged(slot_queries, k_cache, v_cache, home_lens):
    local_reqs, tree_slots, head_local = slot_queries.shape[:3]
    cache_local = k_cache.shape[1]
    width = head_local * HD
    rows = tree_slots * GROUP
    key_start = (lax.axis_index("ty") * cache_local).astype(jnp.int32).reshape(1)
    spread = slot_queries.transpose(0, 1, 3, 2, 4).reshape(local_reqs, rows, width)
    top, total, summed = pl.pallas_call(
        cache_kernel,
        grid_spec=pltpu.PrefetchScalarGridSpec(
            num_scalar_prefetch=2,
            grid=(local_reqs,),
            in_specs=[
                pl.BlockSpec((1, rows, width), lambda s, lens, start: (s, 0, 0)),
                pl.BlockSpec((1, cache_local, width), lambda s, lens, start: (s, 0, 0)),
                pl.BlockSpec((1, cache_local, width), lambda s, lens, start: (s, 0, 0)),
            ],
            out_specs=[
                pl.BlockSpec((1, head_local, rows), lambda s, lens, start: (s, 0, 0)),
                pl.BlockSpec((1, head_local, rows), lambda s, lens, start: (s, 0, 0)),
                pl.BlockSpec((1, rows, width), lambda s, lens, start: (s, 0, 0)),
            ],
        ),
        out_shape=[
            jax.ShapeDtypeStruct((local_reqs, head_local, rows), jnp.float32),
            jax.ShapeDtypeStruct((local_reqs, head_local, rows), jnp.float32),
            jax.ShapeDtypeStruct((local_reqs, rows, width), jnp.float32),
        ],
        cost_estimate=pl.CostEstimate(
            flops=4 * local_reqs * head_local * rows * cache_local * width,
            transcendentals=local_reqs * head_local * rows * cache_local,
            bytes_accessed=2 * k_cache.size * 2 + spread.size * 2 + local_reqs * rows * width * 4,
        ),
    )(home_lens, key_start, spread, k_cache, v_cache)
    top_all = ty_max(top)
    scale = jnp.exp(top - top_all)
    scale_lanes = jnp.repeat(scale.transpose(0, 2, 1), HD, axis=2)
    count = total.size
    joint = jnp.concatenate(
        [(summed * scale_lanes).reshape(-1, 128), (total * scale).reshape(count // 128, 128)],
        axis=0,
    )
    joint = axis_sum(joint, "ty", True, jnp.bfloat16, jnp.bfloat16, 2)[: joint.shape[0]]
    summed = joint[: summed.size // 128].reshape(summed.shape[0], -1)
    total = joint[summed.size // 128 :].reshape(total.shape[0], -1)
    return (top_all, total, summed)


def ty_max_kernel(x_ref, out_ref, held, send_sem, recv_sem):
    n = lax.axis_size("ty")
    me = lax.axis_index("ty")
    row = lax.axis_index("dp")
    col = lax.axis_index("tx")
    barrier = pltpu.get_barrier_semaphore()
    for step in range(1, n):
        peer = lax.rem(me + step, n)
        pl.semaphore_signal(
            barrier, inc=1, device_id=(row, col, peer), device_id_type=pl.DeviceIdType.MESH
        )
    pl.semaphore_wait(barrier, n - 1)
    copies = []
    for step in range(1, n):
        peer = lax.rem(me + step, n)
        copy = pltpu.make_async_remote_copy(
            src_ref=x_ref,
            dst_ref=held.at[step - 1],
            send_sem=send_sem.at[step - 1],
            recv_sem=recv_sem.at[step - 1],
            device_id=(row, col, peer),
            device_id_type=pl.DeviceIdType.MESH,
        )
        copy.start()
        copies.append(copy)
    for copy in copies:
        copy.wait()
    result = x_ref[...]
    for step in range(1, n):
        result = jnp.maximum(result, held[step - 1])
    out_ref[...] = result


def axis_sum_kernel(axis, gather, x_ref, out_ref, held, gathered, sems):
    n = lax.axis_size(axis)
    me = lax.axis_index(axis)
    chunk = held.shape[1]
    where = {name: lax.axis_index(name) for name in ("dp", "tx", "ty")}

    def device(peer):
        return tuple(peer if name == axis else where[name] for name in ("dp", "tx", "ty"))

    barrier = pltpu.get_barrier_semaphore()
    for step in range(1, n):
        pl.semaphore_signal(
            barrier, inc=1, device_id=device(lax.rem(me + step, n)), device_id_type=pl.DeviceIdType.MESH
        )
    pl.semaphore_wait(barrier, n - 1)
    copies = []
    for step in range(1, n):
        peer = lax.rem(me + step, n)
        copy = pltpu.make_async_remote_copy(
            src_ref=x_ref.at[pl.ds(pl.multiple_of(peer * chunk, 16), chunk)],
            dst_ref=held.at[step - 1],
            send_sem=sems.at[0, step - 1],
            recv_sem=sems.at[1, step - 1],
            device_id=device(peer),
            device_id_type=pl.DeviceIdType.MESH,
        )
        copy.start()
        copies.append(copy)
    for copy in copies:
        copy.wait()
    own = pl.ds(pl.multiple_of(me * chunk, 16), chunk)
    total = x_ref[own].astype(jnp.float32)
    for step in range(1, n):
        total = total + held[step - 1].astype(jnp.float32)
    if not gather:
        out_ref[...] = total.astype(out_ref.dtype)
        return
    out_ref[own] = total.astype(out_ref.dtype)
    copies = []
    for step in range(1, n):
        peer = lax.rem(me + step, n)
        copy = pltpu.make_async_remote_copy(
            src_ref=out_ref.at[own],
            dst_ref=gathered.at[step - 1],
            send_sem=sems.at[2, step - 1],
            recv_sem=sems.at[3, step - 1],
            device_id=device(peer),
            device_id_type=pl.DeviceIdType.MESH,
        )
        copy.start()
        copies.append(copy)
    for copy in copies:
        copy.wait()
    for step in range(1, n):
        source = lax.rem(me - step + n, n)
        out_ref[pl.ds(pl.multiple_of(source * chunk, 16), chunk)] = gathered[step - 1]


def axis_sum(values, axis, gather, send_type, out_type, collective_id):
    n = lax.axis_size(axis)
    flat = values.reshape(-1, 128).astype(send_type)
    rows = flat.shape[0]
    padded = -(-rows // (16 * n)) * 16 * n
    flat = jnp.pad(flat, ((0, padded - rows), (0, 0)))
    chunk = padded // n
    out = pl.pallas_call(
        functools.partial(axis_sum_kernel, axis, gather),
        out_shape=jax.ShapeDtypeStruct((padded if gather else chunk, 128), out_type),
        in_specs=[pl.BlockSpec(memory_space=pltpu.VMEM)],
        out_specs=pl.BlockSpec(memory_space=pltpu.VMEM),
        scratch_shapes=[
            pltpu.VMEM((n - 1, chunk, 128), send_type),
            pltpu.VMEM((n - 1, chunk, 128), out_type),
            pltpu.SemaphoreType.DMA((4, n - 1)),
        ],
        compiler_params=pltpu.CompilerParams(collective_id=collective_id, has_side_effects=True),
    )(flat)
    return out


def dp_exchange_kernel(x_ref, out_ref, held, sems):
    n = lax.axis_size("dp")
    me = lax.axis_index("dp")
    col = lax.axis_index("tx")
    row = lax.axis_index("ty")
    barrier = pltpu.get_barrier_semaphore()
    for step in range(1, n):
        pl.semaphore_signal(
            barrier, inc=1, device_id=(lax.rem(me + step, n), col, row), device_id_type=pl.DeviceIdType.MESH
        )
    pl.semaphore_wait(barrier, n - 1)
    copies = []
    for step in range(1, n):
        peer = lax.rem(me + step, n)
        copy = pltpu.make_async_remote_copy(
            src_ref=x_ref.at[peer],
            dst_ref=out_ref.at[me],
            send_sem=sems.at[0, step - 1],
            recv_sem=sems.at[1, step - 1],
            device_id=(peer, col, row),
            device_id_type=pl.DeviceIdType.MESH,
        )
        copy.start()
        copies.append(copy)
    out_ref[me] = x_ref[me]
    for copy in copies:
        copy.wait()


def dp_exchange(blocks, collective_id):
    n = lax.axis_size("dp")
    shape = blocks.shape
    tiles = blocks.reshape(n, -1, 128)
    out = pl.pallas_call(
        dp_exchange_kernel,
        out_shape=jax.ShapeDtypeStruct(tiles.shape, tiles.dtype),
        in_specs=[pl.BlockSpec(memory_space=pltpu.VMEM)],
        out_specs=pl.BlockSpec(memory_space=pltpu.VMEM),
        scratch_shapes=[
            pltpu.VMEM((n - 1,) + tiles.shape[1:], tiles.dtype),
            pltpu.SemaphoreType.DMA((2, n - 1)),
        ],
        compiler_params=pltpu.CompilerParams(collective_id=collective_id, has_side_effects=True),
    )(tiles)
    return out.reshape(shape)


def axis_gather_kernel(axis, x_ref, out_ref, gathered, sems):
    n = lax.axis_size(axis)
    me = lax.axis_index(axis)
    chunk = x_ref.shape[0]
    where = {name: lax.axis_index(name) for name in ("dp", "tx", "ty")}

    def device(peer):
        return tuple(peer if name == axis else where[name] for name in ("dp", "tx", "ty"))

    barrier = pltpu.get_barrier_semaphore()
    for step in range(1, n):
        pl.semaphore_signal(
            barrier, inc=1, device_id=device(lax.rem(me + step, n)), device_id_type=pl.DeviceIdType.MESH
        )
    pl.semaphore_wait(barrier, n - 1)
    copies = []
    for step in range(1, n):
        peer = lax.rem(me + step, n)
        copy = pltpu.make_async_remote_copy(
            src_ref=x_ref,
            dst_ref=gathered.at[step - 1],
            send_sem=sems.at[0, step - 1],
            recv_sem=sems.at[1, step - 1],
            device_id=device(peer),
            device_id_type=pl.DeviceIdType.MESH,
        )
        copy.start()
        copies.append(copy)
    out_ref[pl.ds(pl.multiple_of(me * chunk, 16), chunk)] = x_ref[...]
    for copy in copies:
        copy.wait()
    for step in range(1, n):
        source = lax.rem(me - step + n, n)
        out_ref[pl.ds(pl.multiple_of(source * chunk, 16), chunk)] = gathered[step - 1]


def axis_gather(values, axis, collective_id):
    n = lax.axis_size(axis)
    flat = values.reshape(-1, 128)
    chunk = flat.shape[0]
    out = pl.pallas_call(
        functools.partial(axis_gather_kernel, axis),
        out_shape=jax.ShapeDtypeStruct((n * chunk, 128), flat.dtype),
        in_specs=[pl.BlockSpec(memory_space=pltpu.VMEM)],
        out_specs=pl.BlockSpec(memory_space=pltpu.VMEM),
        scratch_shapes=[
            pltpu.VMEM((n - 1, chunk, 128), flat.dtype),
            pltpu.SemaphoreType.DMA((2, n - 1)),
        ],
        compiler_params=pltpu.CompilerParams(collective_id=collective_id, has_side_effects=True),
    )(flat)
    return out.reshape((n * values.shape[0],) + values.shape[1:])


def ty_max(values):
    n = lax.axis_size("ty")
    flat = values.reshape(-1, 128)
    out = pl.pallas_call(
        ty_max_kernel,
        out_shape=jax.ShapeDtypeStruct(flat.shape, flat.dtype),
        in_specs=[pl.BlockSpec(memory_space=pltpu.VMEM)],
        out_specs=pl.BlockSpec(memory_space=pltpu.VMEM),
        scratch_shapes=[
            pltpu.VMEM((n - 1,) + flat.shape, flat.dtype),
            pltpu.SemaphoreType.DMA((n - 1,)),
            pltpu.SemaphoreType.DMA((n - 1,)),
        ],
        compiler_params=pltpu.CompilerParams(collective_id=0, has_side_effects=True),
    )(flat)
    return out.reshape(values.shape)


def shards(
    hidden_in,
    norm_gain,
    w_qkv,
    w_out,
    k_cache,
    v_cache,
    cache_lens,
    home_slot,
    parents,
    tree_sizes,
    leaf_node,
):
    group_count = lax.axis_size("dp")
    group_index = lax.axis_index("dp")
    local_reqs = k_cache.shape[0]
    tree_slots = parents.shape[1]
    capacity = (local_reqs + group_count - 1) // group_count
    head_local = k_cache.shape[2] // HD
    row_count = hidden_in.shape[0]
    float_in = hidden_in.astype(jnp.float32)
    feature_local = hidden_in.shape[1]
    gain_part = lax.dynamic_slice_in_dim(
        norm_gain, lax.axis_index("ty") * feature_local, feature_local
    )
    scaled = (float_in * gain_part.astype(jnp.float32)).astype(jnp.bfloat16)
    partial_proj = jnp.dot(scaled, w_qkv, preferred_element_type=jnp.float32)
    partial_square = jnp.sum(float_in * float_in, axis=1)
    proj_cols = partial_proj.shape[1]
    n_ty = lax.axis_size("ty")
    chunk_rows = row_count // n_ty
    reqs_mine = local_reqs // n_ty
    square_block = jnp.pad(
        partial_square.reshape(n_ty, 1, chunk_rows),
        ((0, 0), (0, 7), (0, proj_cols - chunk_rows)),
    )
    joint = jnp.concatenate(
        [partial_proj.reshape(n_ty, chunk_rows, proj_cols), square_block], axis=1
    )
    mine = axis_sum(joint, "ty", False, jnp.float32, jnp.float32, 1).reshape(-1, proj_cols)
    square_sum = mine[chunk_rows, :chunk_rows]
    rms_inverse = lax.rsqrt(square_sum / D + norm_eps)
    projected = (mine[:chunk_rows] * rms_inverse[:, None]).reshape(
        reqs_mine, tree_slots, head_local, GROUP + 2, HD
    )
    first_request = group_index * local_reqs
    local_ids = jnp.arange(local_reqs, dtype=jnp.int32)
    request_ids = jnp.arange(home_slot.shape[0], dtype=jnp.int32)
    my_parents = lax.dynamic_slice_in_dim(parents, first_request, local_reqs, 0)
    my_slots = lax.dynamic_slice_in_dim(home_slot, first_request, local_reqs, 0)
    ancestors = jax.vmap(ancestry)(my_parents)
    node_depth = jnp.sum(ancestors > 0.5, axis=2) - 1
    slot_match = my_slots[:, None] == request_ids[None, :]
    my_lens = jnp.sum(jnp.where(slot_match, cache_lens[None, :], 0), axis=1)
    positions = my_lens[:, None] + node_depth
    positions_mine = lax.dynamic_slice_in_dim(
        positions, lax.axis_index("ty") * reqs_mine, reqs_mine, 0
    )
    queries_mine = rotated(
        projected[:, :, :, :GROUP, :], positions_mine[:, :, None, None]
    ).astype(jnp.bfloat16)
    keys_mine = rotated(projected[:, :, :, GROUP, :], positions_mine[:, :, None]).astype(
        jnp.bfloat16
    )
    values_mine = projected[:, :, :, GROUP + 1, :].astype(jnp.bfloat16)
    piece = jnp.concatenate(
        [
            queries_mine.reshape(chunk_rows, -1),
            keys_mine.reshape(chunk_rows, -1),
            values_mine.reshape(chunk_rows, -1),
        ],
        axis=1,
    )
    everything = axis_gather(piece, "ty", 6)
    query_cols = head_local * GROUP * HD
    queries = everything[:, :query_cols].reshape(local_reqs, tree_slots, head_local, GROUP, HD)
    keys_new = everything[:, query_cols : query_cols + head_local * HD].reshape(
        local_reqs, tree_slots, head_local, HD
    )
    values_new = everything[:, query_cols + head_local * HD :].reshape(
        local_reqs, tree_slots, head_local, HD
    )
    dest_group, dest_rank = routing(home_slot, group_count, local_reqs)
    send_pos = lax.dynamic_index_in_dim(
        dest_group, group_index, 0, keepdims=False
    ) * capacity + lax.dynamic_index_in_dim(dest_rank, group_index, 0, keepdims=False)
    buffer_ids = jnp.arange(group_count * capacity, dtype=jnp.int32)
    send_hit = send_pos[None, :] == buffer_ids[:, None]
    send_index = jnp.where(
        jnp.any(send_hit, axis=1),
        jnp.sum(jnp.where(send_hit, local_ids[None, :], 0), axis=1),
        local_reqs,
    )
    target_slots = first_request + local_ids
    owner_match = home_slot[None, :] == target_slots[:, None]
    owner_request = jnp.sum(jnp.where(owner_match, request_ids[None, :], 0), axis=1)
    owner_rank = jnp.sum(jnp.where(owner_match, dest_rank.reshape(-1)[None, :], 0), axis=1)
    recv_index = owner_request // local_reqs * capacity + owner_rank
    back_hit = recv_index[None, :] == buffer_ids[:, None]
    back_index = jnp.where(
        jnp.any(back_hit, axis=1),
        jnp.sum(jnp.where(back_hit, local_ids[None, :], 0), axis=1),
        local_reqs,
    )
    home_lens = lax.dynamic_slice_in_dim(cache_lens, first_request, local_reqs, 0)
    arrived = dp_exchange(packed(queries.reshape(local_reqs, -1), send_index), 4)
    slot_queries = packed(arrived, recv_index).reshape(queries.shape)
    top_score, weight_sum, summed = cache_merged(slot_queries, k_cache, v_cache, home_lens)
    value_width = summed.shape[1]
    sum_width = weight_sum.shape[1]
    log_flat = top_score.reshape(local_reqs, -1)
    log_high = lax.reduce_precision(log_flat, exponent_bits=8, mantissa_bits=7)
    log_rest = log_flat - log_high
    log_mid = lax.reduce_precision(log_rest, exponent_bits=8, mantissa_bits=7)
    log_low = log_rest - log_mid
    payload = jnp.concatenate(
        [
            summed,
            weight_sum,
            log_high.astype(jnp.bfloat16),
            log_mid.astype(jnp.bfloat16),
            log_low.astype(jnp.bfloat16),
        ],
        axis=1,
    )
    outgoing = packed(payload, back_index)
    back = lax.all_to_all(
        outgoing.reshape(outgoing.shape[0], -1, 128), "dp", split_axis=0, concat_axis=0, tiled=True
    ).reshape(outgoing.shape)
    back = packed(back, send_pos).astype(jnp.float32)
    log_width = log_flat.shape[1]
    cache_values = (
        back[:, :value_width]
        .reshape(local_reqs, tree_slots, GROUP, head_local, HD)
        .transpose(0, 1, 3, 2, 4)
    )
    cache_sum = (
        back[:, value_width : value_width + sum_width]
        .reshape(local_reqs, head_local, tree_slots, GROUP)
        .transpose(0, 2, 1, 3)
    )
    logs = value_width + sum_width
    cache_top = (
        (
            back[:, logs : logs + log_width]
            + back[:, logs + log_width : logs + 2 * log_width]
            + back[:, logs + 2 * log_width :]
        )
        .reshape(local_reqs, head_local, tree_slots, GROUP)
        .transpose(0, 2, 1, 3)
    )
    tree_stats = tree_part(queries, keys_new, values_new, ancestors)
    top_all, sum_all, summed_all = combine_stats(
        (cache_top, cache_sum, cache_values), tree_stats
    )
    attention = (summed_all / sum_all[..., None]).astype(jnp.bfloat16)
    attention_rows = attention.reshape(row_count, -1)
    rows_mine = row_count // lax.axis_size("tx")
    mixed_sum = axis_sum(
        jnp.dot(attention_rows, w_out, preferred_element_type=jnp.float32),
        "tx",
        False,
        jnp.bfloat16,
        jnp.float32,
        3,
    ).reshape(row_count // lax.axis_size("tx"), -1)
    row_start = lax.axis_index("tx") * rows_mine
    residual = lax.dynamic_slice_in_dim(float_in, row_start, rows_mine, 0)
    row_ids = row_start + jnp.arange(rows_mine, dtype=jnp.int32)
    request_of = row_ids // tree_slots
    slot_of = row_ids % tree_slots
    size_of = jnp.sum(
        jnp.where(request_of[:, None] == local_ids[None, :], tree_sizes[None, :], 0), axis=1
    )
    layer_out = jnp.where((slot_of < size_of)[:, None], residual + mixed_sum, 0.0).astype(
        jnp.bfloat16
    )
    node_ids = jnp.arange(tree_slots, dtype=jnp.int32)
    leaf_hit = (leaf_node[:, None] == node_ids[None, :]).astype(jnp.float32)
    path_nodes = jnp.einsum("rt,rtu->ru", leaf_hit, ancestors)
    depth_hit = node_depth[:, None, :] == jnp.arange(ACC, dtype=jnp.int32)[None, :, None]
    chooser = jnp.where(depth_hit, path_nodes[:, None, :], 0.0).astype(jnp.bfloat16)
    stacked = jnp.stack(
        [
            keys_new.reshape(local_reqs, tree_slots, -1),
            values_new.reshape(local_reqs, tree_slots, -1),
        ],
        axis=2,
    )
    accepted_kv = jnp.einsum(
        "rsu,ruwc->rswc", chooser, stacked, preferred_element_type=jnp.float32
    ).astype(jnp.bfloat16)
    return (layer_out, accepted_kv)


def solution(mesh):
    return jax.shard_map(
        shards,
        mesh=mesh,
        in_specs=(
            P("dp", "ty"),
            P(),
            P("ty", "tx"),
            P("tx", "ty"),
            P("dp", "ty", "tx"),
            P("dp", "ty", "tx"),
            P(),
            P(),
            P(),
            P("dp"),
            P("dp"),
        ),
        out_specs=(P(("dp", "tx"), "ty"), P("dp", None, None, "tx")),
        check_vma=False,
    )
```

```python
import functools

import jax
import jax.numpy as jnp
from jax import lax
from jax.experimental import pallas as pl
from jax.experimental.pallas import tpu as pltpu
from jax.sharding import PartitionSpec as P

D = 2048
HD = 64
GROUP = 4
ACC = 8


rope_base = 10000000.0
attn_mult = 0.015625
norm_eps = 1e-05
neg_fill = -1e30


def joined(value, axis, join):
    pieces = jax.tree.map(lambda part: lax.all_gather(part, axis), value)
    head = jax.tree.map(lambda part: part[0], pieces)
    tail = jax.tree.map(lambda part: part[1:], pieces)
    so_far, _ = lax.scan(lambda so_far, slab: (join(so_far, slab), None), head, tail)
    return so_far


def ancestry(parent_rows):
    node_count = parent_rows.shape[-1]
    node_ids = jnp.arange(node_count, dtype=jnp.int32)
    linked = (node_ids[None, :] == parent_rows[:, None]) | (node_ids[None, :] == node_ids[:, None])
    reachable = linked.astype(jnp.float32)
    for repeat in range(max(1, (node_count - 1).bit_length())):
        reachable = jnp.minimum(jnp.dot(reachable, reachable, precision=lax.Precision.HIGHEST), 1.0)
    return reachable


def rotated(values, positions):
    half_size = values.shape[-1] // 2
    frequency = rope_base ** (-2.0 * jnp.arange(half_size, dtype=jnp.float32) / values.shape[-1])
    angles = positions.astype(jnp.float32)[..., None] * frequency
    cosine = jnp.cos(angles)
    sine_part = jnp.sin(angles)
    front_half = values[..., :half_size]
    back_half = values[..., half_size:]
    return jnp.concatenate(
        [front_half * cosine - back_half * sine_part, back_half * cosine + front_half * sine_part],
        axis=-1,
    )


def combine_stats(first_stats, second_stats):
    top_first, sum_first, summed_first = first_stats
    top_second, sum_second, summed_second = second_stats
    top_both = jnp.maximum(top_first, top_second)
    scale_first = jnp.exp(top_first - top_both)
    scale_second = jnp.exp(top_second - top_both)
    return (
        top_both,
        sum_first * scale_first + sum_second * scale_second,
        summed_first * scale_first[..., None] + summed_second * scale_second[..., None],
    )


def packed(values, index):
    chooser = (index[:, None] == jnp.arange(values.shape[0], dtype=index.dtype)[None, :]).astype(
        values.dtype
    )
    return jnp.dot(chooser, values, preferred_element_type=jnp.float32).astype(values.dtype)


def routing(home_slot, group_count, local_reqs):
    dest_group = (home_slot // local_reqs).reshape(group_count, local_reqs)
    local_ids = jnp.arange(local_reqs, dtype=jnp.int32)
    earlier = local_ids[None, :] < local_ids[:, None]
    same_dest = dest_group[:, :, None] == dest_group[:, None, :]
    dest_rank = jnp.sum(same_dest & earlier[None], axis=2)
    return (dest_group, dest_rank)


def tree_part(queries, keys_new, values_new, ancestors):
    scores = attn_mult * jnp.einsum(
        "rtkgd,rukd->rtkgu", queries, keys_new, preferred_element_type=jnp.float32
    )
    valid_keys = (ancestors > 0.5)[:, :, None, None, :]
    masked = jnp.where(valid_keys, scores, neg_fill)
    top_score = jnp.max(masked, axis=-1)
    weights = jnp.where(valid_keys, jnp.exp(masked - top_score[..., None]), 0.0)
    summed = jnp.einsum(
        "rtkgu,rukd->rtkgd",
        weights.astype(jnp.bfloat16),
        values_new,
        preferred_element_type=jnp.float32,
    )
    return (top_score, jnp.sum(weights, axis=-1), summed)


def cache_kernel(lens_ref, start_ref, q_ref, k_ref, v_ref, top_ref, sum_ref, acc_ref):
    slot = pl.program_id(0)
    head_local = top_ref.shape[1]
    cache_local = k_ref.shape[1]
    limit = lens_ref[slot] - start_ref[0]
    valid = lax.broadcasted_iota(jnp.int32, (1, cache_local), 1) < limit
    keys = k_ref[0]
    values = v_ref[0]
    lane = lax.broadcasted_iota(jnp.int32, (1, head_local * HD), 1)
    queries = q_ref[0] * jnp.asarray(attn_mult, q_ref.dtype)
    any_valid = limit > 0
    result = None
    for head in range(head_local):
        mine = (lane >= head * HD) & (lane < (head + 1) * HD)
        own = jnp.where(mine, queries, jnp.zeros((), queries.dtype))
        scores = lax.dot_general(
            own, keys, (((1,), (1,)), ((), ())), preferred_element_type=jnp.float32
        )
        masked = jnp.where(valid, scores, neg_fill)
        top = jnp.max(masked, axis=1, keepdims=True)
        weights = jnp.exp(masked - top)
        summed = jnp.dot(weights.astype(jnp.bfloat16), values, preferred_element_type=jnp.float32)
        total = jnp.where(any_valid, jnp.sum(weights, axis=1, keepdims=True), 0.0)
        top_ref[0, head : head + 1, :] = jnp.broadcast_to(top, (top.shape[0], 128)).T[0:1, :]
        sum_ref[0, head : head + 1, :] = jnp.broadcast_to(total, (total.shape[0], 128)).T[0:1, :]
        result = summed if result is None else jnp.where(mine, summed, result)
    acc_ref[0] = jnp.where(any_valid, result, 0.0)


def cache_merged(slot_queries, k_cache, v_cache, home_lens):
    local_reqs, tree_slots, head_local = slot_queries.shape[:3]
    cache_local = k_cache.shape[1]
    width = head_local * HD
    rows = tree_slots * GROUP
    key_start = (lax.axis_index("ty") * cache_local).astype(jnp.int32).reshape(1)
    spread = slot_queries.transpose(0, 1, 3, 2, 4).reshape(local_reqs, rows, width)
    top, total, summed = pl.pallas_call(
        cache_kernel,
        grid_spec=pltpu.PrefetchScalarGridSpec(
            num_scalar_prefetch=2,
            grid=(local_reqs,),
            in_specs=[
                pl.BlockSpec((1, rows, width), lambda s, lens, start: (s, 0, 0)),
                pl.BlockSpec((1, cache_local, width), lambda s, lens, start: (s, 0, 0)),
                pl.BlockSpec((1, cache_local, width), lambda s, lens, start: (s, 0, 0)),
            ],
            out_specs=[
                pl.BlockSpec((1, head_local, rows), lambda s, lens, start: (s, 0, 0)),
                pl.BlockSpec((1, head_local, rows), lambda s, lens, start: (s, 0, 0)),
                pl.BlockSpec((1, rows, width), lambda s, lens, start: (s, 0, 0)),
            ],
        ),
        out_shape=[
            jax.ShapeDtypeStruct((local_reqs, head_local, rows), jnp.float32),
            jax.ShapeDtypeStruct((local_reqs, head_local, rows), jnp.float32),
            jax.ShapeDtypeStruct((local_reqs, rows, width), jnp.float32),
        ],
        cost_estimate=pl.CostEstimate(
            flops=4 * local_reqs * head_local * rows * cache_local * width,
            transcendentals=local_reqs * head_local * rows * cache_local,
            bytes_accessed=2 * k_cache.size * 2 + spread.size * 2 + local_reqs * rows * width * 4,
        ),
    )(home_lens, key_start, spread, k_cache, v_cache)
    top_all = ty_max(top)
    scale = jnp.exp(top - top_all)
    scale_lanes = jnp.repeat(scale.transpose(0, 2, 1), HD, axis=2)
    count = total.size
    joint = jnp.concatenate(
        [(summed * scale_lanes).reshape(-1, 128), (total * scale).reshape(count // 128, 128)],
        axis=0,
    )
    joint = axis_sum(joint, "ty", True, jnp.bfloat16, jnp.bfloat16, 2)[: joint.shape[0]]
    summed = joint[: summed.size // 128].reshape(summed.shape[0], -1)
    total = joint[summed.size // 128 :].reshape(total.shape[0], -1)
    return (top_all, total, summed)


def ty_max_kernel(x_ref, out_ref, held, send_sem, recv_sem):
    n = lax.axis_size("ty")
    me = lax.axis_index("ty")
    row = lax.axis_index("dp")
    col = lax.axis_index("tx")
    barrier = pltpu.get_barrier_semaphore()
    for step in range(1, n):
        peer = lax.rem(me + step, n)
        pl.semaphore_signal(
            barrier, inc=1, device_id=(row, col, peer), device_id_type=pl.DeviceIdType.MESH
        )
    pl.semaphore_wait(barrier, n - 1)
    copies = []
    for step in range(1, n):
        peer = lax.rem(me + step, n)
        copy = pltpu.make_async_remote_copy(
            src_ref=x_ref,
            dst_ref=held.at[step - 1],
            send_sem=send_sem.at[step - 1],
            recv_sem=recv_sem.at[step - 1],
            device_id=(row, col, peer),
            device_id_type=pl.DeviceIdType.MESH,
        )
        copy.start()
        copies.append(copy)
    for copy in copies:
        copy.wait()
    result = x_ref[...]
    for step in range(1, n):
        result = jnp.maximum(result, held[step - 1])
    out_ref[...] = result


def axis_sum_kernel(axis, gather, x_ref, out_ref, held, gathered, sems):
    n = lax.axis_size(axis)
    me = lax.axis_index(axis)
    chunk = held.shape[1]
    where = {name: lax.axis_index(name) for name in ("dp", "tx", "ty")}

    def device(peer):
        return tuple(peer if name == axis else where[name] for name in ("dp", "tx", "ty"))

    barrier = pltpu.get_barrier_semaphore()
    for step in range(1, n):
        pl.semaphore_signal(
            barrier, inc=1, device_id=device(lax.rem(me + step, n)), device_id_type=pl.DeviceIdType.MESH
        )
    pl.semaphore_wait(barrier, n - 1)
    copies = []
    for step in range(1, n):
        peer = lax.rem(me + step, n)
        copy = pltpu.make_async_remote_copy(
            src_ref=x_ref.at[pl.ds(pl.multiple_of(peer * chunk, 16), chunk)],
            dst_ref=held.at[step - 1],
            send_sem=sems.at[0, step - 1],
            recv_sem=sems.at[1, step - 1],
            device_id=device(peer),
            device_id_type=pl.DeviceIdType.MESH,
        )
        copy.start()
        copies.append(copy)
    for copy in copies:
        copy.wait()
    own = pl.ds(pl.multiple_of(me * chunk, 16), chunk)
    total = x_ref[own].astype(jnp.float32)
    for step in range(1, n):
        total = total + held[step - 1].astype(jnp.float32)
    if not gather:
        out_ref[...] = total.astype(out_ref.dtype)
        return
    out_ref[own] = total.astype(out_ref.dtype)
    copies = []
    for step in range(1, n):
        peer = lax.rem(me + step, n)
        copy = pltpu.make_async_remote_copy(
            src_ref=out_ref.at[own],
            dst_ref=gathered.at[step - 1],
            send_sem=sems.at[2, step - 1],
            recv_sem=sems.at[3, step - 1],
            device_id=device(peer),
            device_id_type=pl.DeviceIdType.MESH,
        )
        copy.start()
        copies.append(copy)
    for copy in copies:
        copy.wait()
    for step in range(1, n):
        source = lax.rem(me - step + n, n)
        out_ref[pl.ds(pl.multiple_of(source * chunk, 16), chunk)] = gathered[step - 1]


def axis_sum(values, axis, gather, send_type, out_type, collective_id):
    n = lax.axis_size(axis)
    flat = values.reshape(-1, 128).astype(send_type)
    rows = flat.shape[0]
    padded = -(-rows // (16 * n)) * 16 * n
    flat = jnp.pad(flat, ((0, padded - rows), (0, 0)))
    chunk = padded // n
    out = pl.pallas_call(
        functools.partial(axis_sum_kernel, axis, gather),
        out_shape=jax.ShapeDtypeStruct((padded if gather else chunk, 128), out_type),
        in_specs=[pl.BlockSpec(memory_space=pltpu.VMEM)],
        out_specs=pl.BlockSpec(memory_space=pltpu.VMEM),
        scratch_shapes=[
            pltpu.VMEM((n - 1, chunk, 128), send_type),
            pltpu.VMEM((n - 1, chunk, 128), out_type),
            pltpu.SemaphoreType.DMA((4, n - 1)),
        ],
        compiler_params=pltpu.CompilerParams(collective_id=collective_id, has_side_effects=True),
    )(flat)
    return out


def dp_exchange_kernel(x_ref, out_ref, held, sems):
    n = lax.axis_size("dp")
    me = lax.axis_index("dp")
    col = lax.axis_index("tx")
    row = lax.axis_index("ty")
    barrier = pltpu.get_barrier_semaphore()
    for step in range(1, n):
        pl.semaphore_signal(
            barrier, inc=1, device_id=(lax.rem(me + step, n), col, row), device_id_type=pl.DeviceIdType.MESH
        )
    pl.semaphore_wait(barrier, n - 1)
    copies = []
    for step in range(1, n):
        peer = lax.rem(me + step, n)
        copy = pltpu.make_async_remote_copy(
            src_ref=x_ref.at[peer],
            dst_ref=held.at[step - 1],
            send_sem=sems.at[0, step - 1],
            recv_sem=sems.at[1, step - 1],
            device_id=(peer, col, row),
            device_id_type=pl.DeviceIdType.MESH,
        )
        copy.start()
        copies.append(copy)
    out_ref[me] = x_ref[me]
    for step, copy in enumerate(copies, start=1):
        copy.wait()
        out_ref[lax.rem(me - step + n, n)] = held[step - 1]


def dp_exchange(blocks, collective_id):
    n = lax.axis_size("dp")
    shape = blocks.shape
    tiles = blocks.reshape(n, -1, 128)
    out = pl.pallas_call(
        dp_exchange_kernel,
        out_shape=jax.ShapeDtypeStruct(tiles.shape, tiles.dtype),
        in_specs=[pl.BlockSpec(memory_space=pltpu.VMEM)],
        out_specs=pl.BlockSpec(memory_space=pltpu.VMEM),
        scratch_shapes=[
            pltpu.VMEM((n - 1,) + tiles.shape[1:], tiles.dtype),
            pltpu.SemaphoreType.DMA((2, n - 1)),
        ],
        compiler_params=pltpu.CompilerParams(collective_id=collective_id, has_side_effects=True),
    )(tiles)
    return out.reshape(shape)


def axis_gather_kernel(axis, x_ref, out_ref, gathered, sems):
    n = lax.axis_size(axis)
    me = lax.axis_index(axis)
    chunk = x_ref.shape[0]
    where = {name: lax.axis_index(name) for name in ("dp", "tx", "ty")}

    def device(peer):
        return tuple(peer if name == axis else where[name] for name in ("dp", "tx", "ty"))

    barrier = pltpu.get_barrier_semaphore()
    for step in range(1, n):
        pl.semaphore_signal(
            barrier, inc=1, device_id=device(lax.rem(me + step, n)), device_id_type=pl.DeviceIdType.MESH
        )
    pl.semaphore_wait(barrier, n - 1)
    copies = []
    for step in range(1, n):
        peer = lax.rem(me + step, n)
        copy = pltpu.make_async_remote_copy(
            src_ref=x_ref,
            dst_ref=gathered.at[step - 1],
            send_sem=sems.at[0, step - 1],
            recv_sem=sems.at[1, step - 1],
            device_id=device(peer),
            device_id_type=pl.DeviceIdType.MESH,
        )
        copy.start()
        copies.append(copy)
    out_ref[pl.ds(pl.multiple_of(me * chunk, 16), chunk)] = x_ref[...]
    for copy in copies:
        copy.wait()
    for step in range(1, n):
        source = lax.rem(me - step + n, n)
        out_ref[pl.ds(pl.multiple_of(source * chunk, 16), chunk)] = gathered[step - 1]


def axis_gather(values, axis, collective_id):
    n = lax.axis_size(axis)
    flat = values.reshape(-1, 128)
    chunk = flat.shape[0]
    out = pl.pallas_call(
        functools.partial(axis_gather_kernel, axis),
        out_shape=jax.ShapeDtypeStruct((n * chunk, 128), flat.dtype),
        in_specs=[pl.BlockSpec(memory_space=pltpu.VMEM)],
        out_specs=pl.BlockSpec(memory_space=pltpu.VMEM),
        scratch_shapes=[
            pltpu.VMEM((n - 1, chunk, 128), flat.dtype),
            pltpu.SemaphoreType.DMA((2, n - 1)),
        ],
        compiler_params=pltpu.CompilerParams(collective_id=collective_id, has_side_effects=True),
    )(flat)
    return out.reshape((n * values.shape[0],) + values.shape[1:])


def ty_max(values):
    n = lax.axis_size("ty")
    flat = values.reshape(-1, 128)
    out = pl.pallas_call(
        ty_max_kernel,
        out_shape=jax.ShapeDtypeStruct(flat.shape, flat.dtype),
        in_specs=[pl.BlockSpec(memory_space=pltpu.VMEM)],
        out_specs=pl.BlockSpec(memory_space=pltpu.VMEM),
        scratch_shapes=[
            pltpu.VMEM((n - 1,) + flat.shape, flat.dtype),
            pltpu.SemaphoreType.DMA((n - 1,)),
            pltpu.SemaphoreType.DMA((n - 1,)),
        ],
        compiler_params=pltpu.CompilerParams(collective_id=0, has_side_effects=True),
    )(flat)
    return out.reshape(values.shape)


def shards(
    hidden_in,
    norm_gain,
    w_qkv,
    w_out,
    k_cache,
    v_cache,
    cache_lens,
    home_slot,
    parents,
    tree_sizes,
    leaf_node,
):
    group_count = lax.axis_size("dp")
    group_index = lax.axis_index("dp")
    local_reqs = k_cache.shape[0]
    tree_slots = parents.shape[1]
    capacity = (local_reqs + group_count - 1) // group_count
    head_local = k_cache.shape[2] // HD
    row_count = hidden_in.shape[0]
    float_in = hidden_in.astype(jnp.float32)
    feature_local = hidden_in.shape[1]
    gain_part = lax.dynamic_slice_in_dim(
        norm_gain, lax.axis_index("ty") * feature_local, feature_local
    )
    scaled = (float_in * gain_part.astype(jnp.float32)).astype(jnp.bfloat16)
    partial_proj = jnp.dot(scaled, w_qkv, preferred_element_type=jnp.float32)
    partial_square = jnp.sum(float_in * float_in, axis=1)
    proj_cols = partial_proj.shape[1]
    n_ty = lax.axis_size("ty")
    chunk_rows = row_count // n_ty
    reqs_mine = local_reqs // n_ty
    square_block = jnp.pad(
        partial_square.reshape(n_ty, 1, chunk_rows),
        ((0, 0), (0, 7), (0, proj_cols - chunk_rows)),
    )
    joint = jnp.concatenate(
        [partial_proj.reshape(n_ty, chunk_rows, proj_cols), square_block], axis=1
    )
    mine = axis_sum(joint, "ty", False, jnp.float32, jnp.float32, 1).reshape(-1, proj_cols)
    square_sum = mine[chunk_rows, :chunk_rows]
    rms_inverse = lax.rsqrt(square_sum / D + norm_eps)
    projected = (mine[:chunk_rows] * rms_inverse[:, None]).reshape(
        reqs_mine, tree_slots, head_local, GROUP + 2, HD
    )
    first_request = group_index * local_reqs
    local_ids = jnp.arange(local_reqs, dtype=jnp.int32)
    request_ids = jnp.arange(home_slot.shape[0], dtype=jnp.int32)
    my_parents = lax.dynamic_slice_in_dim(parents, first_request, local_reqs, 0)
    my_slots = lax.dynamic_slice_in_dim(home_slot, first_request, local_reqs, 0)
    ancestors = jax.vmap(ancestry)(my_parents)
    node_depth = jnp.sum(ancestors > 0.5, axis=2) - 1
    slot_match = my_slots[:, None] == request_ids[None, :]
    my_lens = jnp.sum(jnp.where(slot_match, cache_lens[None, :], 0), axis=1)
    positions = my_lens[:, None] + node_depth
    positions_mine = lax.dynamic_slice_in_dim(
        positions, lax.axis_index("ty") * reqs_mine, reqs_mine, 0
    )
    queries_mine = rotated(
        projected[:, :, :, :GROUP, :], positions_mine[:, :, None, None]
    ).astype(jnp.bfloat16)
    keys_mine = rotated(projected[:, :, :, GROUP, :], positions_mine[:, :, None]).astype(
        jnp.bfloat16
    )
    values_mine = projected[:, :, :, GROUP + 1, :].astype(jnp.bfloat16)
    piece = jnp.concatenate(
        [
            queries_mine.reshape(chunk_rows, -1),
            keys_mine.reshape(chunk_rows, -1),
            values_mine.reshape(chunk_rows, -1),
        ],
        axis=1,
    )
    everything = axis_gather(piece, "ty", 6)
    query_cols = head_local * GROUP * HD
    queries = everything[:, :query_cols].reshape(local_reqs, tree_slots, head_local, GROUP, HD)
    keys_new = everything[:, query_cols : query_cols + head_local * HD].reshape(
        local_reqs, tree_slots, head_local, HD
    )
    values_new = everything[:, query_cols + head_local * HD :].reshape(
        local_reqs, tree_slots, head_local, HD
    )
    dest_group, dest_rank = routing(home_slot, group_count, local_reqs)
    send_pos = lax.dynamic_index_in_dim(
        dest_group, group_index, 0, keepdims=False
    ) * capacity + lax.dynamic_index_in_dim(dest_rank, group_index, 0, keepdims=False)
    buffer_ids = jnp.arange(group_count * capacity, dtype=jnp.int32)
    send_hit = send_pos[None, :] == buffer_ids[:, None]
    send_index = jnp.where(
        jnp.any(send_hit, axis=1),
        jnp.sum(jnp.where(send_hit, local_ids[None, :], 0), axis=1),
        local_reqs,
    )
    target_slots = first_request + local_ids
    owner_match = home_slot[None, :] == target_slots[:, None]
    owner_request = jnp.sum(jnp.where(owner_match, request_ids[None, :], 0), axis=1)
    owner_rank = jnp.sum(jnp.where(owner_match, dest_rank.reshape(-1)[None, :], 0), axis=1)
    recv_index = owner_request // local_reqs * capacity + owner_rank
    back_hit = recv_index[None, :] == buffer_ids[:, None]
    back_index = jnp.where(
        jnp.any(back_hit, axis=1),
        jnp.sum(jnp.where(back_hit, local_ids[None, :], 0), axis=1),
        local_reqs,
    )
    home_lens = lax.dynamic_slice_in_dim(cache_lens, first_request, local_reqs, 0)
    arrived = dp_exchange(packed(queries.reshape(local_reqs, -1), send_index), 4)
    slot_queries = packed(arrived, recv_index).reshape(queries.shape)
    top_score, weight_sum, summed = cache_merged(slot_queries, k_cache, v_cache, home_lens)
    value_width = summed.shape[1]
    sum_width = weight_sum.shape[1]
    log_flat = top_score.reshape(local_reqs, -1)
    log_high = lax.reduce_precision(log_flat, exponent_bits=8, mantissa_bits=7)
    log_rest = log_flat - log_high
    log_mid = lax.reduce_precision(log_rest, exponent_bits=8, mantissa_bits=7)
    log_low = log_rest - log_mid
    payload = jnp.concatenate(
        [
            summed,
            weight_sum,
            log_high.astype(jnp.bfloat16),
            log_mid.astype(jnp.bfloat16),
            log_low.astype(jnp.bfloat16),
        ],
        axis=1,
    )
    outgoing = packed(payload, back_index)
    back = lax.all_to_all(
        outgoing.reshape(outgoing.shape[0], -1, 128), "dp", split_axis=0, concat_axis=0, tiled=True
    ).reshape(outgoing.shape)
    back = packed(back, send_pos).astype(jnp.float32)
    log_width = log_flat.shape[1]
    cache_values = (
        back[:, :value_width]
        .reshape(local_reqs, tree_slots, GROUP, head_local, HD)
        .transpose(0, 1, 3, 2, 4)
    )
    cache_sum = (
        back[:, value_width : value_width + sum_width]
        .reshape(local_reqs, head_local, tree_slots, GROUP)
        .transpose(0, 2, 1, 3)
    )
    logs = value_width + sum_width
    cache_top = (
        (
            back[:, logs : logs + log_width]
            + back[:, logs + log_width : logs + 2 * log_width]
            + back[:, logs + 2 * log_width :]
        )
        .reshape(local_reqs, head_local, tree_slots, GROUP)
        .transpose(0, 2, 1, 3)
    )
    tree_stats = tree_part(queries, keys_new, values_new, ancestors)
    top_all, sum_all, summed_all = combine_stats(
        (cache_top, cache_sum, cache_values), tree_stats
    )
    attention = (summed_all / sum_all[..., None]).astype(jnp.bfloat16)
    attention_rows = attention.reshape(row_count, -1)
    rows_mine = row_count // lax.axis_size("tx")
    mixed_sum = axis_sum(
        jnp.dot(attention_rows, w_out, preferred_element_type=jnp.float32),
        "tx",
        False,
        jnp.bfloat16,
        jnp.float32,
        3,
    ).reshape(row_count // lax.axis_size("tx"), -1)
    row_start = lax.axis_index("tx") * rows_mine
    residual = lax.dynamic_slice_in_dim(float_in, row_start, rows_mine, 0)
    row_ids = row_start + jnp.arange(rows_mine, dtype=jnp.int32)
    request_of = row_ids // tree_slots
    slot_of = row_ids % tree_slots
    size_of = jnp.sum(
        jnp.where(request_of[:, None] == local_ids[None, :], tree_sizes[None, :], 0), axis=1
    )
    layer_out = jnp.where((slot_of < size_of)[:, None], residual + mixed_sum, 0.0).astype(
        jnp.bfloat16
    )
    node_ids = jnp.arange(tree_slots, dtype=jnp.int32)
    leaf_hit = (leaf_node[:, None] == node_ids[None, :]).astype(jnp.float32)
    path_nodes = jnp.einsum("rt,rtu->ru", leaf_hit, ancestors)
    depth_hit = node_depth[:, None, :] == jnp.arange(ACC, dtype=jnp.int32)[None, :, None]
    chooser = jnp.where(depth_hit, path_nodes[:, None, :], 0.0).astype(jnp.bfloat16)
    stacked = jnp.stack(
        [
            keys_new.reshape(local_reqs, tree_slots, -1),
            values_new.reshape(local_reqs, tree_slots, -1),
        ],
        axis=2,
    )
    accepted_kv = jnp.einsum(
        "rsu,ruwc->rswc", chooser, stacked, preferred_element_type=jnp.float32
    ).astype(jnp.bfloat16)
    return (layer_out, accepted_kv)


def solution(mesh):
    return jax.shard_map(
        shards,
        mesh=mesh,
        in_specs=(
            P("dp", "ty"),
            P(),
            P("ty", "tx"),
            P("tx", "ty"),
            P("dp", "ty", "tx"),
            P("dp", "ty", "tx"),
            P(),
            P(),
            P(),
            P("dp"),
            P("dp"),
        ),
        out_specs=(P(("dp", "tx"), "ty"), P("dp", None, None, "tx")),
        check_vma=False,
    )
```
